32 devices in a mesh: wide: 8 (over z, y), narrow: 4 (over x, core).
Axes of the slice: x: 2, y: 2, z: 4, core: 2. Of those that a mesh axis runs over, the one named last changes fastest.
Arguments:
- tokens: bfloat16 [16384, 768], P(('wide', 'narrow')), may hold values from -6 to 6
- item_lengths: int32 [32], P('wide'), may hold values from 0 to 1024, as said below
- w_query: bfloat16 [768, 768], P(None, 'narrow'), may hold values from -0.3125 to 0.3125
- b_query: bfloat16 [768], P('narrow'), may hold values from -1.25 to 1.25
- w_key: bfloat16 [768, 768], P(None, 'narrow'), may hold values from -0.3125 to 0.3125
- w_value: bfloat16 [768, 768], P(None, 'narrow'), may hold values from -0.21875 to 0.21875
- b_value: bfloat16 [768], P('narrow'), may hold values from -1.25 to 1.25
- w_out: bfloat16 [768, 768], P('narrow'), may hold values from -0.875 to 0.875
- b_out: bfloat16 [768], replicated, may hold values from -1.25 to 1.25
- gain_attn: bfloat16 [768], replicated, may hold values from 0.5 to 1.5
- shift_attn: bfloat16 [768], replicated, may hold values from -1.25 to 1.25
- w_up: bfloat16 [768, 3072], P(None, 'narrow'), may hold values from -0.21875 to 0.21875
- b_up: bfloat16 [3072], P('narrow'), may hold values from -1.25 to 1.25
- w_down: bfloat16 [3072, 768], P('narrow'), may hold values from -0.109375 to 0.109375
- b_down: bfloat16 [768], replicated, may hold values from -1.25 to 1.25
- gain_ffn: bfloat16 [768], replicated, may hold values from 0.5 to 1.5
- shift_ffn: bfloat16 [768], replicated, may hold values from -1.25 to 1.25
- out_grad: bfloat16 [16384, 768], P(('wide', 'narrow')), may hold values from -6 to 6
Outputs:
- layer_out: bfloat16 [16384, 768], P(('wide', 'narrow'))
- token_grad: float32 [16384, 768], P(('wide', 'narrow'))
- w_query_grad: float32 [768, 768], P(None, 'narrow')
- b_query_grad: float32 [768], P('narrow')
- w_key_grad: float32 [768, 768], P(None, 'narrow')
- w_value_grad: float32 [768, 768], P(None, 'narrow')
- b_value_grad: float32 [768], P('narrow')
- w_out_grad: float32 [768, 768], P('narrow')
- b_out_grad: float32 [768], replicated
- gain_attn_grad: float32 [768], replicated
- shift_attn_grad: float32 [768], replicated
- w_up_grad: float32 [768, 3072], P(None, 'narrow')
- b_up_grad: float32 [3072], P('narrow')
- w_down_grad: float32 [3072, 768], P('narrow')
- b_down_grad: float32 [768], replicated
- gain_ffn_grad: float32 [768], replicated
- shift_ffn_grad: float32 [768], replicated
The draws below stay inside these ranges and needn't reach their ends.
Inputs may be any that keep to these rules, and one draw needn't show every extreme that they name: `item_lengths`: the 4 entries of each index of wide list its items in token order, each of 512 or 1024 tokens, together 2048, followed by zeros; some index of wide holds only items of 1024 tokens.
All inputs are finite; a program needn't handle non-finite values.
Results may differ from the reference program's by a relative error of at most 0.02.
Values may be sent and summed in bfloat16 or wider, within the bound.
No kernel may reach another device: no remote copies, remote signals or barrier semaphores. Data moves between devices by JAX's collectives and lax.ppermute only.
A program may use at most 128 MiB of HBM per device.

```python
import jax
import jax.numpy as jnp
from jax import lax

D = 768
HD = 64
FF = 3072
BLOCK = 512
TOK_DEV = 2048
TOKENS = 16384
N_WIDE = 8


def draw_item_lengths(key, part):
    slot_count = TOK_DEV // BLOCK
    long_counts = jax.random.randint(jax.random.fold_in(key, 11), (N_WIDE,), 0, slot_count // 2 + 1)
    chosen = jax.random.randint(jax.random.fold_in(key, 12), (), 0, N_WIDE)
    long_counts = jnp.where(jnp.arange(N_WIDE) == chosen, slot_count // 2, long_counts)
    item_counts = slot_count - long_counts
    order_keys = jax.random.split(jax.random.fold_in(key, 13), N_WIDE)
    ranks_source = jax.vmap(lambda sub_key: jax.random.permutation(sub_key, slot_count))(order_keys)
    slot_index = jnp.arange(slot_count)
    live_slot = slot_index[None, :] < item_counts[:, None]
    below_mask = (ranks_source[:, None, :] < ranks_source[:, :, None]) & live_slot[:, None, :]
    item_rank = jnp.sum(below_mask.astype(jnp.int32), axis=2)
    is_long = live_slot & (item_rank < long_counts[:, None])
    lengths = jnp.where(live_slot, BLOCK * (1 + is_long.astype(jnp.int32)), 0)
    return lengths.reshape(-1).astype(jnp.int32)


def shard_levels(key, extent, shards, least, largest):
    loudness, own = 1.0, jax.random.fold_in(key, 6)
    for position, parts in shards:
        steps = jnp.exp(jax.random.uniform(jax.random.fold_in(own, position), (parts,), jnp.float32, least / len(shards), largest / len(shards)))
        loudness = loudness * jnp.repeat(steps, extent[position] // parts).reshape([-1 if axis == position else 1 for axis in range(len(extent))])
    return loudness


def gaussian(rng, extent, scale, limit, pieces=(), kind=jnp.bfloat16):
    gain = shard_levels(rng, extent, pieces, -0.22, 0.18) if pieces else 1.0
    entries = jax.random.normal(rng, extent, jnp.float32) * scale * gain
    return jnp.minimum(jnp.maximum(entries, -limit), limit).astype(kind)


def setup_inputs(seed: int = 0) -> dict:
    streams_of = jax.random.split(jax.random.key(seed), 19)
    return {
        "tokens": gaussian(streams_of[0], (TOKENS, D), 1.0, 6.0, ((0, 32),)),
        "item_lengths": draw_item_lengths(jax.random.fold_in(streams_of[18], 71), 0),
        "w_query": gaussian(streams_of[2], (D, D), (D // 2) ** -0.5, 0.3125, ((1, 4),)),
        "b_query": gaussian(streams_of[3], (D,), 0.2, 1.25, ((0, 4),)),
        "w_key": gaussian(streams_of[4], (D, D), (D // 2) ** -0.5, 0.3125, ((1, 4),)),
        "w_value": gaussian(streams_of[5], (D, D), D ** -0.5, 0.21875, ((1, 4),)),
        "b_value": gaussian(streams_of[6], (D,), 0.2, 1.25, ((0, 4),)),
        "w_out": gaussian(streams_of[7], (D, D), (D // 16) ** -0.5, 0.875, ((0, 4),)),
        "b_out": gaussian(streams_of[8], (D,), 0.2, 1.25),
        "gain_attn": jnp.clip(1.0 + 0.1 * jax.random.normal(streams_of[9], (D,), jnp.float32), 0.5, 1.5).astype(jnp.bfloat16),
        "shift_attn": gaussian(streams_of[10], (D,), 0.2, 1.25),
        "w_up": gaussian(streams_of[11], (D, FF), D ** -0.5, 0.21875, ((1, 4),)),
        "b_up": gaussian(streams_of[12], (FF,), 0.2, 1.25, ((0, 4),)),
        "w_down": gaussian(streams_of[13], (FF, D), FF ** -0.5, 0.109375, ((0, 4),)),
        "b_down": gaussian(streams_of[14], (D,), 0.2, 1.25),
        "gain_ffn": jnp.clip(1.0 + 0.1 * jax.random.normal(streams_of[15], (D,), jnp.float32), 0.5, 1.5).astype(jnp.bfloat16),
        "shift_ffn": gaussian(streams_of[16], (D,), 0.2, 1.25),
        "out_grad": gaussian(streams_of[17], (TOKENS, D), 1.0, 6.0, ((0, 32),)),
    }


@jax.custom_vjp
def low(v):
    return lax.optimization_barrier(v.astype(jnp.bfloat16)).astype(jnp.float32)

@jax.custom_vjp
def low_back(v):
    return v

def low_keep(v):
    return (low(v), None)

def low_pass(kept, grad):
    return (grad,)

def back_keep(v):
    return (v, None)

def back_low(kept, grad):
    return (low(grad),)
low.defvjp(low_keep, low_pass)
low_back.defvjp(back_keep, back_low)
norm_eps = 1e-12
masked_score = -1e+30
highest = lax.Precision.HIGHEST

def matmul(left, right):
    return jnp.dot(left, right, precision=highest, preferred_element_type=jnp.float32)

def item_layout(item_lengths, block_rows, block_count):
    item_ends = jnp.cumsum(item_lengths)
    item_starts = item_ends - item_lengths
    block_first = jnp.arange(block_count, dtype=jnp.int32) * block_rows
    owner_item = lax.optimization_barrier(jnp.sum((item_ends[None, :] <= block_first[:, None]).astype(jnp.int32), axis=1))
    picker = owner_item[:, None] == jnp.arange(item_lengths.shape[0], dtype=jnp.int32)[None, :]
    block_start = lax.optimization_barrier(jnp.sum(jnp.where(picker, item_starts[None, :], 0), axis=1)).astype(jnp.int32)
    block_length = lax.optimization_barrier(jnp.sum(jnp.where(picker, item_lengths[None, :], 0), axis=1)).astype(jnp.int32)
    return (block_start, block_length)

def layer_norm(residual, gain_vec, shift_vec):
    centre = lax.optimization_barrier(jnp.mean(residual, axis=1, keepdims=True))
    spread = residual - centre
    inverse = lax.rsqrt(lax.optimization_barrier(jnp.mean(spread * spread, axis=1, keepdims=True)) + norm_eps)
    return spread * inverse * gain_vec + shift_vec

def attention(query_rows, key_rows, value_rows, block_start, block_length):
    token_count, head_cols = query_rows.shape
    head_count = head_cols // HD
    window_rows = 2 * BLOCK
    query_blocks = query_rows.reshape(token_count // BLOCK, BLOCK, head_cols)

    def one_block(inputs):
        query_block, item_start, item_length = inputs
        window_start = jnp.minimum(item_start, token_count - window_rows).astype(jnp.int32)
        window_keys = lax.dynamic_slice_in_dim(key_rows, window_start, window_rows, 0).reshape(window_rows, head_count, HD)
        window_values = lax.dynamic_slice_in_dim(value_rows, window_start, window_rows, 0).reshape(window_rows, head_count, HD)
        queries = query_block.reshape(BLOCK, head_count, HD)
        raw_scores = jnp.einsum('qhd,khd->hqk', queries, window_keys, precision=highest) * HD ** (-0.5)
        positions = window_start + jnp.arange(window_rows, dtype=jnp.int32)
        inside = (positions >= item_start) & (positions < item_start + item_length)
        scores = low_back(jnp.where(inside[None, None, :], raw_scores, masked_score))
        row_top = lax.optimization_barrier(jnp.max(scores, axis=2, keepdims=True))
        shifted = jnp.exp(scores - row_top)
        probabilities = low(shifted / lax.optimization_barrier(jnp.sum(shifted, axis=2, keepdims=True)))
        context = jnp.einsum('hqk,khd->qhd', probabilities, window_values, precision=highest)
        return context.reshape(BLOCK, head_cols)
    context_blocks = lax.map(jax.checkpoint(one_block), (query_blocks, block_start, block_length))
    return context_blocks.reshape(token_count, head_cols)

def group_layer(group_tokens, weights_in, group_lengths):
    w_query, b_query, w_key, w_value, b_value, w_out, b_out, gain_attn, shift_attn, w_up, b_up, w_down, b_down, gain_ffn, shift_ffn = weights_in
    block_start, block_length = item_layout(group_lengths, BLOCK, TOK_DEV // BLOCK)
    query_rows = low(low_back(matmul(group_tokens, w_query) + b_query))
    key_rows = low(low_back(matmul(group_tokens, w_key)))
    value_rows = low(low_back(matmul(group_tokens, w_value) + b_value))
    context = low(low_back(attention(query_rows, key_rows, value_rows, block_start, block_length)))
    attn_branch = low_back(matmul(context, w_out) + b_out)
    normed = layer_norm(group_tokens + attn_branch, gain_attn, shift_attn)
    pre_act = low_back(matmul(low(normed), w_up) + b_up)
    activated = low(jax.nn.gelu(pre_act, approximate=False))
    ffn_branch = low_back(matmul(activated, w_down) + b_down)
    return layer_norm(normed + ffn_branch, gain_ffn, shift_ffn)

def reference(tokens, item_lengths, w_query, b_query, w_key, w_value, b_value, w_out, b_out, gain_attn, shift_attn, w_up, b_up, w_down, b_down, gain_ffn, shift_ffn, out_grad):
    weights_all = (w_query, b_query, w_key, w_value, b_value, w_out, b_out, gain_attn, shift_attn, w_up, b_up, w_down, b_down, gain_ffn, shift_ffn)
    weights_all = jax.tree.map(lambda weight_in: weight_in.astype(jnp.float32), weights_all)
    token_groups = tokens.astype(jnp.float32).reshape(N_WIDE, TOK_DEV, D)
    grad_groups = out_grad.astype(jnp.float32).reshape(N_WIDE, TOK_DEV, D)
    length_groups = item_lengths.reshape(N_WIDE, TOK_DEV // BLOCK)

    def per_group(totals, inputs):
        group_tokens, group_grad, group_lengths = inputs
        outputs, pullback = jax.vjp(lambda token_in, weight_set: group_layer(token_in, weight_set, group_lengths), group_tokens, weights_all)
        token_part, weight_grads = pullback(group_grad)
        totals = jax.tree.map(lambda left_sum, right_sum: left_sum + right_sum, totals, weight_grads)
        return (totals, (outputs, token_part))
    zero_grads = jax.tree.map(jnp.zeros_like, weights_all)
    totals, (outputs, token_parts) = lax.scan(per_group, zero_grads, (token_groups, grad_groups, length_groups))
    return (outputs.reshape(TOKENS, D).astype(jnp.bfloat16), token_parts.reshape(TOKENS, D), totals[0], totals[1], totals[2], totals[3], totals[4], totals[5], totals[6], totals[7], totals[8], totals[9], totals[10], totals[11], totals[12], totals[13], totals[14])
```

```python
import functools

import jax
import jax.numpy as jnp
from jax import lax
from jax.experimental import pallas as pl
from jax.experimental.pallas import tpu as pltpu
from jax.sharding import PartitionSpec as P

HD = 64
F32 = jnp.float32
BF = jnp.bfloat16
MIB = 1 << 20

norm_eps = 1e-12
masked_shift = 1e30
half_root = 0.7071067811865476
inv_root_two_pi = 0.3989422804014327
score_scale = HD**-0.5

VM = pl.BlockSpec(memory_space=pltpu.VMEM)
SM = pl.BlockSpec(memory_space=pltpu.SMEM)
ANY = pl.BlockSpec(memory_space=pl.ANY)


def dot(left, right):
    return jnp.dot(left, right, preferred_element_type=F32)


def contract_rows(left, right):
    return lax.dot_general(left, right, (((0,), (0,)), ((), ())), preferred_element_type=F32)


def contract_cols(left, right):
    return lax.dot_general(left, right, (((1,), (1,)), ((), ())), preferred_element_type=F32)


def shape(dims, dtype):
    return jax.ShapeDtypeStruct(dims, dtype)


def row(ref):
    return ref[...].astype(F32).reshape(1, -1)


def call(kernel, name, out_shape, args, smem=0, scratch=(), vmem=24, aliases=None, after=()):
    count = len(args)

    def body(*refs):
        kernel(*refs[:count], *refs[count + len(after) :])

    return pl.pallas_call(
        body,
        out_shape=tuple(out_shape),
        in_specs=[SM] * smem + [VM] * (count - smem) + [ANY] * len(after),
        out_specs=tuple([VM] * len(out_shape)),
        scratch_shapes=list(scratch),
        input_output_aliases=aliases or {},
        compiler_params=pltpu.CompilerParams(vmem_limit_bytes=vmem * MIB),
        cost_estimate=pl.CostEstimate(flops=1000, transcendentals=0, bytes_accessed=1000),
        name=name,
    )(*args, *after)


def joint_kernel(wq_ref, wk_ref, wv_ref, bq_ref, bv_ref, bu_ref, out_ref, tail_s):
    cols = wq_ref.shape[0]
    for i, ref in enumerate((wq_ref, wk_ref, wv_ref)):
        out_ref[i * cols : (i + 1) * cols] = ref[...]
    tail_s[...] = jnp.zeros_like(tail_s)
    tail_s[0:1, 0:cols] = row(bq_ref)
    tail_s[1:2, 0:cols] = row(bv_ref)
    tail_s[2:3, :] = row(bu_ref)
    out_ref[3 * cols : 3 * cols + 16] = tail_s[...].astype(BF)


def pack_joint(w_query, w_key, w_value, b_query, b_value, b_up):
    width, cols = w_query.shape
    return call(
        joint_kernel, "pack_joint", [shape((3 * cols + 16, width), BF)],
        (w_query.T, w_key.T, w_value.T, b_query, b_value, b_up),
        scratch=[pltpu.VMEM((16, width), F32)], vmem=8,
    )[0]


def neighbour(lens_ref, me_ref, rows):
    me = me_ref[0]
    here = me * rows
    first = jnp.int32(0)
    start = jnp.int32(0)
    length = jnp.int32(0)
    for j in range(lens_ref.shape[0]):
        n = lens_ref[j]
        inside = (first <= here) & (here < first + n)
        start = jnp.where(inside, first, start)
        length = jnp.where(inside, n, length)
        first = first + n
    other = jnp.where(start == here, me + 1, me - 1)
    return length > rows, other == (me ^ 1)


def pick_other(use_core, core_ref, mid_ref, out_s):
    @pl.when(use_core)
    def _():
        out_s[...] = core_ref[...]

    @pl.when(jnp.logical_not(use_core))
    def _():
        out_s[...] = mid_ref[...]


def attend_kernel(
    lens_ref, me_ref, own_ref, core_ref, mid_ref, a_ref,
    ctx_ref, lse_ref, q_ref, k_ref, v_ref,
    oth_s, qt_s, vt_s, ct_s, *, tile,
):
    rows = own_ref.shape[0]
    cols = q_ref.shape[1]
    flag, use_core = neighbour(lens_ref, me_ref, rows)
    pick_other(use_core, core_ref, mid_ref, oth_s)
    tail = a_ref[3 * cols : 3 * cols + 16].astype(F32)
    wk = a_ref[cols : 2 * cols]
    wv = a_ref[2 * cols : 3 * cols]
    own = own_ref[...]
    q = (contract_cols(own, a_ref[0:cols]) + tail[0:1, 0:cols]).astype(BF)
    q = q * jnp.asarray(score_scale, BF)
    q_ref[...] = q
    qt_s[...] = q.T
    k_ref[0:rows] = contract_cols(own, wk).astype(BF)
    v_own = (contract_cols(own, wv) + tail[1:2, 0:cols]).astype(BF)
    v_ref[0:rows] = v_own
    vt_s[:, 0:rows] = v_own.T
    other = oth_s[...]
    k_ref[rows : 2 * rows] = contract_cols(other, wk).astype(BF)
    v_other = (contract_cols(other, wv) + tail[1:2, 0:cols]).astype(BF)
    v_ref[rows : 2 * rows] = v_other
    vt_s[:, rows : 2 * rows] = v_other.T
    for h in range(cols // HD):
        hs = slice(h * HD, (h + 1) * HD)
        for t in range(rows // tile):
            ts = slice(t * tile, (t + 1) * tile)
            q_h = qt_s[hs, ts]
            s_own = dot(k_ref[0:rows, hs], q_h)
            s_other = dot(k_ref[rows : 2 * rows, hs], q_h)
            top_own = jnp.max(s_own, axis=0, keepdims=True)
            top_other = jnp.max(s_other, axis=0, keepdims=True)
            top = jnp.where(flag, jnp.maximum(top_own, top_other), top_own)
            p_own = jnp.exp(s_own - top)
            p_other = jnp.exp(s_other - jnp.where(flag, top, masked_shift))
            total = jnp.sum(p_own, axis=0, keepdims=True) + jnp.sum(p_other, axis=0, keepdims=True)
            c = dot(vt_s[hs, 0:rows], p_own.astype(BF)) + dot(
                vt_s[hs, rows : 2 * rows], p_other.astype(BF)
            )
            ct_s[hs, ts] = c * (1.0 / total)
            lse_ref[h : h + 1, ts] = top + jnp.log(total)
    ctx_ref[...] = ct_s[...].T.astype(BF)


def attend(lens, me, own, tok_core, tok_mid, a, after=(), tile=256):
    rows, width = own.shape
    cols = (a.shape[0] - 16) // 3
    return call(
        functools.partial(attend_kernel, tile=tile), "attend",
        [
            shape((rows, cols), BF), shape((cols // HD, rows), F32), shape((rows, cols), BF),
            shape((2 * rows, cols), BF), shape((2 * rows, cols), BF),
        ],
        (lens, me, own, tok_core, tok_mid, a), smem=2, after=after,
        scratch=[
            pltpu.VMEM((rows, width), BF), pltpu.VMEM((cols, rows), BF),
            pltpu.VMEM((cols, 2 * rows), BF), pltpu.VMEM((cols, rows), F32),
        ],
    )


def attend_back_kernel(
    lens_ref, me_ref, own_ref, core_ref, mid_ref, a_ref, wo_ref, g_ref,
    ctx_ref, lse_ref, q_ref, k_ref, v_ref, tok_in_ref, oth_in_ref,
    qk_ref, vo_ref, tok_ref, oth_ref, bq_ref, bv_ref,
    oth_s, gt_s, qt_s, kt_s, dqt_s, dk_s, dv_s, *, tile,
):
    rows, cols = q_ref.shape
    flag, use_core = neighbour(lens_ref, me_ref, rows)
    pick_other(use_core, core_ref, mid_ref, oth_s)
    attn_grad = g_ref[...]
    g = contract_cols(attn_grad, wo_ref[...]).astype(BF)
    gt_s[...] = g.T
    q = q_ref[...]
    qt_s[...] = q.T
    kt_s[...] = k_ref[...].T
    own = slice(0, rows)
    other = slice(rows, 2 * rows)
    for h in range(cols // HD):
        hs = slice(h * HD, (h + 1) * HD)
        for t in range(rows // tile):
            ts = slice(t * tile, (t + 1) * tile)
            q_h = qt_s[hs, ts]
            g_h = gt_s[hs, ts]
            lse = lse_ref[h : h + 1, ts]
            p_own = jnp.exp(dot(k_ref[own, hs], q_h) - lse)
            p_other = jnp.exp(dot(k_ref[other, hs], q_h) - jnp.where(flag, lse, masked_shift))
            dp_own = dot(v_ref[own, hs], g_h)
            dp_other = dot(v_ref[other, hs], g_h)
            row_dot = jnp.sum(p_own * dp_own, axis=0, keepdims=True) + jnp.sum(
                p_other * dp_other, axis=0, keepdims=True
            )
            ds_own = (p_own * (dp_own - row_dot)).astype(BF)
            ds_other = (p_other * (dp_other - row_dot)).astype(BF)
            dqt_s[hs, ts] = dot(kt_s[hs, own], ds_own) + dot(kt_s[hs, other], ds_other)
            q_n = q[ts, hs]
            g_n = g[ts, hs]
            parts = (
                dot(ds_own, q_n), dot(ds_other, q_n),
                dot(p_own.astype(BF), g_n), dot(p_other.astype(BF), g_n),
            )
            if t == 0:
                dk_s[own, hs], dk_s[other, hs], dv_s[own, hs], dv_s[other, hs] = parts
            else:
                dk_s[own, hs] += parts[0]
                dk_s[other, hs] += parts[1]
                dv_s[own, hs] += parts[2]
                dv_s[other, hs] += parts[3]
    dqt = (dqt_s[...] * score_scale).astype(BF)
    dq = dqt.T
    dk = dk_s[...].astype(BF)
    dv = dv_s[...].astype(BF)
    dkt = dk.T
    dvt = dv.T
    tok = own_ref[...]
    oth = oth_s[...]
    qk_ref[0:cols] = dot(dqt, tok).astype(BF)
    qk_ref[cols : 2 * cols] = (dot(dkt[:, own], tok) + dot(dkt[:, other], oth)).astype(BF)
    vo_ref[0:cols] = (dot(dvt[:, own], tok) + dot(dvt[:, other], oth)).astype(BF)
    vo_ref[cols : 2 * cols] = contract_rows(ctx_ref[...], attn_grad).astype(BF)
    wq = a_ref[0:cols]
    wk = a_ref[cols : 2 * cols]
    wv = a_ref[2 * cols : 3 * cols]
    tok_ref[...] = tok_in_ref[...] + dot(dq, wq) + dot(dk[own], wk) + dot(dv[own], wv)
    oth_ref[...] = oth_in_ref[...] + dot(dk[other], wk) + dot(dv[other], wv)
    bq_ref[...] = jnp.sum(dq.astype(F32), axis=0, keepdims=True)
    bv_ref[...] = jnp.sum(dv.astype(F32), axis=0, keepdims=True)


def attend_back(
    lens, me, own, tok_core, tok_mid, a, w_out, attn_grad, saved, tok_acc, oth_acc, after=(), tile=256
):
    rows, width = own.shape
    ctx, lse, q, k, v = saved
    cols = q.shape[1]
    return call(
        functools.partial(attend_back_kernel, tile=tile), "attend_back",
        [
            shape((2 * cols, width), BF), shape((2 * cols, width), BF),
            shape((rows, width), F32), shape((rows, width), F32),
            shape((1, cols), F32), shape((1, cols), F32),
        ],
        (
            lens, me, own, tok_core, tok_mid, a, w_out, attn_grad, ctx, lse, q, k, v,
            tok_acc, oth_acc,
        ),
        smem=2,
        scratch=[
            pltpu.VMEM((rows, width), BF),
            pltpu.VMEM((cols, rows), BF), pltpu.VMEM((cols, rows), BF),
            pltpu.VMEM((cols, 2 * rows), BF), pltpu.VMEM((cols, rows), F32),
            pltpu.VMEM((2 * rows, cols), F32), pltpu.VMEM((2 * rows, cols), F32),
        ],
        vmem=32,
        aliases={13: 2, 14: 3}, after=after,
    )


def unit_of(residual):
    centre = jnp.mean(residual, axis=1, keepdims=True)
    spread = residual - centre
    inverse = lax.rsqrt(jnp.mean(spread * spread, axis=1, keepdims=True) + norm_eps)
    return spread * inverse, inverse


def norm_back(upstream, unit_rows, inverse, gain):
    unit_grad = upstream * gain
    return inverse * (
        unit_grad
        - jnp.mean(unit_grad, axis=1, keepdims=True)
        - unit_rows * jnp.mean(unit_grad * unit_rows, axis=1, keepdims=True)
    )


def first_norm_kernel(
    tok_ref, c0_ref, c1_ref, c2_ref, c3_ref, a0_ref, a1_ref, a2_ref, a3_ref,
    bo_ref, gain_ref, shift_ref, unit_ref, inv_ref, low_ref,
):
    resid = tok_ref[...].astype(F32) + row(bo_ref)
    for c_ref, a_ref in ((c0_ref, a0_ref), (c1_ref, a1_ref), (c2_ref, a2_ref), (c3_ref, a3_ref)):
        resid = resid + dot(c_ref[...], a_ref[...])
    unit, inverse = unit_of(resid)
    unit_ref[...] = unit
    inv_ref[...] = inverse
    low_ref[...] = (unit * row(gain_ref) + row(shift_ref)).astype(BF)


def first_norm(tokens, ctxs, outs, b_out, gain, shift, after=()):
    rows, width = tokens.shape
    return call(
        first_norm_kernel, "first_norm",
        [shape((rows, width), F32), shape((rows, 1), F32), shape((rows, width), BF)],
        (tokens, *ctxs, *outs, b_out, gain, shift), after=after,
    )


def up_down(low_ref, a_ref, up_refs, down_ref, act_ref, slope_ref):
    units = act_ref.shape[1]
    at = a_ref.shape[0] - 16
    bias = a_ref[at : at + 16].astype(F32)[2:3]
    step = 256
    for c in range(units // step):
        cs = slice(c * step, (c + 1) * step)
        pre = bias[:, cs]
        at = 0
        for up_ref in up_refs:
            depth = up_ref.shape[0]
            pre = pre + dot(low_ref[:, at : at + depth], up_ref[:, cs])
            at += depth
        phi = 0.5 + 0.5 * lax.erf(pre * half_root)
        act_ref[:, cs] = (pre * phi).astype(BF)
        slope_ref[:, cs] = (phi + pre * jnp.exp(-0.5 * pre * pre) * inv_root_two_pi).astype(BF)
    return dot(act_ref[...], down_ref[...])


def ffn_near_kernel(
    low_ref, a0_ref, a1_ref, u0_ref, u1_ref, d0_ref, d1_ref,
    act0_ref, act1_ref, sl0_ref, sl1_ref, sum_ref,
):
    part = up_down(low_ref, a0_ref, (u0_ref,), d0_ref, act0_ref, sl0_ref)
    sum_ref[...] = part + up_down(low_ref, a1_ref, (u1_ref,), d1_ref, act1_ref, sl1_ref)


def ffn_near(low, joints, ups, downs, after=()):
    rows, width = low.shape
    units = ups[0].shape[1]
    piece = shape((rows, units), BF)
    return call(
        ffn_near_kernel, "ffn_near", [piece, piece, piece, piece, shape((rows, width), F32)],
        (low, *joints, *ups, *downs), after=after,
        vmem=32,
    )


def ffn_far_kernel(
    low_ref, a0_ref, a1_ref, u0a_ref, u0b_ref, u1a_ref, u1b_ref, d0_ref, d1_ref,
    unit_ref, sum_ref, out_grad_ref, gain1_ref, shift1_ref, bd_ref, gain2_ref, shift2_ref,
    act0_ref, act1_ref, sl0_ref, sl1_ref, out_ref, resid_ref, low_grad_ref,
    bd_out, gain_out, shift_out,
):
    part = sum_ref[...] + up_down(low_ref, a0_ref, (u0a_ref, u0b_ref), d0_ref, act0_ref, sl0_ref)
    part = part + up_down(low_ref, a1_ref, (u1a_ref, u1b_ref), d1_ref, act1_ref, sl1_ref)
    resid = unit_ref[...] * row(gain1_ref) + (row(shift1_ref) + row(bd_ref)) + part
    unit, inverse = unit_of(resid)
    gain = row(gain2_ref)
    out_ref[...] = (unit * gain + row(shift2_ref)).astype(BF)
    upstream = out_grad_ref[...].astype(F32)
    gain_out[...] = jnp.sum(upstream * unit, axis=0, keepdims=True)
    shift_out[...] = jnp.sum(upstream, axis=0, keepdims=True)
    back = norm_back(upstream, unit, inverse, gain)
    resid_ref[...] = back
    low_grad = back.astype(BF)
    low_grad_ref[...] = low_grad
    bd_out[...] = jnp.sum(low_grad.astype(F32), axis=0, keepdims=True)


def ffn_far(
    low, joints, ups, downs, unit, near_sum, out_grad, gain1, shift1, b_down, gain2, shift2, after=()
):
    rows, width = low.shape
    units = downs[0].shape[0]
    piece = shape((rows, units), BF)
    vec = shape((1, width), F32)
    return call(
        ffn_far_kernel, "ffn_far",
        [
            piece, piece, piece, piece,
            shape((rows, width), BF), shape((rows, width), F32), shape((rows, width), BF),
            vec, vec, vec,
        ],
        (
            low, *joints, *ups[0], *ups[1], *downs, unit, near_sum, out_grad,
            gain1, shift1, b_down, gain2, shift2,
        ),
        after=after,
        vmem=40,
    )


def ffn_back_kernel(g_ref, low_ref, act_ref, slope_ref, sum_in_ref, down_ref, *refs):
    up_refs = refs[:-5]
    down_grad_ref, up_grad_ref, bias_ref, sum_ref, pre_s = refs[-5:]
    g = g_ref[...]
    units = down_ref.shape[0]
    down_grad_ref[...] = contract_rows(act_ref[...], g).astype(BF)
    step = 256
    for c in range(units // step):
        cs = slice(c * step, (c + 1) * step)
        pre = (contract_cols(g, down_ref[cs]) * slope_ref[:, cs].astype(F32)).astype(BF)
        pre_s[:, cs] = pre
        bias_ref[:, cs] = jnp.sum(pre.astype(F32), axis=0, keepdims=True)
    pre = pre_s[...]
    up_grad_ref[...] = contract_rows(low_ref[...], pre).astype(BF)
    at = 0
    for up_ref in up_refs:
        cs = slice(at, at + up_ref.shape[0])
        sum_ref[:, cs] = sum_in_ref[:, cs] + contract_cols(pre, up_ref[...])
        at += up_ref.shape[0]


def ffn_back(g, low, act, slope, up, down, acc, after=()):
    rows, width = low.shape
    units = down.shape[0]
    return call(
        ffn_back_kernel, "ffn_back",
        [
            shape((units, width), BF), shape((width, units), BF),
            shape((1, units), F32), shape((rows, width), F32),
        ],
        (g, low, act, slope, acc, down, *up), after=after,
        scratch=[pltpu.VMEM((rows, units), BF)],
        aliases={4: 3}, vmem=32,
    )


def first_norm_back_kernel(
    up_ref, unit_ref, inv_ref, gain_ref, resid_ref, low_ref, bo_out, gain_out, shift_out
):
    upstream = up_ref[...]
    unit = unit_ref[...]
    gain_out[...] = jnp.sum(upstream * unit, axis=0, keepdims=True)
    shift_out[...] = jnp.sum(upstream, axis=0, keepdims=True)
    back = norm_back(upstream, unit, inv_ref[...], row(gain_ref))
    resid_ref[...] = back
    low = back.astype(BF)
    low_ref[...] = low
    bo_out[...] = jnp.sum(low.astype(F32), axis=0, keepdims=True)


def first_norm_back(upstream, unit, inverse, gain, after=()):
    rows, width = unit.shape
    vec = shape((1, width), F32)
    return call(
        first_norm_back_kernel, "first_norm_back",
        [shape((rows, width), F32), shape((rows, width), BF), vec, vec, vec],
        (upstream, unit, inverse, gain), after=after,
    )


def gather_small_kernel(me_ref, *refs):
    out_ref = refs[-1]
    bq, bv, bu, rest = refs[0:4], refs[4:8], refs[8:12], refs[12:18]
    out_ref[...] = jnp.zeros_like(out_ref)
    cols = bq[0].shape[1]
    for r in range(4):
        at = 3 * (me_ref[0] ^ r)
        out_ref[pl.ds(at, 1), 0:cols] = bq[r][...]
        out_ref[pl.ds(at + 1, 1), 0:cols] = bv[r][...]
        out_ref[pl.ds(at + 2, 1), :] = bu[r][...]
    for i, ref in enumerate(rest):
        out_ref[12 + i : 13 + i, :] = ref[...]


def gather_small(me, bq, bv, bu, rest):
    width = rest[0].shape[1]
    return call(
        gather_small_kernel, "gather_small", [shape((24, width), F32)],
        (me, *bq, *bv, *bu, *rest), smem=1, vmem=4,
    )[0]


def spread_small_kernel(me_ref, in_ref, bq_ref, bv_ref, bu_ref, *rest):
    cols = bq_ref.shape[0]
    at = 3 * me_ref[0]
    bq_ref[...] = in_ref[pl.ds(at, 1), 0:cols].reshape(cols)
    bv_ref[...] = in_ref[pl.ds(at + 1, 1), 0:cols].reshape(cols)
    bu_ref[...] = in_ref[pl.ds(at + 2, 1), :].reshape(-1)
    for i, ref in enumerate(rest):
        ref[...] = in_ref[12 + i : 13 + i, :].reshape(-1)


def spread_small(me, sums, cols, units):
    width = sums.shape[1]
    return call(
        spread_small_kernel, "spread_small",
        [shape((cols,), F32), shape((cols,), F32), shape((units,), F32)] + [shape((width,), F32)] * 6,
        (me, sums), smem=1, vmem=4,
    )


def swap(a, axis, distance):
    size = lax.axis_size(axis)
    return lax.ppermute(a, axis, [(i, i ^ distance) for i in range(size)])


def to_core(a):
    return swap(a, "narrow", 1)


def to_chip(a):
    return swap(a, "narrow", 2)


def to_middle(a):
    return lax.ppermute(a, "narrow", [(1, 2), (2, 1)])


def wide_bits():
    size = lax.axis_size("wide")
    bits = []
    while size > 1:
        assert size % 2 == 0
        bits.append(len(bits))
        size //= 2
    return bits


def sum_small(a):
    for distance in (1, 2):
        a = a + swap(a, "narrow", distance)
    for bit in wide_bits():
        a = a + swap(a, "wide", 1 << bit)
    return a


def half_of(a, which):
    rows = a.shape[0] // 2
    return lax.dynamic_slice_in_dim(a, which * rows, rows, 0)


def side_of(bit):
    return (lax.axis_index("wide") >> bit) & 1


def in_order(side, mine, got):
    return jnp.where(side == 0, jnp.concatenate([mine, got]), jnp.concatenate([got, mine]))


def hold(a, *others):
    return lax.optimization_barrier((a, *others))[0]


def gather_wide(piece, waits=()):
    got = None
    for i, bit in enumerate(reversed(wide_bits())):
        got = swap(piece, "wide", 1 << bit)
        if i < len(waits) and waits[i] is not None:
            got = hold(got, waits[i])
        piece = in_order(side_of(bit), piece, got)
    return piece


def own_piece(a):
    rows = a.shape[0] // lax.axis_size("wide")
    at = 0
    for bit in wide_bits():
        at = 2 * at + side_of(bit)
    return lax.dynamic_slice_in_dim(a, at * rows, rows, 0)


def add_low(*terms):
    total = terms[0].astype(F32)
    for term in terms[1:]:
        total = total + term.astype(F32)
    return total.astype(BF)


def halve(a, bit):
    side = side_of(bit)
    return half_of(a, 1 - side), half_of(a, side)


class Scatter:
    def __init__(self, a):
        self.bits = wide_bits()
        self.a = a
        self.got = []
        self.step = 0
        self.send()

    def send(self):
        bit = self.bits[self.step]
        if bit < 3:
            out, self.keep = halve(self.a, bit)
        else:
            out, self.keep = self.a, self.a
        self.got.append(swap(out, "wide", 1 << bit))

    def advance(self, *waits):
        got = hold(self.got[-1], *waits) if waits else self.got[-1]
        self.a = add_low(self.keep, got)
        self.step += 1
        if self.step < len(self.bits):
            self.send()
            return False
        return True

    def finish(self):
        while self.step < len(self.bits):
            self.advance()
        return self.a


def gather_halves(a):
    for bit in reversed(wide_bits()[:3]):
        a = in_order(side_of(bit), a, swap(a, "wide", 1 << bit))
    return a.astype(F32)


def local(
    tokens, item_lengths, w_query, b_query, w_key, w_value, b_value, w_out, b_out,
    gain_attn, shift_attn, w_up, b_up, w_down, b_down, gain_ffn, shift_ffn, out_grad,
):
    rows, width = tokens.shape
    cols = w_query.shape[1]
    units = w_up.shape[1]
    assert lax.axis_size("narrow") == 4
    me = lax.axis_index("narrow").reshape(1)

    half = width // 2
    up_low, up_high = w_up[:half], w_up[half:]
    down_piece = to_chip(own_piece(w_down))
    high_piece = to_chip(own_piece(up_high))
    tok_mid = to_middle(tokens)
    tok_core = to_core(tokens)
    joint = pack_joint(w_query, w_key, w_value, b_query, b_value, b_up)
    joint_core = to_core(joint)
    joint_chip = to_chip(joint)

    saved = []

    def forward(r, block, *after):
        saved.append(attend(item_lengths, me, tokens, tok_core, tok_mid, block, after))
        return saved[-1][1]

    mark0 = forward(0, joint)
    out_chip = to_chip(hold(w_out, mark0))
    out_core = to_core(hold(w_out, mark0))
    mark1 = forward(1, joint_core, mark0)
    joint_diag = to_core(hold(joint_chip, mark1))
    low_chip = to_chip(hold(up_low, mark1))
    up_core = to_core(hold(w_up, mark1))
    down_chip = gather_wide(down_piece, (None, mark0, mark1))
    high_chip = gather_wide(high_piece, (None, mark0, mark1))
    mark2 = forward(2, joint_chip, mark1)
    out_diag = to_core(hold(out_chip, mark2))
    down_core = to_core(hold(w_down, mark2))
    mark3 = forward(3, joint_diag, mark2)
    down_diag = to_core(hold(down_chip, mark2))
    high_diag = to_core(hold(high_chip, mark3))
    low_diag = to_core(hold(low_chip, mark3))
    joints = [joint, joint_core, joint_chip, joint_diag]
    outs = [w_out, out_core, out_chip, out_diag]
    downs = [w_down, down_core, down_chip, down_diag]
    ups = [(w_up,), (up_core,), (low_chip, high_chip), (low_diag, high_diag)]

    unit_one, inv_one, low = first_norm(
        tokens, [s[0] for s in saved], outs, b_out, gain_attn, shift_attn
    )
    act0, act1, sl0, sl1, near = ffn_near(low, joints[:2], [w_up, up_core], downs[:2])
    (
        act2, act3, sl2, sl3, layer_out, resid_two, ffn_grad, b_down_part, gain_ffn_part,
        shift_ffn_part,
    ) = ffn_far(
        low, joints[2:], ups[2:], downs[2:], unit_one, near, out_grad,
        gain_attn, shift_attn, b_down, gain_ffn, shift_ffn,
    )
    acts = (act0, act1, act2, act3)
    slopes = (sl0, sl1, sl2, sl3)

    acc = resid_two
    down_parts, up_parts, bu_parts = [None] * 4, [None] * 4, [None] * 4

    def back(r, *after):
        nonlocal acc
        down_parts[r], up_parts[r], bu_parts[r], acc = ffn_back(
            ffn_grad, low, acts[r], slopes[r], ups[r], downs[r], acc, after
        )

    back(3)
    up_diag_sum = to_core(up_parts[3])
    down_diag_sum = to_core(down_parts[3])
    back(2)
    back(1, up_diag_sum, down_diag_sum)
    up_to_chip = to_chip(add_low(up_parts[2], up_diag_sum))
    far_down = Scatter(add_low(down_parts[2], down_diag_sum))
    down_core_sum = to_core(down_parts[1])
    up_core_sum = to_core(up_parts[1])
    back(0)

    resid_one, attn_grad, b_out_part, gain_attn_part, shift_attn_part = first_norm_back(
        acc, unit_one, inv_one, gain_attn, (down_core_sum,)
    )
    near_down = Scatter(add_low(down_parts[0], down_core_sum))
    tok_acc = resid_one
    oth_acc = jnp.zeros((rows, width), F32)
    qk_parts, vo_parts, bq_parts, bv_parts = [None] * 4, [None] * 4, [None] * 4, [None] * 4

    def back_attend(r, *after):
        nonlocal tok_acc, oth_acc
        qk_parts[r], vo_parts[r], tok_acc, oth_acc, bq_parts[r], bv_parts[r] = attend_back(
            item_lengths, me, tokens, tok_core, tok_mid, joints[r], outs[r], attn_grad, saved[r],
            tok_acc, oth_acc, after,
        )

    back_attend(3, up_core_sum)
    qk_diag = to_core(qk_parts[3])
    vo_diag = to_core(vo_parts[3])
    far_down.advance()
    back_attend(2, far_down.got[0])
    near_down.advance(bq_parts[2])
    far_down.advance(bq_parts[2])
    near_up = Scatter(add_low(up_parts[0], up_core_sum, hold(up_to_chip, bq_parts[2])))
    back_attend(1, near_down.got[0], far_down.got[1], up_to_chip, qk_diag, vo_diag)
    qk_to_chip = to_chip(add_low(qk_parts[2], qk_diag))
    vo_to_chip = to_chip(add_low(vo_parts[2], vo_diag))
    qk_core = to_core(qk_parts[1])
    vo_core = to_core(vo_parts[1])
    back_attend(0, near_down.got[1], far_down.got[2])
    far_piece = to_chip(far_down.finish())
    near_qk = Scatter(add_low(qk_parts[0], qk_core, qk_to_chip))
    near_vo = Scatter(add_low(vo_parts[0], vo_core, vo_to_chip))
    w_down_grad = gather_halves(add_low(near_down.finish(), far_piece))
    w_up_grad = gather_halves(near_up.finish())
    qk_grad = gather_halves(near_qk.finish())
    vo_grad = gather_halves(near_vo.finish())
    oth_low = oth_acc.astype(BF)
    token_grad = take_back(item_lengths, me, tok_acc, to_core(oth_low), to_middle(oth_low))

    small = gather_small(
        me, bq_parts, bv_parts, bu_parts,
        (b_out_part, b_down_part, gain_attn_part, shift_attn_part, gain_ffn_part, shift_ffn_part),
    )
    bq, bv, bu, b_out_g, b_down_g, gain_attn_g, shift_attn_g, gain_ffn_g, shift_ffn_g = spread_small(
        me, sum_small(small), cols, units
    )
    return (
        layer_out,
        token_grad,
        qk_grad[:cols].T,
        bq,
        qk_grad[cols:].T,
        vo_grad[:cols].T,
        bv,
        vo_grad[cols:],
        b_out_g,
        gain_attn_g,
        shift_attn_g,
        w_up_grad,
        bu,
        w_down_grad,
        b_down_g,
        gain_ffn_g,
        shift_ffn_g,
    )


def take_back_kernel(lens_ref, me_ref, tok_ref, core_ref, mid_ref, out_ref):
    flag, use_core = neighbour(lens_ref, me_ref, tok_ref.shape[0])

    @pl.when(jnp.logical_not(flag))
    def _():
        out_ref[...] = tok_ref[...]

    @pl.when(flag & use_core)
    def _():
        out_ref[...] = tok_ref[...] + core_ref[...].astype(F32)

    @pl.when(flag & jnp.logical_not(use_core))
    def _():
        out_ref[...] = tok_ref[...] + mid_ref[...].astype(F32)


def take_back(lens, me, tok_acc, core, mid):
    return call(
        take_back_kernel, "take_back", [shape(tok_acc.shape, F32)],
        (lens, me, tok_acc, core, mid), smem=2, vmem=12,
    )[0]


def solution(mesh):
    rows_spec = P(("wide", "narrow"), None)
    col_spec = P(None, "narrow")
    vec_spec = P("narrow")
    row_spec = P("narrow", None)
    full = P()
    return jax.shard_map(
        local,
        mesh=mesh,
        in_specs=(
            rows_spec, P("wide"), col_spec, vec_spec, col_spec, col_spec, vec_spec, row_spec, full,
            full, full, col_spec, vec_spec, row_spec, full, full, full, rows_spec,
        ),
        out_specs=(
            rows_spec, rows_spec, col_spec, vec_spec, col_spec, col_spec, vec_spec, row_spec, full,
            full, full, col_spec, vec_spec, row_spec, full, full, full,
        ),
        check_vma=False,
    )
```

```python
import functools

import jax
import jax.numpy as jnp
from jax import lax
from jax.experimental import pallas as pl
from jax.experimental.pallas import tpu as pltpu
from jax.sharding import PartitionSpec as P

HD = 64
F32 = jnp.float32
BF = jnp.bfloat16
MIB = 1 << 20

norm_eps = 1e-12
masked_shift = 1e30
half_root = 0.7071067811865476
inv_root_two_pi = 0.3989422804014327
score_scale = HD**-0.5

VM = pl.BlockSpec(memory_space=pltpu.VMEM)
SM = pl.BlockSpec(memory_space=pltpu.SMEM)
ANY = pl.BlockSpec(memory_space=pl.ANY)


def dot(left, right):
    return jnp.dot(left, right, preferred_element_type=F32)


def contract_rows(left, right):
    return lax.dot_general(left, right, (((0,), (0,)), ((), ())), preferred_element_type=F32)


def contract_cols(left, right):
    return lax.dot_general(left, right, (((1,), (1,)), ((), ())), preferred_element_type=F32)


def shape(dims, dtype):
    return jax.ShapeDtypeStruct(dims, dtype)


def row(ref):
    return ref[...].astype(F32).reshape(1, -1)


class Arriving:
    def __init__(self, source, buffer, sem):
        self.buffer = buffer
        self.shape = buffer.shape
        self.copy = pltpu.make_async_copy(source, buffer, sem)
        self.started = False
        self.waiting = True
        self.then = []

    def start(self):
        if not self.started:
            self.copy.start()
            self.started = True

    def wait(self):
        self.start()
        if self.waiting:
            self.copy.wait()
            self.waiting = False
            for other in self.then:
                other.start()

    def __getitem__(self, index):
        self.wait()
        return self.buffer[index]


class Leaving:
    def __init__(self, target, buffer, sem):
        self.buffer = buffer
        self.shape = buffer.shape
        self.copy = pltpu.make_async_copy(buffer, target, sem)
        self.sent = False

    def __getitem__(self, index):
        return self.buffer[index]

    def __setitem__(self, index, value):
        self.buffer[index] = value

    def send(self):
        if not self.sent:
            self.copy.start()
            self.sent = True


def call(
    kernel, name, out_shape, args, smem=0, scratch=(), vmem=60, after=(), raw=(), part=(), first=0,
    stay=(), stay_out=(),
):
    count = len(args)
    outs = len(out_shape)
    loaded = [i for i in range(smem, count) if i not in raw and i not in stay]
    leaving_out = [n for n in range(outs) if n not in stay_out]
    part = dict(part)

    def held(i):
        dims = (part[i][1], *args[i].shape[1:]) if i in part else args[i].shape
        return pltpu.VMEM(dims, args[i].dtype)

    buffers = [held(i) for i in loaded]
    buffers += [pltpu.VMEM(out_shape[n].shape, out_shape[n].dtype) for n in leaving_out]

    def body(*refs):
        given = list(refs[:count])
        refs = refs[count + len(after) :]
        results, refs = list(refs[:outs]), refs[outs:]
        own, refs = refs[: len(buffers)], refs[len(buffers) :]
        in_sems, out_sems, refs = refs[0], refs[1], refs[2:]
        for n, i in enumerate(loaded):
            source = given[i].at[pl.ds(*part[i])] if i in part else given[i]
            given[i] = Arriving(source, own[n], in_sems.at[n])
        late = [given[i] for i in loaded if first and i >= first]
        for i in loaded:
            if given[i] not in late:
                given[i].start()
                given[i].then = late
        for m, n in enumerate(leaving_out):
            results[n] = Leaving(results[n], own[len(loaded) + m], out_sems.at[m])
        kernel(*given, *results, *refs)
        for i in loaded:
            given[i].wait()
        for n in leaving_out:
            results[n].send()
        for n in leaving_out:
            results[n].copy.wait()

    in_specs = [SM] * smem + [VM if i in stay else ANY for i in range(smem, count)]
    return pl.pallas_call(
        body,
        out_shape=tuple(out_shape),
        in_specs=in_specs + [ANY] * len(after),
        out_specs=tuple(VM if n in stay_out else ANY for n in range(outs)),
        scratch_shapes=[
            *buffers, pltpu.SemaphoreType.DMA((max(len(loaded), 1),)),
            pltpu.SemaphoreType.DMA((max(len(leaving_out), 1),)), *scratch,
        ],
        compiler_params=pltpu.CompilerParams(vmem_limit_bytes=vmem * MIB),
        cost_estimate=pl.CostEstimate(flops=1000, transcendentals=0, bytes_accessed=1000),
        name=name,
    )(*args, *after)


def send(ref):
    if isinstance(ref, Leaving):
        ref.send()


def joint_kernel(wq_ref, wk_ref, wv_ref, wo_ref, bq_ref, bv_ref, bu_ref, out_ref, tail_s):
    cols = wq_ref.shape[0]
    for i, ref in enumerate((wq_ref, wk_ref, wv_ref, wo_ref)):
        out_ref[i * cols : (i + 1) * cols] = ref[...]
    tail_s[...] = jnp.zeros_like(tail_s)
    tail_s[0:1, 0:cols] = row(bq_ref)
    tail_s[1:2, 0:cols] = row(bv_ref)
    tail_s[2:3, :] = row(bu_ref)
    out_ref[4 * cols : 4 * cols + 16] = tail_s[...].astype(BF)


def pack_joint(w_query, w_key, w_value, w_out, b_query, b_value, b_up):
    width, cols = w_query.shape
    return call(
        joint_kernel, "pack_joint", [shape((4 * cols + 16, width), BF)],
        (w_query.T, w_key.T, w_value.T, w_out, b_query, b_value, b_up),
        scratch=[pltpu.VMEM((16, width), F32)],
    )[0]


def neighbour(lens_ref, me_ref, rows):
    me = me_ref[0]
    here = me * rows
    first = jnp.int32(0)
    start = jnp.int32(0)
    length = jnp.int32(0)
    for j in range(lens_ref.shape[0]):
        n = lens_ref[j]
        inside = (first <= here) & (here < first + n)
        start = jnp.where(inside, first, start)
        length = jnp.where(inside, n, length)
        first = first + n
    other = jnp.where(start == here, me + 1, me - 1)
    return length > rows, other == (me ^ 1)


def pick_other(use_core, core_ref, mid_ref, buffer, sem):
    from_core = pltpu.make_async_copy(core_ref, buffer, sem)
    from_mid = pltpu.make_async_copy(mid_ref, buffer, sem)

    @pl.when(use_core)
    def _():
        from_core.start()

    @pl.when(jnp.logical_not(use_core))
    def _():
        from_mid.start()

    return from_core


def attend_block(flag, own, other, a_ref, outs, scratch):
    ctx_ref, ct_ref, lse_ref, q_ref, k_ref, v_ref = outs
    qt_s, vt_s = scratch
    rows, cols = q_ref.shape
    tail = a_ref[4 * cols : 4 * cols + 16].astype(F32)
    wk = a_ref[cols : 2 * cols]
    wv = a_ref[2 * cols : 3 * cols]
    q = (contract_cols(own, a_ref[0:cols]) + tail[0:1, 0:cols]).astype(BF)
    q = q * jnp.asarray(score_scale, BF)
    q_ref[...] = q
    send(q_ref)
    qt_s[...] = q.T
    near = slice(0, rows)
    far = slice(rows, 2 * rows)
    k_ref[near] = contract_cols(own, wk).astype(BF)
    v_own = (contract_cols(own, wv) + tail[1:2, 0:cols]).astype(BF)
    v_ref[near] = v_own
    vt_s[:, near] = v_own.T
    other = other()
    k_ref[far] = contract_cols(other, wk).astype(BF)
    send(k_ref)
    v_other = (contract_cols(other, wv) + tail[1:2, 0:cols]).astype(BF)
    v_ref[far] = v_other
    send(v_ref)
    vt_s[:, far] = v_other.T
    for h in range(cols // HD):
        hs = slice(h * HD, (h + 1) * HD)
        q_h = qt_s[hs]
        s_own = dot(k_ref[near, hs], q_h)
        s_other = dot(k_ref[far, hs], q_h)
        top_own = jnp.max(s_own, axis=0, keepdims=True)
        top_other = jnp.max(s_other, axis=0, keepdims=True)
        top = jnp.where(flag, jnp.maximum(top_own, top_other), top_own)
        p_own = jnp.exp(s_own - top)
        p_other = jnp.exp(s_other - jnp.where(flag, top, masked_shift))
        total = jnp.sum(p_own, axis=0, keepdims=True) + jnp.sum(p_other, axis=0, keepdims=True)
        c = dot(vt_s[hs, near], p_own.astype(BF)) + dot(vt_s[hs, far], p_other.astype(BF))
        ct_ref[hs] = c * (1.0 / total)
        lse_ref[h : h + 1] = top + jnp.log(total)
    send(ct_ref)
    ctx_ref[...] = ct_ref[...].T.astype(BF)
    send(ctx_ref)


def block_outs(rows, cols):
    return [
        shape((rows, cols), BF), shape((cols, rows), F32), shape((cols // HD, rows), F32),
        shape((rows, cols), BF), shape((2 * rows, cols), BF), shape((2 * rows, cols), BF),
    ]


def attend_scratch(rows, width, cols):
    return [
        pltpu.VMEM((rows, width), BF), pltpu.SemaphoreType.DMA,
        pltpu.VMEM((cols, rows), BF), pltpu.VMEM((cols, 2 * rows), BF),
    ]


class Once:
    def __init__(self, copy, buffer):
        self.copy = copy
        self.buffer = buffer

    def __call__(self):
        if self.copy is not None:
            self.copy.wait()
            self.copy = None
        return self.buffer[...]


def attend_pair_kernel(lens_ref, me_ref, core_ref, mid_ref, own_ref, a0_ref, a1_ref, *refs):
    oth_s, oth_sem, qt_s, vt_s = refs[12:]
    flag, use_core = neighbour(lens_ref, me_ref, own_ref.shape[0])
    other = Once(pick_other(use_core, core_ref, mid_ref, oth_s, oth_sem), oth_s)
    own = own_ref[...]
    attend_block(flag, own, other, a0_ref, refs[0:6], (qt_s, vt_s))
    attend_block(flag, own, other, a1_ref, refs[6:12], (qt_s, vt_s))


def attend_pair(name, lens, me, own, tok_core, tok_mid, blocks, after=()):
    rows, width = own.shape
    cols = (blocks[0].shape[0] - 16) // 4
    outs = call(
        attend_pair_kernel, name, block_outs(rows, cols) * 2,
        (lens, me, tok_core, tok_mid, own, *blocks), smem=2, raw=(2, 3), after=after, first=6,
        scratch=attend_scratch(rows, width, cols),
    )
    return outs[:6], outs[6:]


def norm_near_kernel(
    own_ref, c0_ref, w0_ref, c1_ref, w1_ref, c2_ref, w2_ref, c3_ref, w3_ref, bo_ref, gain_ref, shift_ref,
    u0_ref, bias0_ref, d0_ref, u1_ref, bias1_ref, d1_ref,
    unit_ref, inv_ref, low_ref, act0_ref, sl0_ref, act1_ref, sl1_ref, sum_ref,
):
    resid = own_ref[...].astype(F32) + row(bo_ref)
    for c_ref, w_ref in ((c0_ref, w0_ref), (c1_ref, w1_ref), (c2_ref, w2_ref), (c3_ref, w3_ref)):
        resid = resid + dot(c_ref[...], w_ref[...])
    unit, inverse = unit_of(resid)
    unit_ref[...] = unit
    send(unit_ref)
    inv_ref[...] = inverse
    send(inv_ref)
    low_ref[...] = (unit * row(gain_ref) + row(shift_ref)).astype(BF)
    send(low_ref)
    part = up_down(low_ref, bias0_ref, (u0_ref,), d0_ref, act0_ref, sl0_ref)
    sum_ref[...] = part + up_down(low_ref, bias1_ref, (u1_ref,), d1_ref, act1_ref, sl1_ref)


def norm_near(own, ctxs, joints, b_out, gain, shift, ups, downs, after=()):
    rows, width = own.shape
    units = downs[0].shape[0]
    at = joints[0].shape[0] - 16
    piece = shape((rows, units), BF)
    cols = ctxs[0].shape[1]
    terms = [x for pair in zip(ctxs, joints) for x in pair]
    return call(
        norm_near_kernel, "norm_near",
        [
            shape((rows, width), F32), shape((rows, 1), F32), shape((rows, width), BF),
            piece, piece, piece, piece, shape((rows, width), F32),
        ],
        (
            own, *terms, b_out, gain, shift,
            ups[0], joints[0], downs[0], ups[1], joints[1], downs[1],
        ),
        part={2 * i + 2: (3 * cols, cols) for i in range(4)} | {13: (at, 16), 16: (at, 16)},
        after=after, first=12,
    )


def attend_back_block(
    flag, g_ref, a_ref, wo_ref, saved, own_ref, other, grad_ref, sums, b_s, bu_ref, vec_ref, scratch
):
    ct_ref, lse_ref, q_ref, k_ref, v_ref = saved
    tok_in_ref, oth_in_ref, tok_ref, oth_ref = sums
    gt_s, qt_s, kt_s, dqt_s, p_s, ds_s, dk_s, dv_s = scratch
    rows, cols = q_ref.shape
    near = slice(0, rows)
    far = slice(rows, 2 * rows)
    attn_grad = g_ref[...]
    g = contract_cols(attn_grad, wo_ref[...]).astype(BF)
    other = other()
    gt = g.T
    gt_s[...] = gt
    q = q_ref[...]
    qt_s[...] = q.T
    kt_s[...] = k_ref[...].T
    dots = gt.astype(F32) * ct_ref[...]
    for h in range(cols // HD):
        hs = slice(h * HD, (h + 1) * HD)
        row_dot = jnp.sum(dots[hs], axis=0, keepdims=True)
        q_h = qt_s[hs]
        g_h = gt_s[hs]
        lse = lse_ref[h : h + 1]
        for part, shift in ((near, lse), (far, jnp.where(flag, lse, masked_shift))):
            p = jnp.exp(dot(k_ref[part, hs], q_h) - shift)
            p_s[part] = p.astype(BF)
            ds_s[part] = (p * (dot(v_ref[part, hs], g_h) - row_dot)).astype(BF)
        dqt_s[hs] = dot(kt_s[hs], ds_s[...])
        dk_s[:, hs] = dot(ds_s[...], q[:, hs])
        dv_s[:, hs] = dot(p_s[...], g[:, hs])
    dqt = (dqt_s[...] * score_scale).astype(BF)
    dq = dqt.T
    dk = dk_s[...].astype(BF)
    dv = dv_s[...].astype(BF)
    dkt = dk.T
    dvt = dv.T
    b_s[...] = jnp.zeros(b_s.shape, F32)
    b_s[0:1, 0:cols] = jnp.sum(dq.astype(F32), axis=0, keepdims=True)
    b_s[1:2, 0:cols] = jnp.sum(dv.astype(F32), axis=0, keepdims=True)
    b_s[2:3] = bu_ref[...]
    b_s[8:16] = vec_ref[...]
    grad_ref[4 * cols : 4 * cols + 16] = b_s[...].astype(BF)
    grad_ref[4 * cols + 16 :] = jnp.zeros((grad_ref.shape[0] - 4 * cols - 16, b_s.shape[1]), BF)
    grad_ref[3 * cols : 4 * cols] = dot(ct_ref[...].astype(BF), attn_grad).astype(BF)
    tok = own_ref[...]
    oth = other()
    grad_ref[0:cols] = dot(dqt, tok).astype(BF)
    grad_ref[cols : 2 * cols] = (dot(dkt[:, near], tok) + dot(dkt[:, far], oth)).astype(BF)
    grad_ref[2 * cols : 3 * cols] = (dot(dvt[:, near], tok) + dot(dvt[:, far], oth)).astype(BF)
    send(grad_ref)
    wq = a_ref[0:cols]
    wk = a_ref[cols : 2 * cols]
    wv = a_ref[2 * cols : 3 * cols]
    tok_ref[...] = tok_in_ref[...] + dot(dq, wq) + dot(dk[near], wk) + dot(dv[near], wv)
    oth_part = dot(dk[far], wk) + dot(dv[far], wv)
    oth_ref[...] = oth_part if oth_in_ref is None else oth_in_ref[...] + oth_part


def attend_back_kernel(
    start, lens_ref, me_ref, core_ref, mid_ref,
    g_ref, wo_ref, q_ref, k_ref, lse_ref, v_ref, ct_ref, a_ref, own_ref, bu_ref, vec_ref, tok_in_ref,
    *refs,
):
    oth_in_ref, refs = (None, refs) if start else (refs[0], refs[1:])
    grad_ref, tok_ref, oth_ref = refs[:3]
    oth_s, oth_sem, b_s = refs[3:6]
    cols = q_ref.shape[1]
    flag, use_core = neighbour(lens_ref, me_ref, own_ref.shape[0])
    attend_back_block(
        flag, g_ref, a_ref, wo_ref, (ct_ref, lse_ref, q_ref, k_ref, v_ref), own_ref,
        lambda: Once(pick_other(use_core, core_ref, mid_ref, oth_s, oth_sem), oth_s),
        grad_ref, (tok_in_ref, oth_in_ref, tok_ref, oth_ref), b_s, bu_ref, vec_ref, refs[6:],
    )


def attend_back(lens, me, own, tok_core, tok_mid, g, block, bu, vecs, tok_acc, oth_acc, after=()):
    rows, width = own.shape
    a, (_, ct, lse, q, k, v) = block
    cols = q.shape[1]
    sums = [tok_acc] if oth_acc is None else [tok_acc, oth_acc]
    args = (lens, me, tok_core, tok_mid, g, a, q, k, lse, v, ct, a, own, bu, vecs, *sums)
    return call(
        functools.partial(attend_back_kernel, oth_acc is None), "attend_back",
        [shape((4 * cols + 64, width), BF), shape((rows, width), F32), shape((rows, width), F32)],
        args, smem=2, raw=(2, 3), after=after, first=8, vmem=57,
        part={5: (3 * cols, cols), 11: (0, 3 * cols)},
        stay=range(15, len(args)), stay_out=(1, 2),
        scratch=[
            pltpu.VMEM((rows, width), BF), pltpu.SemaphoreType.DMA, pltpu.VMEM((16, width), F32),
            pltpu.VMEM((cols, rows), BF), pltpu.VMEM((cols, rows), BF),
            pltpu.VMEM((cols, 2 * rows), BF), pltpu.VMEM((cols, rows), F32),
            pltpu.VMEM((2 * rows, rows), BF), pltpu.VMEM((2 * rows, rows), BF),
            pltpu.VMEM((2 * rows, cols), F32), pltpu.VMEM((2 * rows, cols), F32),
        ],
    )


def unit_of(residual):
    centre = jnp.mean(residual, axis=1, keepdims=True)
    spread = residual - centre
    inverse = lax.rsqrt(jnp.mean(spread * spread, axis=1, keepdims=True) + norm_eps)
    return spread * inverse, inverse


def norm_back(upstream, unit_rows, inverse, gain):
    unit_grad = upstream * gain
    return inverse * (
        unit_grad
        - jnp.mean(unit_grad, axis=1, keepdims=True)
        - unit_rows * jnp.mean(unit_grad * unit_rows, axis=1, keepdims=True)
    )


def up_down(low_ref, bias_ref, up_refs, down_ref, act_ref, slope_ref):
    units = act_ref.shape[1]
    bias = bias_ref[...].astype(F32)[2:3]
    step = 256
    for c in range(units // step):
        cs = slice(c * step, (c + 1) * step)
        pre = bias[:, cs]
        at = 0
        for up_ref in up_refs:
            depth = up_ref.shape[0]
            pre = pre + dot(low_ref[:, at : at + depth], up_ref[:, cs])
            at += depth
        phi = 0.5 + 0.5 * lax.erf(pre * half_root)
        act_ref[:, cs] = (pre * phi).astype(BF)
        slope_ref[:, cs] = (phi + pre * jnp.exp(-0.5 * pre * pre) * inv_root_two_pi).astype(BF)
    send(act_ref)
    send(slope_ref)
    return dot(act_ref[...], down_ref[...])


def ffn_back_block(g, low_ref, act_ref, slope_ref, down_ref, up_refs, outs, sum_ref, pre_s):
    down_grad_ref, up_grad_ref, bias_ref = outs
    units = down_ref.shape[0]
    down_grad_ref[...] = contract_rows(act_ref[...], g).astype(BF)
    send(down_grad_ref)
    step = 256
    for c in range(units // step):
        cs = slice(c * step, (c + 1) * step)
        pre = (contract_cols(g, down_ref[cs]) * slope_ref[:, cs].astype(F32)).astype(BF)
        pre_s[:, cs] = pre
        bias_ref[:, cs] = jnp.sum(pre.astype(F32), axis=0, keepdims=True)
    pre = pre_s[...]
    up_grad_ref[...] = contract_rows(low_ref[...], pre).astype(BF)
    send(up_grad_ref)
    at = 0
    for up_ref in up_refs:
        cs = slice(at, at + up_ref.shape[0])
        sum_ref[:, cs] += contract_cols(pre, up_ref[...])
        at += up_ref.shape[0]


def ffn_grad_outs(width, units):
    return [shape((units, width), BF), shape((width, units), BF), shape((1, units), F32)]


def ffn_far_kernel(
    low_ref, u2_ref, bias2_ref, d2_ref, u3_ref, bias3_ref, d3_ref,
    sum_in_ref, unit_ref, gain1_ref, shift1_ref, bd_ref, gain2_ref, shift2_ref, out_grad_ref,
    act2_ref, sl2_ref, out_ref, low_grad_ref, vec_ref,
    down_grad_ref, up_grad_ref, bu_ref, sum_ref,
    act3_s, sl3_s, pre_s,
):
    part = up_down(low_ref, bias2_ref, (u2_ref,), d2_ref, act2_ref, sl2_ref)
    part = part + up_down(low_ref, bias3_ref, (u3_ref,), d3_ref, act3_s, sl3_s)
    part = part + sum_in_ref[...]
    resid = unit_ref[...] * row(gain1_ref) + (row(shift1_ref) + row(bd_ref)) + part
    unit, inverse = unit_of(resid)
    gain = row(gain2_ref)
    out_ref[...] = (unit * gain + row(shift2_ref)).astype(BF)
    send(out_ref)
    upstream = out_grad_ref[...].astype(F32)
    vec_ref[...] = jnp.zeros(vec_ref.shape, F32)
    vec_ref[0:1] = jnp.sum(upstream * unit, axis=0, keepdims=True)
    vec_ref[1:2] = jnp.sum(upstream, axis=0, keepdims=True)
    back = norm_back(upstream, unit, inverse, gain)
    sum_ref[...] = back
    g = back.astype(BF)
    low_grad_ref[...] = g
    send(low_grad_ref)
    vec_ref[2:3] = jnp.sum(g.astype(F32), axis=0, keepdims=True)
    ffn_back_block(
        g, low_ref, act3_s, sl3_s, d3_ref, (u3_ref,),
        (down_grad_ref, up_grad_ref, bu_ref), sum_ref, pre_s,
    )


def ffn_far(
    low, joints, ups, downs, near, unit, gain1, shift1, b_down, gain2, shift2, out_grad, after=()
):
    rows, width = low.shape
    units = downs[0].shape[0]
    at = joints[0].shape[0] - 16
    piece = shape((rows, units), BF)
    return call(
        ffn_far_kernel, "ffn_far",
        [
            piece, piece, shape((rows, width), BF), shape((rows, width), BF), shape((8, width), F32),
            *ffn_grad_outs(width, units), shape((rows, width), F32),
        ],
        (
            low, ups[0], joints[0], downs[0], ups[1], joints[1], downs[1], near, unit,
            gain1, shift1, b_down, gain2, shift2, out_grad,
        ),
        part={2: (at, 16), 5: (at, 16)}, first=4, stay_out=(8,), vmem=60, after=after,
        scratch=[pltpu.VMEM((rows, units), BF)] * 3,
    )


def ffn_back_kernel(
    g_ref, act_ref, down_ref, slope_ref, low_ref, up_ref, sum_in_ref,
    down_grad_ref, up_grad_ref, bu_ref, sum_ref, pre_s,
):
    sum_ref[...] = sum_in_ref[...]
    ffn_back_block(
        g_ref[...], low_ref, act_ref, slope_ref, down_ref, (up_ref,),
        (down_grad_ref, up_grad_ref, bu_ref), sum_ref, pre_s,
    )


def ffn_back(g, low, act, slope, up, down, acc, after=()):
    rows, width = low.shape
    units = down.shape[0]
    return call(
        ffn_back_kernel, "ffn_back",
        [*ffn_grad_outs(width, units), shape((rows, width), F32)],
        (g, act, down, slope, low, up, acc), after=after, first=2, stay=(6,), stay_out=(3,), vmem=60,
        scratch=[pltpu.VMEM((rows, units), BF)],
    )


def ffn_last_kernel(
    g_ref, act1_ref, d1_ref, sl1_ref, low_ref, u1_ref, act0_ref, d0_ref, sl0_ref, u0_ref, sum_in_ref,
    unit_ref, inv_ref, gain_ref, vec_in_ref, *refs,
):
    low_ref_out, resid_ref, vec_ref = refs[6:9]
    sum_s, pre_s = refs[9:]
    g = g_ref[...]
    sum_s[...] = sum_in_ref[...]
    ffn_back_block(g, low_ref, act1_ref, sl1_ref, d1_ref, (u1_ref,), refs[0:3], sum_s, pre_s)
    ffn_back_block(g, low_ref, act0_ref, sl0_ref, d0_ref, (u0_ref,), refs[3:6], sum_s, pre_s)
    upstream = sum_s[...]
    unit = unit_ref[...]
    vec_ref[0:4] = vec_in_ref[0:4]
    vec_ref[4:5] = jnp.sum(upstream * unit, axis=0, keepdims=True)
    vec_ref[5:6] = jnp.sum(upstream, axis=0, keepdims=True)
    back = norm_back(upstream, unit, inv_ref[...], row(gain_ref))
    resid_ref[...] = back
    send(resid_ref)
    low = back.astype(BF)
    low_ref_out[...] = low
    send(low_ref_out)
    vec_ref[6:7] = jnp.sum(low.astype(F32), axis=0, keepdims=True)
    vec_ref[7:8] = jnp.zeros(vec_ref.shape, F32)[7:8]


def ffn_last(g, low, acts, slopes, ups, downs, acc, unit, inverse, gain, vecs, after=()):
    rows, width = low.shape
    units = downs[0].shape[0]
    return call(
        ffn_last_kernel, "ffn_last",
        [
            *ffn_grad_outs(width, units), *ffn_grad_outs(width, units),
            shape((rows, width), BF), shape((rows, width), F32), shape((8, width), F32),
        ],
        (
            g, acts[1], downs[1], slopes[1], low, ups[1], acts[0], downs[0], slopes[0], ups[0], acc,
            unit, inverse, gain, vecs,
        ),
        after=after, first=2, stay=(10,), stay_out=(7,), vmem=60,
        scratch=[pltpu.VMEM((rows, width), F32), pltpu.VMEM((rows, units), BF)],
    )


def spread_small_kernel(in_ref, bq_ref, bv_ref, bu_ref, *rest):
    sums = in_ref[...]
    cols = bq_ref.shape[0]
    bq_ref[...] = sums[0:1, 0:cols].reshape(cols)
    bv_ref[...] = sums[1:2, 0:cols].reshape(cols)
    bu_ref[...] = sums[2:3].reshape(-1)
    for at, ref in zip((8, 9, 10, 12, 13, 14), rest):
        ref[...] = sums[at : at + 1].reshape(-1)


def spread_small(sums, cols, units):
    width = sums.shape[1]
    return call(
        spread_small_kernel, "spread_small",
        [shape((cols,), F32), shape((cols,), F32), shape((units,), F32)] + [shape((width,), F32)] * 6,
        (sums,), part={0: (4 * cols, 16)},
    )


def swap(a, axis, distance):
    size = lax.axis_size(axis)
    return lax.ppermute(a, axis, [(i, i ^ distance) for i in range(size)])


def to_core(a):
    return swap(a, "narrow", 1)


def to_chip(a):
    return swap(a, "narrow", 2)


def to_middle(a):
    return lax.ppermute(a, "narrow", [(1, 2), (2, 1)])


def wide_bits():
    size = lax.axis_size("wide")
    bits = []
    while size > 1:
        assert size % 2 == 0
        bits.append(len(bits))
        size //= 2
    return bits


def part_of(a, which, parts):
    rows = a.shape[0] // parts
    return lax.dynamic_slice_in_dim(a, which * rows, rows, 0)


def in_order(side, mine, got):
    return jnp.where(side == 0, jnp.concatenate([mine, got]), jnp.concatenate([got, mine]))


def hold(a, *others):
    return lax.optimization_barrier((a, *others))[0]


def add_low(*terms):
    total = terms[0].astype(F32)
    for term in terms[1:]:
        total = total + term.astype(F32)
    return total.astype(BF)


def side_of(bit):
    return (lax.axis_index("wide") >> bit) & 1


def own_piece(a):
    at = 0
    for bit in wide_bits():
        at = 2 * at + side_of(bit)
    return part_of(a, at, lax.axis_size("wide"))


class WideSum:
    def __init__(self, a):
        self.a = a
        self.step = 0
        self.send()

    def send(self):
        bit = self.step
        if bit < 3:
            side = side_of(bit)
            self.keep = part_of(self.a, side, 2)
            self.sent = part_of(self.a, 1 - side, 2)
        else:
            self.keep = self.sent = self.a
        self.got = swap(self.sent, "wide", 1 << bit)

    def advance(self, *waits):
        got = hold(self.got, *waits) if waits else self.got
        self.a = add_low(self.keep, got)
        self.step += 1
        if self.step < len(wide_bits()):
            self.send()

    def piece(self, *waits):
        while self.step < len(wide_bits()):
            self.advance(*waits)
            waits = ()
        return self.a


class WideGather:
    def __init__(self, a, bits=(2, 1, 0)):
        self.a = self.sent = a
        self.bits = bits
        self.step = 0
        self.send()

    def send(self):
        self.sent = self.a
        self.got = swap(self.a, "wide", 1 << self.bits[self.step])

    def advance(self, *waits):
        got = hold(self.got, *waits) if waits else self.got
        self.a = in_order(side_of(self.bits[self.step]), self.a, got)
        self.step += 1
        if self.step < len(self.bits):
            self.send()

    def whole(self, *waits):
        while self.step < len(self.bits):
            self.advance(*waits)
            waits = ()
        return self.a


def local(
    tokens, item_lengths, w_query, b_query, w_key, w_value, b_value, w_out, b_out,
    gain_attn, shift_attn, w_up, b_up, w_down, b_down, gain_ffn, shift_ffn, out_grad,
):
    rows, width = tokens.shape
    cols = w_query.shape[1]
    units = w_up.shape[1]
    assert lax.axis_size("narrow") == 4
    me = lax.axis_index("narrow").reshape(1)

    tok_mid = to_middle(tokens)
    tok_core = to_core(tokens)
    pieces = to_chip(own_piece(w_down))
    joint = pack_joint(w_query, w_key, w_value, w_out, b_query, b_value, b_up)
    joint_core = to_core(joint)
    joint_chip = to_chip(hold(joint, pieces, tok_mid))
    down_gather = WideGather(pieces, wide_bits()[::-1])
    while down_gather.step < len(down_gather.bits) - 2:
        down_gather.advance(joint_core)
    near0, near1 = attend_pair(
        "attend_near", item_lengths, me, tokens, tok_core, tok_mid, [joint, joint_core],
        (down_gather.sent,),
    )
    down_gather.advance(near1[2])
    gate = down_gather.sent
    joint_chip = hold(joint_chip, gate)
    joint_diag = to_core(joint_chip)
    up_chip = to_chip(hold(w_up, joint_chip))
    up_core = to_core(hold(w_up, joint_chip))
    down_core = to_core(hold(w_down, joint_chip))
    far2, far3 = attend_pair(
        "attend_far", item_lengths, me, tokens, tok_core, tok_mid, [joint_chip, joint_diag], (gate,)
    )
    joints = [joint, joint_core, joint_chip, joint_diag]
    saved = [near0, near1, far2, far3]
    unit_one, inv_one, low, act0, sl0, act1, sl1, near_sum = norm_near(
        tokens, [s[0] for s in saved], joints, b_out, gain_attn, shift_attn,
        [w_up, up_core], [w_down, down_core],
    )
    down_chip = down_gather.whole(inv_one)
    down_diag = to_core(down_chip)
    up_chip = hold(up_chip, down_chip)
    up_diag = to_core(up_chip)
    act2, sl2, layer_out, ffn_grad, vecs, down_d, up_d, bu_d, acc = ffn_far(
        low, joints[2:], [up_chip, up_diag], [down_chip, down_diag],
        near_sum, unit_one, gain_attn, shift_attn, b_down, gain_ffn, shift_ffn, out_grad,
    )

    up_from_core = to_core(up_d)
    down_from_core = to_core(down_d)
    down_x, up_x, bu_x, acc = ffn_back(ffn_grad, low, act2, sl2, up_chip, down_chip, acc)
    up_far = add_low(up_x, hold(up_from_core, bu_x))
    up_sum = to_chip(up_far)
    down_far = add_low(down_x, hold(down_from_core, up_far))
    down_sum = to_chip(down_far)
    down_c, up_c, bu_c, down_o, up_o, bu_o, attn_grad, tok_acc, vecs = ffn_last(
        ffn_grad, low, (act0, act1), (sl0, sl1), (w_up, up_core), (w_down, down_core), acc,
        unit_one, inv_one, gain_attn, vecs, (up_far, down_far),
    )
    up_back = to_core(up_c)
    down_back = to_core(down_c)
    oth_acc = None
    grads = [None] * 4
    bus = (bu_o, bu_c, bu_x, bu_d)

    def back_attend(r, *after):
        nonlocal tok_acc, oth_acc
        grads[r], tok_acc, oth_acc = attend_back(
            item_lengths, me, tokens, tok_core, tok_mid, attn_grad, (joints[r], saved[r]),
            bus[r], vecs, tok_acc, oth_acc, after,
        )
        return grads[r]

    mark = back_attend(3)
    up_sum = hold(up_sum, mark)
    near_up = WideSum(add_low(up_o, hold(up_back, up_sum), up_sum))
    down_near = add_low(down_o, hold(down_back, near_up.sent))
    joint_from_core = to_core(hold(grads[3], down_near))
    mark = back_attend(2, near_up.sent, down_near)
    near_up.advance(mark)
    joint_far = add_low(grads[2], hold(joint_from_core, near_up.sent))
    joint_sum = to_chip(joint_far)
    mark = back_attend(1, near_up.sent, joint_far)
    near_up.advance(mark)
    near_down = WideSum(add_low(down_near, hold(down_sum, near_up.sent)))
    joint_back = to_core(hold(grads[1], near_down.sent))
    mark = back_attend(0, near_up.sent, near_down.sent)
    up_gather = WideGather(near_up.piece(mark))
    near_down.advance(up_gather.sent)
    joint_near = add_low(grads[0], hold(joint_back, near_down.sent))
    up_gather.advance(joint_near)
    near_down.advance(up_gather.sent)
    near_joint = WideSum(add_low(joint_near, hold(joint_sum, near_down.sent)))
    up_gather.advance(near_joint.sent)
    down_gather = WideGather(near_down.piece(up_gather.sent))
    near_joint.advance(down_gather.sent)
    down_gather.advance(near_joint.sent)
    near_joint.advance(down_gather.sent)
    down_gather.advance(near_joint.sent)
    joint_gather = WideGather(near_joint.piece(down_gather.sent))
    w_up_grad = up_gather.whole(joint_gather.sent).astype(F32)
    oth_low = hold(oth_acc.astype(BF), joint_gather.sent)
    oth_core, oth_mid = to_core(oth_low), to_middle(oth_low)
    joint_gather.advance(w_up_grad)
    joint_gather.advance()
    w_down_grad = down_gather.whole(joint_gather.sent).astype(F32)
    token_grad = take_back(item_lengths, me, tok_acc, hold(oth_core, w_down_grad), oth_mid)
    joint_grad = joint_gather.whole(token_grad).astype(F32)
    bq, bv, bu, gain_ffn_g, shift_ffn_g, b_down_g, gain_attn_g, shift_attn_g, b_out_g = spread_small(
        joint_grad, cols, units
    )
    joint_grads = [joint_grad[i * cols : (i + 1) * cols] for i in range(3)]
    w_out_grad = joint_grad[3 * cols : 4 * cols]
    return (
        layer_out,
        token_grad,
        joint_grads[0].T,
        bq,
        joint_grads[1].T,
        joint_grads[2].T,
        bv,
        w_out_grad,
        b_out_g,
        gain_attn_g,
        shift_attn_g,
        w_up_grad,
        bu,
        w_down_grad,
        b_down_g,
        gain_ffn_g,
        shift_ffn_g,
    )


def take_back_kernel(lens_ref, me_ref, tok_ref, core_ref, mid_ref, out_ref, oth_s, oth_sem):
    flag, use_core = neighbour(lens_ref, me_ref, tok_ref.shape[0])
    pick_other(use_core, core_ref, mid_ref, oth_s, oth_sem).wait()
    out_ref[...] = tok_ref[...] + jnp.where(flag, oth_s[...].astype(F32), 0.0)


def take_back(lens, me, tok_acc, core, mid):
    return call(
        take_back_kernel, "take_back", [shape(tok_acc.shape, F32)],
        (lens, me, tok_acc, core, mid), smem=2, raw=(3, 4),
        scratch=[pltpu.VMEM(core.shape, BF), pltpu.SemaphoreType.DMA],
    )[0]


def solution(mesh):
    rows_spec = P(("wide", "narrow"), None)
    col_spec = P(None, "narrow")
    vec_spec = P("narrow")
    row_spec = P("narrow", None)
    full = P()
    return jax.shard_map(
        local,
        mesh=mesh,
        in_specs=(
            rows_spec, P("wide"), col_spec, vec_spec, col_spec, col_spec, vec_spec, row_spec, full,
            full, full, col_spec, vec_spec, row_spec, full, full, full, rows_spec,
        ),
        out_specs=(
            rows_spec, rows_spec, col_spec, vec_spec, col_spec, col_spec, vec_spec, row_spec, full,
            full, full, col_spec, vec_spec, row_spec, full, full, full,
        ),
        check_vma=False,
    )
```

```python
import functools

import jax
import jax.numpy as jnp
from jax import lax
from jax.experimental import pallas as pl
from jax.experimental.pallas import tpu as pltpu
from jax.sharding import PartitionSpec as P

HD = 64
F32 = jnp.float32
BF = jnp.bfloat16
MIB = 1 << 20

norm_eps = 1e-12
masked_shift = 1e30
half_root = 0.7071067811865476
inv_root_two_pi = 0.3989422804014327
score_scale = HD**-0.5

VM = pl.BlockSpec(memory_space=pltpu.VMEM)
SM = pl.BlockSpec(memory_space=pltpu.SMEM)
ANY = pl.BlockSpec(memory_space=pl.ANY)


def dot(left, right):
    return jnp.dot(left, right, preferred_element_type=F32)


def contract_rows(left, right):
    return lax.dot_general(left, right, (((0,), (0,)), ((), ())), preferred_element_type=F32)


def contract_cols(left, right):
    return lax.dot_general(left, right, (((1,), (1,)), ((), ())), preferred_element_type=F32)


def shape(dims, dtype):
    return jax.ShapeDtypeStruct(dims, dtype)


def row(ref):
    return ref[...].astype(F32).reshape(1, -1)


class Arriving:
    def __init__(self, source, buffer, sem):
        self.buffer = buffer
        self.shape = buffer.shape
        self.dtype = buffer.dtype
        self.copy = pltpu.make_async_copy(source, buffer, sem)
        self.started = False
        self.waiting = True
        self.then = []

    def start(self):
        if not self.started:
            self.copy.start()
            self.started = True

    def wait(self):
        self.start()
        if self.waiting:
            self.copy.wait()
            self.waiting = False
            for other in self.then:
                other.start()

    def __getitem__(self, index):
        self.wait()
        return self.buffer[index]


class Leaving:
    def __init__(self, target, buffer, sem):
        self.buffer = buffer
        self.shape = buffer.shape
        self.dtype = buffer.dtype
        self.copy = pltpu.make_async_copy(buffer, target, sem)
        self.sent = False

    def __getitem__(self, index):
        return self.buffer[index]

    def __setitem__(self, index, value):
        self.buffer[index] = value

    def send(self):
        if not self.sent:
            self.copy.start()
            self.sent = True


def call(
    kernel, name, out_shape, args, smem=0, scratch=(), vmem=60, after=(), raw=(), part=(), first=0,
    stay=(), stay_out=(),
):
    count = len(args)
    outs = len(out_shape)
    loaded = [i for i in range(smem, count) if i not in raw and i not in stay]
    leaving_out = [n for n in range(outs) if n not in stay_out]
    part = dict(part)

    def held(i):
        dims = (part[i][1], *args[i].shape[1:]) if i in part else args[i].shape
        return pltpu.VMEM(dims, args[i].dtype)

    buffers = [held(i) for i in loaded]
    buffers += [pltpu.VMEM(out_shape[n].shape, out_shape[n].dtype) for n in leaving_out]

    def body(*refs):
        given = list(refs[:count])
        refs = refs[count + len(after) :]
        results, refs = list(refs[:outs]), refs[outs:]
        own, refs = refs[: len(buffers)], refs[len(buffers) :]
        in_sems, out_sems, refs = refs[0], refs[1], refs[2:]
        for n, i in enumerate(loaded):
            source = given[i].at[pl.ds(*part[i])] if i in part else given[i]
            given[i] = Arriving(source, own[n], in_sems.at[n])
        late = [given[i] for i in loaded if first and i >= first]
        for i in loaded:
            if given[i] not in late:
                given[i].start()
                given[i].then = late
        for m, n in enumerate(leaving_out):
            results[n] = Leaving(results[n], own[len(loaded) + m], out_sems.at[m])
        kernel(*given, *results, *refs)
        for i in loaded:
            given[i].wait()
        for n in leaving_out:
            results[n].send()
        for n in leaving_out:
            results[n].copy.wait()

    in_specs = [SM] * smem + [VM if i in stay else ANY for i in range(smem, count)]
    return pl.pallas_call(
        body,
        out_shape=tuple(out_shape),
        in_specs=in_specs + [ANY] * len(after),
        out_specs=tuple(VM if n in stay_out else ANY for n in range(outs)),
        scratch_shapes=[
            *buffers, pltpu.SemaphoreType.DMA((max(len(loaded), 1),)),
            pltpu.SemaphoreType.DMA((max(len(leaving_out), 1),)), *scratch,
        ],
        compiler_params=pltpu.CompilerParams(vmem_limit_bytes=vmem * MIB),
        cost_estimate=pl.CostEstimate(flops=1000, transcendentals=0, bytes_accessed=1000),
        name=name,
    )(*args, *after)


def send(ref):
    if isinstance(ref, Leaving):
        ref.send()


def arrive(*refs):
    for ref in refs:
        if isinstance(ref, Arriving):
            ref.wait()


def chunks(extent, size, body):
    def step(i, carry):
        body(pl.ds(pl.multiple_of(i * size, size), size))
        return carry

    lax.fori_loop(0, extent // size, step, 0)


def masked(picked, a):
    return jnp.where(picked, a.astype(F32), 0.0).astype(BF)


def joint_kernel(wq_ref, wk_ref, wv_ref, wo_ref, bq_ref, bv_ref, bu_ref, out_ref, tail_s):
    cols = wq_ref.shape[0]
    for i, ref in enumerate((wq_ref, wk_ref, wv_ref, wo_ref)):
        out_ref[i * cols : (i + 1) * cols] = ref[...]
    tail_s[...] = jnp.zeros_like(tail_s)
    tail_s[0:1, 0:cols] = row(bq_ref)
    tail_s[1:2, 0:cols] = row(bv_ref)
    tail_s[2:3, :] = row(bu_ref)
    out_ref[4 * cols : 4 * cols + 16] = tail_s[...].astype(BF)


def pack_joint(w_query, w_key, w_value, w_out, b_query, b_value, b_up):
    width, cols = w_query.shape
    return call(
        joint_kernel, "pack_joint", [shape((4 * cols + 16, width), BF)],
        (w_query.T, w_key.T, w_value.T, w_out, b_query, b_value, b_up),
        scratch=[pltpu.VMEM((16, width), F32)],
    )[0]


def neighbour(lens_ref, me_ref, rows):
    me = me_ref[0]
    here = me * rows
    first = jnp.int32(0)
    start = jnp.int32(0)
    length = jnp.int32(0)
    for j in range(lens_ref.shape[0]):
        n = lens_ref[j]
        inside = (first <= here) & (here < first + n)
        start = jnp.where(inside, first, start)
        length = jnp.where(inside, n, length)
        first = first + n
    other = jnp.where(start == here, me + 1, me - 1)
    return length > rows, other == (me ^ 1)


def pick_other(use_core, core_ref, mid_ref, buffer, sem):
    from_core = pltpu.make_async_copy(core_ref, buffer, sem)
    from_mid = pltpu.make_async_copy(mid_ref, buffer, sem)

    @pl.when(use_core)
    def _():
        from_core.start()

    @pl.when(jnp.logical_not(use_core))
    def _():
        from_mid.start()

    return from_core


def attend_block(flag, own_ref, oth_s, a_ref, outs, scratch):
    ctx_ref, ct_ref, lse_ref, q_ref, k_ref, v_ref = outs
    qt_s, vt_s = scratch
    rows, cols = q_ref.shape
    tail = a_ref[4 * cols : 4 * cols + 16].astype(F32)
    wk = a_ref[cols : 2 * cols]
    wv = a_ref[2 * cols : 3 * cols]
    near = slice(0, rows)
    far = slice(rows, 2 * rows)
    q = (contract_cols(own_ref[...], a_ref[0:cols]) + tail[0:1, 0:cols]).astype(BF)
    q = q * jnp.asarray(score_scale, BF)
    q_ref[...] = q
    qt_s[...] = q.T
    for part, tok_ref in ((near, own_ref), (far, oth_s)):
        k_ref[part] = contract_cols(tok_ref[...], wk).astype(BF)
        v = (contract_cols(tok_ref[...], wv) + tail[1:2, 0:cols]).astype(BF)
        v_ref[part] = v
        vt_s[:, part] = v.T
    head_of_row = lax.broadcasted_iota(jnp.int32, (cols, 1), 0) // HD

    def head(h, carry):
        hs = pl.ds(pl.multiple_of(h * HD, HD), HD)
        q_h = masked(head_of_row == h, qt_s[...])
        s_own = dot(k_ref[near], q_h)
        s_other = dot(k_ref[far], q_h)
        top_own = jnp.max(s_own, axis=0, keepdims=True)
        top_other = jnp.max(s_other, axis=0, keepdims=True)
        top = jnp.where(flag, jnp.maximum(top_own, top_other), top_own)
        p_own = jnp.exp(s_own - top)
        p_other = jnp.exp(s_other - jnp.where(flag, top, masked_shift))
        total = jnp.sum(p_own, axis=0, keepdims=True) + jnp.sum(p_other, axis=0, keepdims=True)
        c = dot(vt_s[hs, near], p_own.astype(BF)) + dot(vt_s[hs, far], p_other.astype(BF))
        ct_ref[hs] = c * (1.0 / total)
        lse_ref[pl.ds(h, 1)] = top + jnp.log(total)
        return carry

    lax.fori_loop(0, cols // HD, head, 0)
    ctx_ref[...] = ct_ref[...].T.astype(BF)


def block_outs(rows, cols):
    return [
        shape((rows, cols), BF), shape((cols, rows), F32), shape((cols // HD, rows), F32),
        shape((rows, cols), BF), shape((2 * rows, cols), BF), shape((2 * rows, cols), BF),
    ]


def attend_scratch(rows, width, cols):
    return [
        pltpu.VMEM((rows, width), BF), pltpu.SemaphoreType.DMA,
        pltpu.VMEM((cols, rows), BF), pltpu.VMEM((cols, 2 * rows), BF),
    ]


class Once:
    def __init__(self, copy, buffer):
        self.copy = copy
        self.buffer = buffer

    def __call__(self):
        if self.copy is not None:
            self.copy.wait()
            self.copy = None
        return self.buffer[...]


def attend_pair_kernel(
    lens_ref, me_ref, core_ref, mid_ref, own_ref, a0_ref, a1_ref, *refs, after
):
    targets = refs[after : after + 12]
    own_s, a_s, *held = refs[after + 12 : after + 20]
    own_sem, a_sem, out_sem, oth_s, oth_sem, qt_s, vt_s = refs[after + 20 :]
    own_copy = pltpu.make_async_copy(own_ref, own_s, own_sem)
    own_copy.start()
    weights = [
        pltpu.make_async_copy(ref, a_s.at[i], a_sem.at[i]) for i, ref in enumerate((a0_ref, a1_ref))
    ]
    weights[0].start()
    flag, use_core = neighbour(lens_ref, me_ref, own_ref.shape[0])
    other = pick_other(use_core, core_ref, mid_ref, oth_s, oth_sem)
    leaving = [
        [
            pltpu.make_async_copy(buffer.at[i], targets[6 * i + n], out_sem.at[i, n])
            for n, buffer in enumerate(held)
        ]
        for i in range(2)
    ]
    own_copy.wait()

    def block(i, carry):
        @pl.when(i == 0)
        def _():
            weights[0].wait()
            other.wait()
            weights[1].start()

        @pl.when(i == 1)
        def _():
            weights[1].wait()

        attend_block(
            flag, own_s, oth_s, a_s.at[i], [buffer.at[i] for buffer in held], (qt_s, vt_s)
        )
        for n in range(2):

            @pl.when(i == n)
            def _():
                for copy in leaving[n]:
                    copy.start()

        return carry

    lax.fori_loop(0, 2, block, 0)
    for copies in leaving:
        for copy in copies:
            copy.wait()


def attend_pair(name, lens, me, own, tok_core, tok_mid, blocks, after=()):
    rows, width = own.shape
    cols = (blocks[0].shape[0] - 16) // 4
    outs = block_outs(rows, cols)
    got = pl.pallas_call(
        functools.partial(attend_pair_kernel, after=len(after)),
        out_shape=tuple(outs * 2),
        in_specs=[SM, SM] + [ANY] * (5 + len(after)),
        out_specs=tuple([ANY] * 12),
        scratch_shapes=[
            pltpu.VMEM(own.shape, BF), pltpu.VMEM((2, *blocks[0].shape), BF),
            *[pltpu.VMEM((2, *o.shape), o.dtype) for o in outs],
            pltpu.SemaphoreType.DMA, pltpu.SemaphoreType.DMA((2,)), pltpu.SemaphoreType.DMA((2, 6)),
            *attend_scratch(rows, width, cols),
        ],
        compiler_params=pltpu.CompilerParams(vmem_limit_bytes=60 * MIB),
        cost_estimate=pl.CostEstimate(flops=1000, transcendentals=0, bytes_accessed=1000),
        name=name,
    )(lens, me, tok_core, tok_mid, own, *blocks, *after)
    return got[:6], got[6:]


def norm_near_kernel(
    own_ref, c0_ref, w0_ref, c1_ref, w1_ref, c2_ref, w2_ref, c3_ref, w3_ref, bo_ref, gain_ref, shift_ref,
    u0_ref, bias0_ref, d0_ref, u1_ref, bias1_ref, d1_ref,
    unit_ref, inv_ref, low_ref, act0_ref, sl0_ref, act1_ref, sl1_ref, sum_ref,
):
    pairs = ((c0_ref, w0_ref), (c1_ref, w1_ref), (c2_ref, w2_ref), (c3_ref, w3_ref))
    vectors = row(bo_ref), row(gain_ref), row(shift_ref)
    for pair in pairs:
        arrive(*pair)
    arrive(own_ref)

    def rows_of(rs):
        resid = own_ref[rs].astype(F32) + vectors[0]
        for c_ref, w_ref in pairs:
            resid = resid + dot(c_ref[rs], w_ref[...])
        unit, inverse = unit_of(resid)
        unit_ref[rs] = unit
        inv_ref[rs] = inverse
        low_ref[rs] = (unit * vectors[1] + vectors[2]).astype(BF)

    chunks(own_ref.shape[0], 256, rows_of)
    send(unit_ref)
    send(inv_ref)
    send(low_ref)
    up_down(low_ref, bias0_ref, (u0_ref,), d0_ref, act0_ref, sl0_ref, sum_ref, True)
    up_down(low_ref, bias1_ref, (u1_ref,), d1_ref, act1_ref, sl1_ref, sum_ref, False)


def norm_near(own, ctxs, joints, b_out, gain, shift, ups, downs, after=()):
    rows, width = own.shape
    units = downs[0].shape[0]
    at = joints[0].shape[0] - 16
    piece = shape((rows, units), BF)
    cols = ctxs[0].shape[1]
    terms = [x for pair in zip(ctxs, joints) for x in pair]
    return call(
        norm_near_kernel, "norm_near",
        [
            shape((rows, width), F32), shape((rows, 1), F32), shape((rows, width), BF),
            piece, piece, piece, piece, shape((rows, width), F32),
        ],
        (
            own, *terms, b_out, gain, shift,
            ups[0], joints[0], downs[0], ups[1], joints[1], downs[1],
        ),
        part={2 * i + 2: (3 * cols, cols) for i in range(4)} | {13: (at, 16), 16: (at, 16)},
        after=after, first=12,
    )


def attend_back_block(
    flag, g_ref, wo_ref, saved, own_ref, other, grad_ref, sums, b_s, bu_ref, vec_ref, scratch
):
    ct_ref, lse_ref, q_ref, k_ref, v_ref = saved
    d_s = sums
    gt_s, qt_s, kt_s, dqt_s, p_s, ds_s, dk_s, dv_s, dot_s, g_s, t_s = scratch
    rows, cols = q_ref.shape
    near = slice(0, rows)
    far = slice(rows, 2 * rows)
    arrive(g_ref, wo_ref)
    other = other()
    arrive(q_ref)

    def query_rows(rs):
        g = contract_cols(g_ref[rs], wo_ref[...]).astype(BF)
        g_s[rs] = g
        gt_s[:, rs] = g.T
        qt_s[:, rs] = q_ref[rs].T

    chunks(rows, 256, query_rows)
    arrive(k_ref)

    def key_rows(rs):
        kt_s[:, rs] = k_ref[rs].T

    chunks(2 * rows, 256, key_rows)
    dot_s[...] = gt_s[...].astype(F32) * ct_ref[...]
    dk_s[...] = jnp.zeros(dk_s.shape, F32)
    dv_s[...] = jnp.zeros(dv_s.shape, F32)
    head_of_row = lax.broadcasted_iota(jnp.int32, (cols, 1), 0) // HD
    head_of_lane = lax.broadcasted_iota(jnp.int32, (1, cols), 1) // HD
    arrive(q_ref, k_ref, v_ref, lse_ref)

    def head(h, carry):
        hs = pl.ds(pl.multiple_of(h * HD, HD), HD)
        row_dot = jnp.sum(dot_s[hs], axis=0, keepdims=True)
        q_h = masked(head_of_row == h, qt_s[...])
        g_h = masked(head_of_row == h, gt_s[...])
        lse = lse_ref[pl.ds(h, 1)]
        for part, shift in ((near, lse), (far, jnp.where(flag, lse, masked_shift))):
            p = jnp.exp(dot(k_ref[part], q_h) - shift)
            p_s[part] = p.astype(BF)
            ds_s[part] = (p * (dot(v_ref[part], g_h) - row_dot)).astype(BF)
        dqt_s[hs] = dot(kt_s[hs], ds_s[...])
        dk_s[...] += dot(ds_s[...], masked(head_of_lane == h, q_ref[...]))
        dv_s[...] += dot(p_s[...], masked(head_of_lane == h, g_s[...]))
        return carry

    lax.fori_loop(0, cols // HD, head, 0)
    dqt = (dqt_s[...] * score_scale).astype(BF)
    dq = dqt.T
    d_s[near, 0:cols] = dq
    d_s[far, 0:cols] = jnp.zeros((rows, cols), BF)
    t_s[0:cols, near] = dqt
    b_s[...] = jnp.zeros(b_s.shape, F32)

    def grad_rows(rs):
        dk = dk_s[rs].astype(BF)
        dv = dv_s[rs].astype(BF)
        d_s[rs, cols : 2 * cols] = dk
        d_s[rs, 2 * cols : 3 * cols] = dv
        t_s[cols : 2 * cols, rs] = dk.T
        t_s[2 * cols : 3 * cols, rs] = dv.T
        b_s[1:2, 0:cols] += jnp.sum(dv.astype(F32), axis=0, keepdims=True)

    chunks(2 * rows, 256, grad_rows)
    t_s[3 * cols : 4 * cols, near] = ct_ref[...].astype(BF)
    b_s[0:1, 0:cols] = jnp.sum(dq.astype(F32), axis=0, keepdims=True)
    b_s[2:3] = bu_ref[...]
    b_s[8:16] = vec_ref[...]
    grad_ref[4 * cols : 4 * cols + 16] = b_s[...].astype(BF)
    grad_ref[4 * cols + 16 :] = jnp.zeros((grad_ref.shape[0] - 4 * cols - 16, b_s.shape[1]), BF)
    other()
    send(d_s)
    arrive(own_ref)
    width = own_ref.shape[1]

    def weight_terms(cs):
        tok = own_ref[:, cs]
        grad_ref[0:cols, cs] = dot(t_s[0:cols, near], tok).astype(BF)
        grad_ref[cols : 3 * cols, cs] = (
            dot(t_s[cols : 3 * cols, near], tok) + dot(t_s[cols : 3 * cols, far], other.buffer[:, cs])
        ).astype(BF)
        grad_ref[3 * cols : 4 * cols, cs] = dot(t_s[3 * cols : 4 * cols, near], g_ref[:, cs]).astype(BF)

    chunks(width, 256, weight_terms)
    send(grad_ref)


def attend_back_kernel(
    lens_ref, me_ref, core_ref, mid_ref,
    g_ref, wo_ref, q_ref, k_ref, lse_ref, v_ref, ct_ref, own_ref, bu_ref, vec_ref,
    grad_ref, d_ref, oth_s, oth_sem, b_s, *scratch,
):
    flag, use_core = neighbour(lens_ref, me_ref, own_ref.shape[0])
    attend_back_block(
        flag, g_ref, wo_ref, (ct_ref, lse_ref, q_ref, k_ref, v_ref), own_ref,
        lambda: Once(pick_other(use_core, core_ref, mid_ref, oth_s, oth_sem), oth_s),
        grad_ref, d_ref, b_s, bu_ref, vec_ref, scratch,
    )


def attend_back(lens, me, own, tok_core, tok_mid, g, block, bu, vecs, after=()):
    rows, width = own.shape
    a, (_, ct, lse, q, k, v) = block
    cols = q.shape[1]
    args = (lens, me, tok_core, tok_mid, g, a, q, k, lse, v, ct, own, bu, vecs)
    return call(
        attend_back_kernel, "attend_back",
        [shape((4 * cols + 64, width), BF), shape((2 * rows, 3 * cols), BF)],
        args, smem=2, raw=(2, 3), after=after, first=8, part={5: (3 * cols, cols)},
        scratch=[
            pltpu.VMEM((rows, width), BF), pltpu.SemaphoreType.DMA, pltpu.VMEM((16, width), F32),
            pltpu.VMEM((cols, rows), BF), pltpu.VMEM((cols, rows), BF),
            pltpu.VMEM((cols, 2 * rows), BF), pltpu.VMEM((cols, rows), F32),
            pltpu.VMEM((2 * rows, rows), BF), pltpu.VMEM((2 * rows, rows), BF),
            pltpu.VMEM((2 * rows, cols), F32), pltpu.VMEM((2 * rows, cols), F32),
            pltpu.VMEM((cols, rows), F32), pltpu.VMEM((rows, cols), BF),
            pltpu.VMEM((4 * cols, 2 * rows), BF),
        ],
    )


def other_grad_kernel(*refs):
    ds, weights, out_ref = refs[0:4], refs[4:8], refs[8]
    arrive(*ds, *weights)
    depth = ds[0].shape[1]

    def features_of(cs):
        total = dot(ds[0][...], weights[0][0:depth, cs])
        for d_ref, w_ref in zip(ds[1:], weights[1:]):
            total = total + dot(d_ref[...], w_ref[0:depth, cs])
        out_ref[:, cs] = total.astype(out_ref.dtype)

    chunks(out_ref.shape[1], 256, features_of)


def other_grad(ds, joints, rows, after=()):
    width = joints[0].shape[1]
    return call(
        other_grad_kernel, "other_grad", [shape((rows, width), BF)], (*ds, *joints), after=after,
        part={i: (rows, rows) for i in range(4)} | {i: (0, ds[0].shape[1]) for i in range(4, 8)},
    )[0]


def unit_of(residual):
    centre = jnp.mean(residual, axis=1, keepdims=True)
    spread = residual - centre
    inverse = lax.rsqrt(jnp.mean(spread * spread, axis=1, keepdims=True) + norm_eps)
    return spread * inverse, inverse


def norm_back(upstream, unit_rows, inverse, gain):
    unit_grad = upstream * gain
    return inverse * (
        unit_grad
        - jnp.mean(unit_grad, axis=1, keepdims=True)
        - unit_rows * jnp.mean(unit_grad * unit_rows, axis=1, keepdims=True)
    )


def up_down(low_ref, bias_ref, up_refs, down_ref, act_ref, slope_ref, sum_ref, start):
    up_ref = up_refs[0]
    arrive(low_ref, bias_ref, up_ref)

    def units_of(cs):
        pre = bias_ref[:, cs].astype(F32)[2:3] + dot(low_ref[...], up_ref[:, cs])
        phi = 0.5 + 0.5 * lax.erf(pre * half_root)
        act_ref[:, cs] = (pre * phi).astype(BF)
        slope_ref[:, cs] = (phi + pre * jnp.exp(-0.5 * pre * pre) * inv_root_two_pi).astype(BF)

    chunks(up_ref.shape[1], 256, units_of)
    send(act_ref)
    send(slope_ref)
    arrive(down_ref)

    def features_of(cs):
        part = dot(act_ref[...], down_ref[:, cs])
        sum_ref[:, cs] = part if start else sum_ref[:, cs] + part

    chunks(down_ref.shape[1], 256, features_of)


def ffn_back_block(
    g_ref, low_ref, act_ref, slope_ref, down_ref, up_refs, outs, sum_in_ref, sum_ref, pre_s
):
    down_grad_ref, up_grad_ref, bias_ref = outs
    up_ref = up_refs[0]
    arrive(g_ref, act_ref, slope_ref, down_ref)

    def units_of(cs):
        g = g_ref[...]
        down_grad_ref[cs] = contract_rows(act_ref[:, cs], g).astype(BF)
        pre = (contract_cols(g, down_ref[cs]) * slope_ref[:, cs].astype(F32)).astype(BF)
        pre_s[:, cs] = pre
        bias_ref[:, cs] = jnp.sum(pre.astype(F32), axis=0, keepdims=True)

    chunks(down_ref.shape[0], 256, units_of)
    send(down_grad_ref)
    arrive(low_ref, up_ref, sum_in_ref)

    def features_of(cs):
        pre = pre_s[...]
        up_grad_ref[cs] = contract_rows(low_ref[:, cs], pre).astype(BF)
        sum_ref[:, cs] = sum_in_ref[:, cs] + contract_cols(pre, up_ref[cs])

    chunks(up_ref.shape[0], 256, features_of)
    send(up_grad_ref)


def ffn_grad_outs(width, units):
    return [shape((units, width), BF), shape((width, units), BF), shape((1, units), F32)]


def ffn_far_kernel(
    low_ref, u2_ref, bias2_ref, d2_ref, u3_ref, bias3_ref, d3_ref,
    sum_in_ref, unit_ref, gain1_ref, shift1_ref, bd_ref, gain2_ref, shift2_ref, out_grad_ref,
    act2_ref, sl2_ref, out_ref, low_grad_ref, vec_ref,
    down_grad_ref, up_grad_ref, bu_ref, sum_ref,
    act3_s, sl3_s, pre_s, part_s,
):
    up_down(low_ref, bias2_ref, (u2_ref,), d2_ref, act2_ref, sl2_ref, part_s, True)
    up_down(low_ref, bias3_ref, (u3_ref,), d3_ref, act3_s, sl3_s, part_s, False)
    gain1, gain2, shift2 = row(gain1_ref), row(gain2_ref), row(shift2_ref)
    shift1 = row(shift1_ref) + row(bd_ref)
    arrive(unit_ref, sum_in_ref, out_grad_ref)
    vec_ref[...] = jnp.zeros(vec_ref.shape, F32)

    def rows_of(rs):
        resid = unit_ref[rs] * gain1 + shift1 + sum_in_ref[rs] + part_s[rs]
        unit, inverse = unit_of(resid)
        out_ref[rs] = (unit * gain2 + shift2).astype(BF)
        upstream = out_grad_ref[rs].astype(F32)
        vec_ref[0:1] += jnp.sum(upstream * unit, axis=0, keepdims=True)
        vec_ref[1:2] += jnp.sum(upstream, axis=0, keepdims=True)
        back = norm_back(upstream, unit, inverse, gain2)
        sum_ref[rs] = back
        g = back.astype(BF)
        low_grad_ref[rs] = g
        vec_ref[2:3] += jnp.sum(g.astype(F32), axis=0, keepdims=True)

    chunks(unit_ref.shape[0], 256, rows_of)
    send(out_ref)
    send(low_grad_ref)
    ffn_back_block(
        low_grad_ref, low_ref, act3_s, sl3_s, d3_ref, (u3_ref,),
        (down_grad_ref, up_grad_ref, bu_ref), sum_ref, sum_ref, pre_s,
    )


def ffn_far(
    low, joints, ups, downs, near, unit, gain1, shift1, b_down, gain2, shift2, out_grad, after=()
):
    rows, width = low.shape
    units = downs[0].shape[0]
    at = joints[0].shape[0] - 16
    piece = shape((rows, units), BF)
    return call(
        ffn_far_kernel, "ffn_far",
        [
            piece, piece, shape((rows, width), BF), shape((rows, width), BF), shape((8, width), F32),
            *ffn_grad_outs(width, units), shape((rows, width), F32),
        ],
        (
            low, ups[0], joints[0], downs[0], ups[1], joints[1], downs[1], near, unit,
            gain1, shift1, b_down, gain2, shift2, out_grad,
        ),
        part={2: (at, 16), 5: (at, 16)}, first=4, after=after,
        scratch=[pltpu.VMEM((rows, units), BF)] * 3 + [pltpu.VMEM((rows, width), F32)],
    )


def ffn_back_kernel(
    g_ref, act_ref, down_ref, slope_ref, low_ref, up_ref, sum_in_ref,
    down_grad_ref, up_grad_ref, bu_ref, sum_ref, pre_s,
):
    ffn_back_block(
        g_ref, low_ref, act_ref, slope_ref, down_ref, (up_ref,),
        (down_grad_ref, up_grad_ref, bu_ref), sum_in_ref, sum_ref, pre_s,
    )


def ffn_back(g, low, act, slope, up, down, acc, after=()):
    rows, width = low.shape
    units = down.shape[0]
    return call(
        ffn_back_kernel, "ffn_back",
        [*ffn_grad_outs(width, units), shape((rows, width), F32)],
        (g, act, down, slope, low, up, acc), after=after, first=2,
        scratch=[pltpu.VMEM((rows, units), BF)],
    )


def ffn_last_kernel(
    g_ref, act1_ref, d1_ref, sl1_ref, low_ref, u1_ref, act0_ref, d0_ref, sl0_ref, u0_ref, sum_in_ref,
    unit_ref, inv_ref, gain_ref, vec_in_ref, *refs,
):
    low_ref_out, resid_ref, vec_ref = refs[6:9]
    sum_s, pre_s = refs[9:]
    ffn_back_block(
        g_ref, low_ref, act1_ref, sl1_ref, d1_ref, (u1_ref,), refs[0:3], sum_in_ref, sum_s, pre_s
    )
    ffn_back_block(
        g_ref, low_ref, act0_ref, sl0_ref, d0_ref, (u0_ref,), refs[3:6], sum_s, sum_s, pre_s
    )
    gain = row(gain_ref)
    arrive(unit_ref, inv_ref)
    vec_ref[...] = vec_in_ref[...]

    def rows_of(rs):
        upstream = sum_s[rs]
        unit = unit_ref[rs]
        vec_ref[4:5] += jnp.sum(upstream * unit, axis=0, keepdims=True)
        vec_ref[5:6] += jnp.sum(upstream, axis=0, keepdims=True)
        back = norm_back(upstream, unit, inv_ref[rs], gain)
        resid_ref[rs] = back
        low = back.astype(BF)
        low_ref_out[rs] = low
        vec_ref[6:7] += jnp.sum(low.astype(F32), axis=0, keepdims=True)

    chunks(unit_ref.shape[0], 256, rows_of)
    send(resid_ref)
    send(low_ref_out)


def ffn_last(g, low, acts, slopes, ups, downs, acc, unit, inverse, gain, vecs, after=()):
    rows, width = low.shape
    units = downs[0].shape[0]
    return call(
        ffn_last_kernel, "ffn_last",
        [
            *ffn_grad_outs(width, units), *ffn_grad_outs(width, units),
            shape((rows, width), BF), shape((rows, width), F32), shape((8, width), F32),
        ],
        (
            g, acts[1], downs[1], slopes[1], low, ups[1], acts[0], downs[0], slopes[0], ups[0], acc,
            unit, inverse, gain, vecs,
        ),
        after=after, first=2,
        scratch=[pltpu.VMEM((rows, width), F32), pltpu.VMEM((rows, units), BF)],
    )


def spread_small_kernel(in_ref, bq_ref, bv_ref, bu_ref, *rest):
    sums = in_ref[...]
    cols = bq_ref.shape[0]
    bq_ref[...] = sums[0:1, 0:cols].reshape(cols)
    bv_ref[...] = sums[1:2, 0:cols].reshape(cols)
    bu_ref[...] = sums[2:3].reshape(-1)
    for at, ref in zip((8, 9, 10, 12, 13, 14), rest):
        ref[...] = sums[at : at + 1].reshape(-1)


def spread_small(sums, cols, units):
    width = sums.shape[1]
    return call(
        spread_small_kernel, "spread_small",
        [shape((cols,), F32), shape((cols,), F32), shape((units,), F32)] + [shape((width,), F32)] * 6,
        (sums,), part={0: (2 * cols, 16)},
    )


def swap(a, axis, distance):
    size = lax.axis_size(axis)
    return lax.ppermute(a, axis, [(i, i ^ distance) for i in range(size)])


def to_core(a):
    return swap(a, "narrow", 1)


def to_chip(a):
    return swap(a, "narrow", 2)


def to_middle(a):
    return lax.ppermute(a, "narrow", [(1, 2), (2, 1)])


def wide_bits():
    size = lax.axis_size("wide")
    bits = []
    while size > 1:
        assert size % 2 == 0
        bits.append(len(bits))
        size //= 2
    return bits


def part_of(a, which, parts):
    rows = a.shape[0] // parts
    return lax.dynamic_slice_in_dim(a, which * rows, rows, 0)


def in_order(side, mine, got):
    return jnp.where(side == 0, jnp.concatenate([mine, got]), jnp.concatenate([got, mine]))


def hold(a, *others):
    return lax.optimization_barrier((a, *others))[0]


def add_low(*terms):
    total = terms[0].astype(F32)
    for term in terms[1:]:
        total = total + term.astype(F32)
    return total.astype(BF)


def side_of(bit):
    return (lax.axis_index("wide") >> bit) & 1


def own_piece(a):
    at = 0
    for bit in wide_bits():
        at = 2 * at + side_of(bit)
    return part_of(a, at, lax.axis_size("wide"))


class WideSum:
    def __init__(self, a):
        self.a = a
        self.step = 0
        self.send()

    def send(self):
        bit = self.step
        if bit < 3:
            side = side_of(bit)
            self.keep = part_of(self.a, side, 2)
            self.sent = part_of(self.a, 1 - side, 2)
        else:
            self.keep = self.sent = self.a
        self.got = swap(self.sent, "wide", 1 << bit)

    def advance(self, *waits):
        got = hold(self.got, *waits) if waits else self.got
        self.a = add_low(self.keep, got)
        self.step += 1
        if self.step < len(wide_bits()):
            self.send()

    def piece(self, *waits):
        while self.step < len(wide_bits()):
            self.advance(*waits)
            waits = ()
        return self.a


class WideGather:
    def __init__(self, a, bits=(2, 1, 0)):
        self.a = self.sent = a
        self.bits = bits
        self.step = 0
        self.send()

    def send(self):
        self.sent = self.a
        self.got = swap(self.a, "wide", 1 << self.bits[self.step])

    def advance(self, *waits):
        got = hold(self.got, *waits) if waits else self.got
        self.a = in_order(side_of(self.bits[self.step]), self.a, got)
        self.step += 1
        if self.step < len(self.bits):
            self.send()

    def whole(self, *waits):
        while self.step < len(self.bits):
            self.advance(*waits)
            waits = ()
        return self.a


def local(
    tokens, item_lengths, w_query, b_query, w_key, w_value, b_value, w_out, b_out,
    gain_attn, shift_attn, w_up, b_up, w_down, b_down, gain_ffn, shift_ffn, out_grad,
):
    rows, width = tokens.shape
    cols = w_query.shape[1]
    units = w_up.shape[1]
    assert lax.axis_size("narrow") == 4
    me = lax.axis_index("narrow").reshape(1)

    tok_mid = to_middle(tokens)
    tok_core = to_core(tokens)
    pieces = to_chip(own_piece(w_down))
    joint = pack_joint(w_query, w_key, w_value, w_out, b_query, b_value, b_up)
    joint_core = to_core(joint)
    joint_chip = to_chip(hold(joint, pieces, tok_mid))
    down_gather = WideGather(pieces, wide_bits()[::-1])
    while down_gather.step < len(down_gather.bits) - 2:
        down_gather.advance(joint_core)
    near0, near1 = attend_pair(
        "attend_near", item_lengths, me, tokens, tok_core, tok_mid, [joint, joint_core],
        (down_gather.sent,),
    )
    down_gather.advance(near1[2])
    gate = down_gather.sent
    joint_chip = hold(joint_chip, gate)
    joint_diag = to_core(joint_chip)
    up_chip = to_chip(hold(w_up, joint_chip))
    up_core = to_core(hold(w_up, joint_chip))
    down_core = to_core(hold(w_down, joint_chip))
    far2, far3 = attend_pair(
        "attend_far", item_lengths, me, tokens, tok_core, tok_mid, [joint_chip, joint_diag], (gate,)
    )
    joints = [joint, joint_core, joint_chip, joint_diag]
    saved = [near0, near1, far2, far3]
    unit_one, inv_one, low, act0, sl0, act1, sl1, near_sum = norm_near(
        tokens, [s[0] for s in saved], joints, b_out, gain_attn, shift_attn,
        [w_up, up_core], [w_down, down_core],
    )
    down_chip = down_gather.whole(inv_one)
    down_diag = to_core(down_chip)
    up_chip = hold(up_chip, down_chip)
    up_diag = to_core(up_chip)
    act2, sl2, layer_out, ffn_grad, vecs, down_d, up_d, bu_d, acc = ffn_far(
        low, joints[2:], [up_chip, up_diag], [down_chip, down_diag],
        near_sum, unit_one, gain_attn, shift_attn, b_down, gain_ffn, shift_ffn, out_grad,
    )

    up_from_core = to_core(up_d)
    down_from_core = to_core(down_d)
    down_x, up_x, bu_x, acc = ffn_back(ffn_grad, low, act2, sl2, up_chip, down_chip, acc)
    up_far = add_low(up_x, hold(up_from_core, bu_x))
    up_sum = to_chip(up_far)
    down_far = add_low(down_x, hold(down_from_core, up_far))
    down_sum = to_chip(down_far)
    down_c, up_c, bu_c, down_o, up_o, bu_o, attn_grad, resid_one, vecs = ffn_last(
        ffn_grad, low, (act0, act1), (sl0, sl1), (w_up, up_core), (w_down, down_core), acc,
        unit_one, inv_one, gain_attn, vecs, (up_far, down_far),
    )
    up_back = to_core(up_c)
    down_back = to_core(down_c)
    grads, parts = [None] * 4, [None] * 4
    bus = (bu_o, bu_c, bu_x, bu_d)

    def back_attend(r, *after):
        grads[r], parts[r] = attend_back(
            item_lengths, me, tokens, tok_core, tok_mid, attn_grad, (joints[r], saved[r]),
            bus[r], vecs, after,
        )
        return grads[r]

    mark = back_attend(3)
    up_sum = hold(up_sum, mark)
    near_up = WideSum(add_low(up_o, hold(up_back, up_sum), up_sum))
    down_near = add_low(down_o, hold(down_back, near_up.sent))
    joint_from_core = to_core(hold(grads[3], down_near))
    mark = back_attend(2, near_up.sent, down_near)
    down_sum = hold(down_sum, mark)
    near_down = WideSum(add_low(down_near, down_sum))
    joint_far = add_low(grads[2], hold(joint_from_core, near_down.a))
    joint_sum = to_chip(joint_far)
    near_up.advance(joint_far)
    mark = back_attend(1, joint_far, near_up.sent, near_down.sent)
    near_up.advance(mark)
    near_down.advance(near_up.sent)
    joint_back = to_core(hold(grads[1], near_down.sent))
    mark = back_attend(0, near_up.sent, near_down.sent)
    joint_sum = hold(joint_sum, mark)
    joint_back = hold(joint_back, joint_sum)

    def rows_of(a, part):
        return a[: 2 * cols] if part == 0 else a[2 * cols :]

    def joint_part(i, *waits):
        own = rows_of(grads[0], i)
        return WideSum(add_low(own, hold(rows_of(joint_sum, i), *waits), rows_of(joint_back, i)))

    first = joint_part(0)
    second = joint_part(1, first.sent)
    up_gather = WideGather(near_up.piece(second.sent))
    near_down.advance(up_gather.sent)
    oth_low = other_grad(parts, joints, rows, (near_down.sent,))
    oth_core, oth_mid = to_core(oth_low), to_middle(oth_low)
    first.advance(oth_low)
    up_gather.advance(first.sent)
    down_gather = WideGather(near_down.piece(up_gather.sent))
    second.advance(down_gather.sent)
    first.advance(second.sent)
    up_gather.advance(first.sent)
    down_gather.advance(up_gather.sent)
    second.advance(down_gather.sent)
    first = WideGather(first.piece(second.sent))
    down_gather.advance(first.sent)
    second = WideGather(second.piece(down_gather.sent))
    first.advance(second.sent)
    second.advance(first.sent)
    first.advance(second.sent)
    token_grad = take_back(
        item_lengths, me, hold(oth_core, first.sent), hold(oth_mid, first.sent), resid_one,
        parts, joints,
    )
    second.advance(first.sent)
    w_up_grad = up_gather.whole(token_grad).astype(F32)
    w_down_grad = down_gather.whole(w_up_grad).astype(F32)
    qk_grad = first.whole(w_down_grad).astype(F32)
    vo_grad = second.whole(qk_grad).astype(F32)
    bq, bv, bu, gain_ffn_g, shift_ffn_g, b_down_g, gain_attn_g, shift_attn_g, b_out_g = spread_small(
        vo_grad, cols, units
    )
    joint_grads = [qk_grad[:cols], qk_grad[cols:], vo_grad[:cols]]
    w_out_grad = vo_grad[cols : 2 * cols]
    return (
        layer_out,
        token_grad,
        joint_grads[0].T,
        bq,
        joint_grads[1].T,
        joint_grads[2].T,
        bv,
        w_out_grad,
        b_out_g,
        gain_attn_g,
        shift_attn_g,
        w_up_grad,
        bu,
        w_down_grad,
        b_down_g,
        gain_ffn_g,
        shift_ffn_g,
    )


def take_back_kernel(lens_ref, me_ref, core_ref, mid_ref, *refs):
    ds, weights, resid_ref, out_ref, oth_s, oth_sem = refs[0:4], refs[4:8], *refs[8:]
    flag, use_core = neighbour(lens_ref, me_ref, resid_ref.shape[0])
    other = pick_other(use_core, core_ref, mid_ref, oth_s, oth_sem)
    arrive(*ds, *weights, resid_ref)
    other.wait()
    depth = ds[0].shape[1]

    def features_of(cs):
        total = resid_ref[:, cs] + jnp.where(flag, oth_s[:, cs].astype(F32), 0.0)
        for d_ref, w_ref in zip(ds, weights):
            total = total + dot(d_ref[...], w_ref[0:depth, cs])
        out_ref[:, cs] = total

    chunks(out_ref.shape[1], 256, features_of)


def take_back(lens, me, core, mid, resid, ds, joints):
    rows, width = resid.shape
    depth = ds[0].shape[1]
    return call(
        take_back_kernel, "take_back", [shape((rows, width), F32)],
        (lens, me, core, mid, *ds, *joints, resid), smem=2, raw=(2, 3),
        part={i: (0, rows) for i in range(4, 8)} | {i: (0, depth) for i in range(8, 12)},
        scratch=[pltpu.VMEM(core.shape, BF), pltpu.SemaphoreType.DMA],
    )[0]


def solution(mesh):
    rows_spec = P(("wide", "narrow"), None)
    col_spec = P(None, "narrow")
    vec_spec = P("narrow")
    row_spec = P("narrow", None)
    full = P()
    return jax.shard_map(
        local,
        mesh=mesh,
        in_specs=(
            rows_spec, P("wide"), col_spec, vec_spec, col_spec, col_spec, vec_spec, row_spec, full,
            full, full, col_spec, vec_spec, row_spec, full, full, full, rows_spec,
        ),
        out_specs=(
            rows_spec, rows_spec, col_spec, vec_spec, col_spec, col_spec, vec_spec, row_spec, full,
            full, full, col_spec, vec_spec, row_spec, full, full, full,
        ),
        check_vma=False,
    )
```

```python
import functools

import jax
import jax.numpy as jnp
from jax import lax
from jax.experimental import pallas as pl
from jax.experimental.pallas import tpu as pltpu
from jax.sharding import PartitionSpec as P

HD = 64
F32 = jnp.float32
BF = jnp.bfloat16
MIB = 1 << 20

norm_eps = 1e-12
masked_shift = 1e30
half_root = 0.7071067811865476
inv_root_two_pi = 0.3989422804014327
score_scale = HD**-0.5

VM = pl.BlockSpec(memory_space=pltpu.VMEM)
SM = pl.BlockSpec(memory_space=pltpu.SMEM)
ANY = pl.BlockSpec(memory_space=pl.ANY)


def dot(left, right):
    return jnp.dot(left, right, preferred_element_type=F32)


def contract_rows(left, right):
    return lax.dot_general(left, right, (((0,), (0,)), ((), ())), preferred_element_type=F32)


def contract_cols(left, right):
    return lax.dot_general(left, right, (((1,), (1,)), ((), ())), preferred_element_type=F32)


def shape(dims, dtype):
    return jax.ShapeDtypeStruct(dims, dtype)


def row(ref):
    return ref[...].astype(F32).reshape(1, -1)


class Arriving:
    def __init__(self, source, buffer, sem):
        self.buffer = buffer
        self.shape = buffer.shape
        self.dtype = buffer.dtype
        self.copy = pltpu.make_async_copy(source, buffer, sem)
        self.started = False
        self.waiting = True
        self.then = []

    def start(self):
        if not self.started:
            self.copy.start()
            self.started = True

    def wait(self):
        self.start()
        if self.waiting:
            self.copy.wait()
            self.waiting = False
            for other in self.then:
                other.start()

    def __getitem__(self, index):
        self.wait()
        return self.buffer[index]


class Leaving:
    def __init__(self, target, buffer, sem):
        self.buffer = buffer
        self.shape = buffer.shape
        self.dtype = buffer.dtype
        self.copy = pltpu.make_async_copy(buffer, target, sem)
        self.sent = False

    def __getitem__(self, index):
        return self.buffer[index]

    def __setitem__(self, index, value):
        self.buffer[index] = value

    def send(self):
        if not self.sent:
            self.copy.start()
            self.sent = True


def call(
    kernel, name, out_shape, args, smem=0, scratch=(), vmem=60, after=(), raw=(), part=(), first=0,
    stay=(), stay_out=(),
):
    count = len(args)
    outs = len(out_shape)
    loaded = [i for i in range(smem, count) if i not in raw and i not in stay]
    leaving_out = [n for n in range(outs) if n not in stay_out]
    part = dict(part)

    def held(i):
        dims = (part[i][1], *args[i].shape[1:]) if i in part else args[i].shape
        return pltpu.VMEM(dims, args[i].dtype)

    buffers = [held(i) for i in loaded]
    buffers += [pltpu.VMEM(out_shape[n].shape, out_shape[n].dtype) for n in leaving_out]

    def body(*refs):
        given = list(refs[:count])
        refs = refs[count + len(after) :]
        results, refs = list(refs[:outs]), refs[outs:]
        own, refs = refs[: len(buffers)], refs[len(buffers) :]
        in_sems, out_sems, refs = refs[0], refs[1], refs[2:]
        for n, i in enumerate(loaded):
            source = given[i].at[pl.ds(*part[i])] if i in part else given[i]
            given[i] = Arriving(source, own[n], in_sems.at[n])
        late = [given[i] for i in loaded if first and i >= first]
        for i in loaded:
            if given[i] not in late:
                given[i].start()
                given[i].then = late
        for m, n in enumerate(leaving_out):
            results[n] = Leaving(results[n], own[len(loaded) + m], out_sems.at[m])
        kernel(*given, *results, *refs)
        for i in loaded:
            given[i].wait()
        for n in leaving_out:
            results[n].send()
        for n in leaving_out:
            results[n].copy.wait()

    in_specs = [SM] * smem + [VM if i in stay else ANY for i in range(smem, count)]
    return pl.pallas_call(
        body,
        out_shape=tuple(out_shape),
        in_specs=in_specs + [ANY] * len(after),
        out_specs=tuple(VM if n in stay_out else ANY for n in range(outs)),
        scratch_shapes=[
            *buffers, pltpu.SemaphoreType.DMA((max(len(loaded), 1),)),
            pltpu.SemaphoreType.DMA((max(len(leaving_out), 1),)), *scratch,
        ],
        compiler_params=pltpu.CompilerParams(vmem_limit_bytes=vmem * MIB),
        cost_estimate=pl.CostEstimate(flops=1000, transcendentals=0, bytes_accessed=1000),
        name=name,
    )(*args, *after)


def send(ref):
    if isinstance(ref, Leaving):
        ref.send()


def arrive(*refs):
    for ref in refs:
        if isinstance(ref, Arriving):
            ref.wait()


def chunks(extent, size, body):
    def step(i, carry):
        body(pl.ds(pl.multiple_of(i * size, size), size))
        return carry

    lax.fori_loop(0, extent // size, step, 0)


def masked(picked, a):
    return jnp.where(picked, a.astype(F32), 0.0).astype(BF)


def joint_kernel(wq_ref, wk_ref, wv_ref, wo_ref, bq_ref, bv_ref, bu_ref, out_ref, tail_s):
    cols = wq_ref.shape[0]
    for i, ref in enumerate((wq_ref, wk_ref, wv_ref, wo_ref)):
        out_ref[i * cols : (i + 1) * cols] = ref[...]
    tail_s[...] = jnp.zeros_like(tail_s)
    tail_s[0:1, 0:cols] = row(bq_ref)
    tail_s[1:2, 0:cols] = row(bv_ref)
    tail_s[2:3, :] = row(bu_ref)
    out_ref[4 * cols : 4 * cols + 16] = tail_s[...].astype(BF)


def pack_joint(w_query, w_key, w_value, w_out, b_query, b_value, b_up):
    width, cols = w_query.shape
    return call(
        joint_kernel, "pack_joint", [shape((4 * cols + 16, width), BF)],
        (w_query.T, w_key.T, w_value.T, w_out, b_query, b_value, b_up),
        scratch=[pltpu.VMEM((16, width), F32)],
    )[0]


def neighbour(lens_ref, me_ref, rows):
    me = me_ref[0]
    here = me * rows
    first = jnp.int32(0)
    start = jnp.int32(0)
    length = jnp.int32(0)
    for j in range(lens_ref.shape[0]):
        n = lens_ref[j]
        inside = (first <= here) & (here < first + n)
        start = jnp.where(inside, first, start)
        length = jnp.where(inside, n, length)
        first = first + n
    other = jnp.where(start == here, me + 1, me - 1)
    return length > rows, other == (me ^ 1)


def pick_other(use_core, core_ref, mid_ref, buffer, sem):
    from_core = pltpu.make_async_copy(core_ref, buffer, sem)
    from_mid = pltpu.make_async_copy(mid_ref, buffer, sem)

    @pl.when(use_core)
    def _():
        from_core.start()

    @pl.when(jnp.logical_not(use_core))
    def _():
        from_mid.start()

    return from_core


def attend_block(flag, own_ref, oth_s, a_ref, outs, scratch):
    ctx_ref, ct_ref, lse_ref, q_ref, k_ref, v_ref = outs
    qt_s, vt_s = scratch
    rows, cols = q_ref.shape
    tail = a_ref[4 * cols : 4 * cols + 16].astype(F32)
    wk = a_ref[cols : 2 * cols]
    wv = a_ref[2 * cols : 3 * cols]
    near = slice(0, rows)
    far = slice(rows, 2 * rows)
    q = (contract_cols(own_ref[...], a_ref[0:cols]) + tail[0:1, 0:cols]).astype(BF)
    q = q * jnp.asarray(score_scale, BF)
    q_ref[...] = q
    qt_s[...] = q.T
    for part, tok_ref in ((near, own_ref), (far, oth_s)):
        k_ref[part] = contract_cols(tok_ref[...], wk).astype(BF)
        v = (contract_cols(tok_ref[...], wv) + tail[1:2, 0:cols]).astype(BF)
        v_ref[part] = v
        vt_s[:, part] = v.T
    head_of_row = lax.broadcasted_iota(jnp.int32, (cols, 1), 0) // HD

    def head(h, carry):
        hs = pl.ds(pl.multiple_of(h * HD, HD), HD)
        q_h = masked(head_of_row == h, qt_s[...])
        s_own = dot(k_ref[near], q_h)
        s_other = dot(k_ref[far], q_h)
        top_own = jnp.max(s_own, axis=0, keepdims=True)
        top_other = jnp.max(s_other, axis=0, keepdims=True)
        top = jnp.where(flag, jnp.maximum(top_own, top_other), top_own)
        p_own = jnp.exp(s_own - top)
        p_other = jnp.exp(s_other - jnp.where(flag, top, masked_shift))
        total = jnp.sum(p_own, axis=0, keepdims=True) + jnp.sum(p_other, axis=0, keepdims=True)
        c = dot(vt_s[hs, near], p_own.astype(BF)) + dot(vt_s[hs, far], p_other.astype(BF))
        ct_ref[hs] = c * (1.0 / total)
        lse_ref[pl.ds(h, 1)] = top + jnp.log(total)
        return carry

    lax.fori_loop(0, cols // HD, head, 0)
    ctx_ref[...] = ct_ref[...].T.astype(BF)


def block_outs(rows, cols):
    return [
        shape((rows, cols), BF), shape((cols, rows), F32), shape((cols // HD, rows), F32),
        shape((rows, cols), BF), shape((2 * rows, cols), BF), shape((2 * rows, cols), BF),
    ]


def attend_scratch(rows, width, cols):
    return [
        pltpu.VMEM((rows, width), BF), pltpu.SemaphoreType.DMA,
        pltpu.VMEM((cols, rows), BF), pltpu.VMEM((cols, 2 * rows), BF),
    ]


class Once:
    def __init__(self, copy, buffer):
        self.copy = copy
        self.buffer = buffer

    def __call__(self):
        if self.copy is not None:
            self.copy.wait()
            self.copy = None
        return self.buffer[...]


def attend_pair_kernel(
    lens_ref, me_ref, core_ref, mid_ref, own_ref, a0_ref, a1_ref, *refs, after
):
    targets = refs[after : after + 12]
    own_s, a_s, *held = refs[after + 12 : after + 20]
    own_sem, a_sem, out_sem, oth_s, oth_sem, qt_s, vt_s = refs[after + 20 :]
    own_copy = pltpu.make_async_copy(own_ref, own_s, own_sem)
    own_copy.start()
    weights = [
        pltpu.make_async_copy(ref, a_s.at[i], a_sem.at[i]) for i, ref in enumerate((a0_ref, a1_ref))
    ]
    weights[0].start()
    flag, use_core = neighbour(lens_ref, me_ref, own_ref.shape[0])
    other = pick_other(use_core, core_ref, mid_ref, oth_s, oth_sem)
    leaving = [
        [
            pltpu.make_async_copy(buffer.at[i], targets[6 * i + n], out_sem.at[i, n])
            for n, buffer in enumerate(held)
        ]
        for i in range(2)
    ]
    own_copy.wait()

    def block(i, carry):
        @pl.when(i == 0)
        def _():
            weights[0].wait()
            other.wait()
            weights[1].start()

        @pl.when(i == 1)
        def _():
            weights[1].wait()

        attend_block(
            flag, own_s, oth_s, a_s.at[i], [buffer.at[i] for buffer in held], (qt_s, vt_s)
        )
        for n in range(2):

            @pl.when(i == n)
            def _():
                for copy in leaving[n]:
                    copy.start()

        return carry

    lax.fori_loop(0, 2, block, 0)
    for copies in leaving:
        for copy in copies:
            copy.wait()


def attend_pair(name, lens, me, own, tok_core, tok_mid, blocks, after=()):
    rows, width = own.shape
    cols = (blocks[0].shape[0] - 16) // 4
    outs = block_outs(rows, cols)
    got = pl.pallas_call(
        functools.partial(attend_pair_kernel, after=len(after)),
        out_shape=tuple(outs * 2),
        in_specs=[SM, SM] + [ANY] * (5 + len(after)),
        out_specs=tuple([ANY] * 12),
        scratch_shapes=[
            pltpu.VMEM(own.shape, BF), pltpu.VMEM((2, *blocks[0].shape), BF),
            *[pltpu.VMEM((2, *o.shape), o.dtype) for o in outs],
            pltpu.SemaphoreType.DMA, pltpu.SemaphoreType.DMA((2,)), pltpu.SemaphoreType.DMA((2, 6)),
            *attend_scratch(rows, width, cols),
        ],
        compiler_params=pltpu.CompilerParams(vmem_limit_bytes=60 * MIB),
        cost_estimate=pl.CostEstimate(flops=1000, transcendentals=0, bytes_accessed=1000),
        name=name,
    )(lens, me, tok_core, tok_mid, own, *blocks, *after)
    return got[:6], got[6:]


def norm_near_kernel(
    own_ref, c0_ref, w0_ref, c1_ref, w1_ref, c2_ref, w2_ref, c3_ref, w3_ref, bo_ref, gain_ref, shift_ref,
    u0_ref, bias0_ref, d0_ref, u1_ref, bias1_ref, d1_ref,
    unit_ref, inv_ref, low_ref, act0_ref, sl0_ref, act1_ref, sl1_ref, sum_ref,
):
    pairs = ((c0_ref, w0_ref), (c1_ref, w1_ref), (c2_ref, w2_ref), (c3_ref, w3_ref))
    vectors = row(bo_ref), row(gain_ref), row(shift_ref)
    for pair in pairs:
        arrive(*pair)
    arrive(own_ref)

    def rows_of(rs):
        resid = own_ref[rs].astype(F32) + vectors[0]
        for c_ref, w_ref in pairs:
            resid = resid + dot(c_ref[rs], w_ref[...])
        unit, inverse = unit_of(resid)
        unit_ref[rs] = unit
        inv_ref[rs] = inverse
        low_ref[rs] = (unit * vectors[1] + vectors[2]).astype(BF)

    chunks(own_ref.shape[0], 256, rows_of)
    send(unit_ref)
    send(inv_ref)
    send(low_ref)
    up_down(low_ref, bias0_ref, (u0_ref,), d0_ref, act0_ref, sl0_ref, sum_ref, True)
    up_down(low_ref, bias1_ref, (u1_ref,), d1_ref, act1_ref, sl1_ref, sum_ref, False)


def norm_near(own, ctxs, joints, b_out, gain, shift, ups, downs, after=()):
    rows, width = own.shape
    units = downs[0].shape[0]
    at = joints[0].shape[0] - 16
    piece = shape((rows, units), BF)
    cols = ctxs[0].shape[1]
    terms = [x for pair in zip(ctxs, joints) for x in pair]
    return call(
        norm_near_kernel, "norm_near",
        [
            shape((rows, width), F32), shape((rows, 1), F32), shape((rows, width), BF),
            piece, piece, piece, piece, shape((rows, width), F32),
        ],
        (
            own, *terms, b_out, gain, shift,
            ups[0], joints[0], downs[0], ups[1], joints[1], downs[1],
        ),
        part={2 * i + 2: (3 * cols, cols) for i in range(4)} | {13: (at, 16), 16: (at, 16)},
        after=after, first=12,
    )


def attend_back_block(
    flag, g_ref, wo_ref, saved, own_ref, other, grad_ref, sums, b_s, bu_ref, vec_ref, scratch
):
    ct_ref, lse_ref, q_ref, k_ref, v_ref = saved
    d_s = sums
    gt_s, qt_s, kt_s, dqt_s, p_s, ds_s, dk_s, dv_s, dot_s, g_s, t_s = scratch
    rows, cols = q_ref.shape
    near = slice(0, rows)
    far = slice(rows, 2 * rows)
    arrive(g_ref, wo_ref)
    other = other()
    arrive(q_ref)

    def query_rows(rs):
        g = contract_cols(g_ref[rs], wo_ref[...]).astype(BF)
        g_s[rs] = g
        gt_s[:, rs] = g.T
        qt_s[:, rs] = q_ref[rs].T

    chunks(rows, 256, query_rows)
    arrive(k_ref)

    def key_rows(rs):
        kt_s[:, rs] = k_ref[rs].T

    chunks(2 * rows, 256, key_rows)
    dot_s[...] = gt_s[...].astype(F32) * ct_ref[...]
    dk_s[...] = jnp.zeros(dk_s.shape, F32)
    dv_s[...] = jnp.zeros(dv_s.shape, F32)
    head_of_row = lax.broadcasted_iota(jnp.int32, (cols, 1), 0) // HD
    head_of_lane = lax.broadcasted_iota(jnp.int32, (1, cols), 1) // HD
    arrive(q_ref, k_ref, v_ref, lse_ref)

    def head(h, carry):
        hs = pl.ds(pl.multiple_of(h * HD, HD), HD)
        row_dot = jnp.sum(dot_s[hs], axis=0, keepdims=True)
        q_h = masked(head_of_row == h, qt_s[...])
        g_h = masked(head_of_row == h, gt_s[...])
        lse = lse_ref[pl.ds(h, 1)]
        for part, shift in ((near, lse), (far, jnp.where(flag, lse, masked_shift))):
            p = jnp.exp(dot(k_ref[part], q_h) - shift)
            p_s[part] = p.astype(BF)
            ds_s[part] = (p * (dot(v_ref[part], g_h) - row_dot)).astype(BF)
        dqt_s[hs] = dot(kt_s[hs], ds_s[...])
        dk_s[...] += dot(ds_s[...], masked(head_of_lane == h, q_ref[...]))
        dv_s[...] += dot(p_s[...], masked(head_of_lane == h, g_s[...]))
        return carry

    lax.fori_loop(0, cols // HD, head, 0)
    dqt = (dqt_s[...] * score_scale).astype(BF)
    dq = dqt.T
    d_s[near, 0:cols] = dq
    d_s[far, 0:cols] = jnp.zeros((rows, cols), BF)
    t_s[0:cols, near] = dqt
    b_s[...] = jnp.zeros(b_s.shape, F32)

    def grad_rows(rs):
        dk = dk_s[rs].astype(BF)
        dv = dv_s[rs].astype(BF)
        d_s[rs, cols : 2 * cols] = dk
        d_s[rs, 2 * cols : 3 * cols] = dv
        t_s[cols : 2 * cols, rs] = dk.T
        t_s[2 * cols : 3 * cols, rs] = dv.T
        b_s[1:2, 0:cols] += jnp.sum(dv.astype(F32), axis=0, keepdims=True)

    chunks(2 * rows, 256, grad_rows)
    t_s[3 * cols : 4 * cols, near] = ct_ref[...].astype(BF)
    b_s[0:1, 0:cols] = jnp.sum(dq.astype(F32), axis=0, keepdims=True)
    b_s[2:3] = bu_ref[...]
    b_s[8:16] = vec_ref[...]
    at = 2 * cols
    grad_ref[at : at + 16] = b_s[...].astype(BF)
    grad_ref[at + 16 : at + 64] = jnp.zeros((48, b_s.shape[1]), BF)
    other()
    send(d_s)
    arrive(own_ref)
    width = own_ref.shape[1]

    def weight_terms(cs):
        tok = own_ref[:, cs]
        grad_ref[0:cols, cs] = dot(t_s[0:cols, near], tok).astype(BF)
        terms = (
            dot(t_s[cols : 3 * cols, near], tok) + dot(t_s[cols : 3 * cols, far], other.buffer[:, cs])
        ).astype(BF)
        grad_ref[cols : 2 * cols, cs] = terms[0:cols]
        grad_ref[at + 64 : at + 64 + cols, cs] = terms[cols : 2 * cols]
        grad_ref[at + 64 + cols : at + 64 + 2 * cols, cs] = dot(
            t_s[3 * cols : 4 * cols, near], g_ref[:, cs]
        ).astype(BF)

    chunks(width, 256, weight_terms)
    send(grad_ref)


def attend_back_kernel(
    lens_ref, me_ref, core_ref, mid_ref,
    g_ref, wo_ref, q_ref, k_ref, lse_ref, v_ref, ct_ref, own_ref, bu_ref, vec_ref,
    grad_ref, d_ref, oth_s, oth_sem, b_s, *scratch,
):
    flag, use_core = neighbour(lens_ref, me_ref, own_ref.shape[0])
    attend_back_block(
        flag, g_ref, wo_ref, (ct_ref, lse_ref, q_ref, k_ref, v_ref), own_ref,
        lambda: Once(pick_other(use_core, core_ref, mid_ref, oth_s, oth_sem), oth_s),
        grad_ref, d_ref, b_s, bu_ref, vec_ref, scratch,
    )


def attend_back(lens, me, own, tok_core, tok_mid, g, block, bu, vecs, after=()):
    rows, width = own.shape
    a, (_, ct, lse, q, k, v) = block
    cols = q.shape[1]
    args = (lens, me, tok_core, tok_mid, g, a, q, k, lse, v, ct, own, bu, vecs)
    return call(
        attend_back_kernel, "attend_back",
        [shape((4 * cols + 64, width), BF), shape((2 * rows, 3 * cols), BF)],
        args, smem=2, raw=(2, 3), after=after, first=8, part={5: (3 * cols, cols)},
        scratch=[
            pltpu.VMEM((rows, width), BF), pltpu.SemaphoreType.DMA, pltpu.VMEM((16, width), F32),
            pltpu.VMEM((cols, rows), BF), pltpu.VMEM((cols, rows), BF),
            pltpu.VMEM((cols, 2 * rows), BF), pltpu.VMEM((cols, rows), F32),
            pltpu.VMEM((2 * rows, rows), BF), pltpu.VMEM((2 * rows, rows), BF),
            pltpu.VMEM((2 * rows, cols), F32), pltpu.VMEM((2 * rows, cols), F32),
            pltpu.VMEM((cols, rows), F32), pltpu.VMEM((rows, cols), BF),
            pltpu.VMEM((4 * cols, 2 * rows), BF),
        ],
    )


def other_grad_kernel(*refs):
    ds, weights, out_ref = refs[0:4], refs[4:8], refs[8]
    arrive(*ds, *weights)
    depth = ds[0].shape[1]

    def features_of(cs):
        total = dot(ds[0][...], weights[0][0:depth, cs])
        for d_ref, w_ref in zip(ds[1:], weights[1:]):
            total = total + dot(d_ref[...], w_ref[0:depth, cs])
        out_ref[:, cs] = total.astype(out_ref.dtype)

    chunks(out_ref.shape[1], 256, features_of)


def other_grad(ds, joints, rows, after=()):
    width = joints[0].shape[1]
    return call(
        other_grad_kernel, "other_grad", [shape((rows, width), BF)], (*ds, *joints), after=after,
        part={i: (rows, rows) for i in range(4)} | {i: (0, ds[0].shape[1]) for i in range(4, 8)},
    )[0]


def unit_of(residual):
    centre = jnp.mean(residual, axis=1, keepdims=True)
    spread = residual - centre
    inverse = lax.rsqrt(jnp.mean(spread * spread, axis=1, keepdims=True) + norm_eps)
    return spread * inverse, inverse


def norm_back(upstream, unit_rows, inverse, gain):
    unit_grad = upstream * gain
    return inverse * (
        unit_grad
        - jnp.mean(unit_grad, axis=1, keepdims=True)
        - unit_rows * jnp.mean(unit_grad * unit_rows, axis=1, keepdims=True)
    )


def up_down(low_ref, bias_ref, up_refs, down_ref, act_ref, slope_ref, sum_ref, start):
    up_ref = up_refs[0]
    arrive(low_ref, bias_ref, up_ref)

    def units_of(cs):
        pre = bias_ref[:, cs].astype(F32)[2:3] + dot(low_ref[...], up_ref[:, cs])
        phi = 0.5 + 0.5 * lax.erf(pre * half_root)
        act_ref[:, cs] = (pre * phi).astype(BF)
        slope_ref[:, cs] = (phi + pre * jnp.exp(-0.5 * pre * pre) * inv_root_two_pi).astype(BF)

    chunks(up_ref.shape[1], 256, units_of)
    send(act_ref)
    send(slope_ref)
    arrive(down_ref)

    def features_of(cs):
        part = dot(act_ref[...], down_ref[:, cs])
        sum_ref[:, cs] = part if start else sum_ref[:, cs] + part

    chunks(down_ref.shape[1], 256, features_of)


def ffn_back_block(
    g_ref, low_ref, act_ref, slope_ref, down_ref, up_refs, outs, sum_in_ref, sum_ref, pre_s
):
    down_grad_ref, up_grad_ref, bias_ref = outs
    up_ref = up_refs[0]
    arrive(g_ref, act_ref, slope_ref, down_ref)

    def units_of(cs):
        g = g_ref[...]
        down_grad_ref[cs] = contract_rows(act_ref[:, cs], g).astype(BF)
        pre = (contract_cols(g, down_ref[cs]) * slope_ref[:, cs].astype(F32)).astype(BF)
        pre_s[:, cs] = pre
        bias_ref[:, cs] = jnp.sum(pre.astype(F32), axis=0, keepdims=True)

    chunks(down_ref.shape[0], 256, units_of)
    send(down_grad_ref)
    arrive(low_ref, up_ref, sum_in_ref)

    def features_of(cs):
        pre = pre_s[...]
        up_grad_ref[cs] = contract_rows(low_ref[:, cs], pre).astype(BF)
        sum_ref[:, cs] = sum_in_ref[:, cs] + contract_cols(pre, up_ref[cs])

    chunks(up_ref.shape[0], 256, features_of)
    send(up_grad_ref)


def ffn_grad_outs(width, units):
    return [shape((units, width), BF), shape((width, units), BF), shape((1, units), F32)]


def ffn_far_kernel(
    low_ref, u2_ref, bias2_ref, d2_ref, u3_ref, bias3_ref, d3_ref,
    sum_in_ref, unit_ref, gain1_ref, shift1_ref, bd_ref, gain2_ref, shift2_ref, out_grad_ref,
    act2_ref, sl2_ref, out_ref, low_grad_ref, vec_ref,
    down_grad_ref, up_grad_ref, bu_ref, sum_ref,
    act3_s, sl3_s, pre_s, part_s,
):
    up_down(low_ref, bias2_ref, (u2_ref,), d2_ref, act2_ref, sl2_ref, part_s, True)
    up_down(low_ref, bias3_ref, (u3_ref,), d3_ref, act3_s, sl3_s, part_s, False)
    gain1, gain2, shift2 = row(gain1_ref), row(gain2_ref), row(shift2_ref)
    shift1 = row(shift1_ref) + row(bd_ref)
    arrive(unit_ref, sum_in_ref, out_grad_ref)
    vec_ref[...] = jnp.zeros(vec_ref.shape, F32)

    def rows_of(rs):
        resid = unit_ref[rs] * gain1 + shift1 + sum_in_ref[rs] + part_s[rs]
        unit, inverse = unit_of(resid)
        out_ref[rs] = (unit * gain2 + shift2).astype(BF)
        upstream = out_grad_ref[rs].astype(F32)
        vec_ref[0:1] += jnp.sum(upstream * unit, axis=0, keepdims=True)
        vec_ref[1:2] += jnp.sum(upstream, axis=0, keepdims=True)
        back = norm_back(upstream, unit, inverse, gain2)
        sum_ref[rs] = back
        g = back.astype(BF)
        low_grad_ref[rs] = g
        vec_ref[2:3] += jnp.sum(g.astype(F32), axis=0, keepdims=True)

    chunks(unit_ref.shape[0], 256, rows_of)
    send(out_ref)
    send(low_grad_ref)
    ffn_back_block(
        low_grad_ref, low_ref, act3_s, sl3_s, d3_ref, (u3_ref,),
        (down_grad_ref, up_grad_ref, bu_ref), sum_ref, sum_ref, pre_s,
    )


def ffn_far(
    low, joints, ups, downs, near, unit, gain1, shift1, b_down, gain2, shift2, out_grad, after=()
):
    rows, width = low.shape
    units = downs[0].shape[0]
    at = joints[0].shape[0] - 16
    piece = shape((rows, units), BF)
    return call(
        ffn_far_kernel, "ffn_far",
        [
            piece, piece, shape((rows, width), BF), shape((rows, width), BF), shape((8, width), F32),
            *ffn_grad_outs(width, units), shape((rows, width), F32),
        ],
        (
            low, ups[0], joints[0], downs[0], ups[1], joints[1], downs[1], near, unit,
            gain1, shift1, b_down, gain2, shift2, out_grad,
        ),
        part={2: (at, 16), 5: (at, 16)}, first=4, after=after,
        scratch=[pltpu.VMEM((rows, units), BF)] * 3 + [pltpu.VMEM((rows, width), F32)],
    )


def ffn_back_kernel(
    g_ref, act_ref, down_ref, slope_ref, low_ref, up_ref, sum_in_ref,
    down_grad_ref, up_grad_ref, bu_ref, sum_ref, pre_s,
):
    ffn_back_block(
        g_ref, low_ref, act_ref, slope_ref, down_ref, (up_ref,),
        (down_grad_ref, up_grad_ref, bu_ref), sum_in_ref, sum_ref, pre_s,
    )


def ffn_back(g, low, act, slope, up, down, acc, after=()):
    rows, width = low.shape
    units = down.shape[0]
    return call(
        ffn_back_kernel, "ffn_back",
        [*ffn_grad_outs(width, units), shape((rows, width), F32)],
        (g, act, down, slope, low, up, acc), after=after, first=2,
        scratch=[pltpu.VMEM((rows, units), BF)],
    )


def ffn_last_kernel(
    g_ref, act1_ref, d1_ref, sl1_ref, low_ref, u1_ref, act0_ref, d0_ref, sl0_ref, u0_ref, sum_in_ref,
    unit_ref, inv_ref, gain_ref, vec_in_ref, *refs,
):
    low_ref_out, resid_ref, vec_ref = refs[6:9]
    sum_s, pre_s = refs[9:]
    ffn_back_block(
        g_ref, low_ref, act1_ref, sl1_ref, d1_ref, (u1_ref,), refs[0:3], sum_in_ref, sum_s, pre_s
    )
    ffn_back_block(
        g_ref, low_ref, act0_ref, sl0_ref, d0_ref, (u0_ref,), refs[3:6], sum_s, sum_s, pre_s
    )
    gain = row(gain_ref)
    arrive(unit_ref, inv_ref)
    vec_ref[...] = vec_in_ref[...]

    def rows_of(rs):
        upstream = sum_s[rs]
        unit = unit_ref[rs]
        vec_ref[4:5] += jnp.sum(upstream * unit, axis=0, keepdims=True)
        vec_ref[5:6] += jnp.sum(upstream, axis=0, keepdims=True)
        back = norm_back(upstream, unit, inv_ref[rs], gain)
        resid_ref[rs] = back
        low = back.astype(BF)
        low_ref_out[rs] = low
        vec_ref[6:7] += jnp.sum(low.astype(F32), axis=0, keepdims=True)

    chunks(unit_ref.shape[0], 256, rows_of)
    send(resid_ref)
    send(low_ref_out)


def ffn_last(g, low, acts, slopes, ups, downs, acc, unit, inverse, gain, vecs, after=()):
    rows, width = low.shape
    units = downs[0].shape[0]
    return call(
        ffn_last_kernel, "ffn_last",
        [
            *ffn_grad_outs(width, units), *ffn_grad_outs(width, units),
            shape((rows, width), BF), shape((rows, width), F32), shape((8, width), F32),
        ],
        (
            g, acts[1], downs[1], slopes[1], low, ups[1], acts[0], downs[0], slopes[0], ups[0], acc,
            unit, inverse, gain, vecs,
        ),
        after=after, first=2,
        scratch=[pltpu.VMEM((rows, width), F32), pltpu.VMEM((rows, units), BF)],
    )


def spread_small_kernel(in_ref, bq_ref, bv_ref, bu_ref, *rest):
    sums = in_ref[...]
    cols = bq_ref.shape[0]
    bq_ref[...] = sums[0:1, 0:cols].reshape(cols)
    bv_ref[...] = sums[1:2, 0:cols].reshape(cols)
    bu_ref[...] = sums[2:3].reshape(-1)
    for at, ref in zip((8, 9, 10, 12, 13, 14), rest):
        ref[...] = sums[at : at + 1].reshape(-1)


def spread_small(sums, cols, units):
    width = sums.shape[1]
    return call(
        spread_small_kernel, "spread_small",
        [shape((cols,), F32), shape((cols,), F32), shape((units,), F32)] + [shape((width,), F32)] * 6,
        (sums,), part={0: (2 * cols, 16)},
    )


def swap(a, axis, distance):
    size = lax.axis_size(axis)
    return lax.ppermute(a, axis, [(i, i ^ distance) for i in range(size)])


def to_core(a):
    return swap(a, "narrow", 1)


def to_chip(a):
    return swap(a, "narrow", 2)


def to_middle(a):
    return lax.ppermute(a, "narrow", [(1, 2), (2, 1)])


def wide_bits():
    size = lax.axis_size("wide")
    bits = []
    while size > 1:
        assert size % 2 == 0
        bits.append(len(bits))
        size //= 2
    return bits


def part_of(a, which, parts):
    rows = a.shape[0] // parts
    return lax.dynamic_slice_in_dim(a, which * rows, rows, 0)


def in_order(side, mine, got):
    return jnp.where(side == 0, jnp.concatenate([mine, got]), jnp.concatenate([got, mine]))


def hold(a, *others):
    return lax.optimization_barrier((a, *others))[0]


def add_low(*terms):
    total = terms[0].astype(F32)
    for term in terms[1:]:
        total = total + term.astype(F32)
    return total.astype(BF)


def side_of(bit):
    return (lax.axis_index("wide") >> bit) & 1


def own_piece(a):
    at = 0
    for bit in wide_bits():
        at = 2 * at + side_of(bit)
    return part_of(a, at, lax.axis_size("wide"))


class WideSum:
    def __init__(self, a):
        self.a = a
        self.step = 0
        self.send()

    def send(self):
        bit = self.step
        if bit < 3:
            side = side_of(bit)
            self.keep = part_of(self.a, side, 2)
            self.sent = part_of(self.a, 1 - side, 2)
        else:
            self.keep = self.sent = self.a
        self.got = swap(self.sent, "wide", 1 << bit)

    def advance(self, *waits):
        got = hold(self.got, *waits) if waits else self.got
        self.a = add_low(self.keep, got)
        self.step += 1
        if self.step < len(wide_bits()):
            self.send()

    def piece(self, *waits):
        while self.step < len(wide_bits()):
            self.advance(*waits)
            waits = ()
        return self.a


class WideGather:
    def __init__(self, a, bits=(2, 1, 0)):
        self.a = self.sent = a
        self.bits = bits
        self.step = 0
        self.send()

    def send(self):
        self.sent = self.a
        self.got = swap(self.a, "wide", 1 << self.bits[self.step])

    def advance(self, *waits):
        got = hold(self.got, *waits) if waits else self.got
        self.a = in_order(side_of(self.bits[self.step]), self.a, got)
        self.step += 1
        if self.step < len(self.bits):
            self.send()

    def whole(self, *waits):
        while self.step < len(self.bits):
            self.advance(*waits)
            waits = ()
        return self.a


def local(
    tokens, item_lengths, w_query, b_query, w_key, w_value, b_value, w_out, b_out,
    gain_attn, shift_attn, w_up, b_up, w_down, b_down, gain_ffn, shift_ffn, out_grad,
):
    rows, width = tokens.shape
    cols = w_query.shape[1]
    units = w_up.shape[1]
    assert lax.axis_size("narrow") == 4
    me = lax.axis_index("narrow").reshape(1)

    tok_mid = to_middle(tokens)
    tok_core = to_core(tokens)
    pieces = to_chip(own_piece(w_down))
    joint = pack_joint(w_query, w_key, w_value, w_out, b_query, b_value, b_up)
    joint_core = to_core(joint)
    joint_chip = to_chip(hold(joint, pieces, tok_mid))
    down_gather = WideGather(pieces, wide_bits()[::-1])
    while down_gather.step < len(down_gather.bits) - 2:
        down_gather.advance(joint_core)
    near0, near1 = attend_pair(
        "attend_near", item_lengths, me, tokens, tok_core, tok_mid, [joint, joint_core],
        (down_gather.sent,),
    )
    down_gather.advance(near1[2])
    gate = down_gather.sent
    joint_chip = hold(joint_chip, gate)
    joint_diag = to_core(joint_chip)
    up_chip = to_chip(hold(w_up, joint_chip))
    up_core = to_core(hold(w_up, joint_chip))
    down_core = to_core(hold(w_down, joint_chip))
    far2, far3 = attend_pair(
        "attend_far", item_lengths, me, tokens, tok_core, tok_mid, [joint_chip, joint_diag], (gate,)
    )
    joints = [joint, joint_core, joint_chip, joint_diag]
    saved = [near0, near1, far2, far3]
    unit_one, inv_one, low, act0, sl0, act1, sl1, near_sum = norm_near(
        tokens, [s[0] for s in saved], joints, b_out, gain_attn, shift_attn,
        [w_up, up_core], [w_down, down_core],
    )
    down_chip = down_gather.whole(inv_one)
    down_diag = to_core(down_chip)
    up_chip = hold(up_chip, down_chip)
    up_diag = to_core(up_chip)
    act2, sl2, layer_out, ffn_grad, vecs, down_d, up_d, bu_d, acc = ffn_far(
        low, joints[2:], [up_chip, up_diag], [down_chip, down_diag],
        near_sum, unit_one, gain_attn, shift_attn, b_down, gain_ffn, shift_ffn, out_grad,
    )

    up_from_core = to_core(up_d)
    down_from_core = to_core(down_d)
    down_x, up_x, bu_x, acc = ffn_back(ffn_grad, low, act2, sl2, up_chip, down_chip, acc)
    up_far = add_low(up_x, hold(up_from_core, bu_x))
    up_sum = to_chip(up_far)
    down_far = add_low(down_x, hold(down_from_core, up_far))
    down_sum = to_chip(down_far)
    down_c, up_c, bu_c, down_o, up_o, bu_o, attn_grad, resid_one, vecs = ffn_last(
        ffn_grad, low, (act0, act1), (sl0, sl1), (w_up, up_core), (w_down, down_core), acc,
        unit_one, inv_one, gain_attn, vecs, (up_far, down_far),
    )
    up_back = to_core(up_c)
    down_back = to_core(down_c)
    grads, parts = [None] * 4, [None] * 4
    bus = (bu_o, bu_c, bu_x, bu_d)

    def back_attend(r, *after):
        grads[r], parts[r] = attend_back(
            item_lengths, me, tokens, tok_core, tok_mid, attn_grad, (joints[r], saved[r]),
            bus[r], vecs, after,
        )
        return grads[r]

    mark = back_attend(3)
    up_sum = hold(up_sum, mark)
    near_up = WideSum(add_low(up_o, hold(up_back, up_sum), up_sum))
    down_near = add_low(down_o, hold(down_back, near_up.sent))
    joint_from_core = to_core(hold(grads[3], down_near))
    mark = back_attend(2, near_up.sent, down_near)
    down_sum = hold(down_sum, mark)
    near_down = WideSum(add_low(down_near, down_sum))
    joint_far = add_low(grads[2], hold(joint_from_core, near_down.a))
    joint_sum = to_chip(joint_far)
    near_up.advance(joint_far)
    mark = back_attend(1, joint_far, near_up.sent, near_down.sent)
    near_up.advance(mark)
    near_down.advance(near_up.sent)
    joint_back = to_core(hold(grads[1], near_down.sent))
    mark = back_attend(0, near_up.sent, near_down.sent)
    joint_sum = hold(joint_sum, mark)
    joint_back = hold(joint_back, joint_sum)

    def rows_of(a, part):
        return a[: 2 * cols + 64] if part == 0 else a[2 * cols + 64 :]

    def joint_part(i, own, got):
        return WideSum(add_low(rows_of(own, i), rows_of(got, i), rows_of(joint_back, i)))

    first = joint_part(0, grads[0], joint_sum)
    second = joint_part(1, grads[0], hold(joint_sum, first.sent))
    up_gather = WideGather(near_up.piece(second.sent))
    near_down.advance(up_gather.sent)
    first.advance(near_down.sent)
    down_gather = WideGather(near_down.piece(first.sent))
    up_gather.advance(down_gather.sent)
    second.advance(up_gather.sent)
    oth_low = other_grad(parts, joints, rows, (second.sent,))
    first.advance(oth_low)
    up_gather.advance(first.sent)
    down_gather.advance(up_gather.sent)
    oth_core, oth_mid = to_core(hold(oth_low, down_gather.sent)), to_middle(hold(oth_low, down_gather.sent))
    second.advance(down_gather.sent)
    first = WideGather(first.piece(second.sent))
    down_gather.advance(first.sent)
    second = WideGather(second.piece(down_gather.sent))
    first.advance(second.sent)
    token_grad = take_back(
        item_lengths, me, hold(oth_core, first.sent), hold(oth_mid, first.sent), resid_one,
        parts, joints, (first.sent, second.sent),
    )
    second.advance(token_grad)
    first.advance(second.sent)
    w_up_grad = up_gather.whole(first.sent).astype(F32)
    second.advance(w_up_grad)
    w_down_grad = down_gather.whole(second.sent).astype(F32)
    qk_grad = first.whole(w_down_grad).astype(F32)
    bq, bv, bu, gain_ffn_g, shift_ffn_g, b_down_g, gain_attn_g, shift_attn_g, b_out_g = spread_small(
        qk_grad, cols, units
    )
    vo_grad = second.whole(qk_grad).astype(F32)
    joint_grads = [qk_grad[:cols], qk_grad[cols : 2 * cols], vo_grad[:cols]]
    w_out_grad = vo_grad[cols:]
    return (
        layer_out,
        token_grad,
        joint_grads[0].T,
        bq,
        joint_grads[1].T,
        joint_grads[2].T,
        bv,
        w_out_grad,
        b_out_g,
        gain_attn_g,
        shift_attn_g,
        w_up_grad,
        bu,
        w_down_grad,
        b_down_g,
        gain_ffn_g,
        shift_ffn_g,
    )


def take_back_kernel(lens_ref, me_ref, core_ref, mid_ref, *refs):
    ds, weights, resid_ref, out_ref, oth_s, oth_sem = refs[0:4], refs[4:8], *refs[8:]
    flag, use_core = neighbour(lens_ref, me_ref, resid_ref.shape[0])
    other = pick_other(use_core, core_ref, mid_ref, oth_s, oth_sem)
    arrive(*ds, *weights, resid_ref)
    other.wait()
    depth = ds[0].shape[1]

    def features_of(cs):
        total = resid_ref[:, cs] + jnp.where(flag, oth_s[:, cs].astype(F32), 0.0)
        for d_ref, w_ref in zip(ds, weights):
            total = total + dot(d_ref[...], w_ref[0:depth, cs])
        out_ref[:, cs] = total

    chunks(out_ref.shape[1], 256, features_of)


def take_back(lens, me, core, mid, resid, ds, joints, after):
    rows, width = resid.shape
    depth = ds[0].shape[1]
    return call(
        take_back_kernel, "take_back", [shape((rows, width), F32)],
        (lens, me, core, mid, *ds, *joints, resid), smem=2, raw=(2, 3), after=after,
        part={i: (0, rows) for i in range(4, 8)} | {i: (0, depth) for i in range(8, 12)},
        scratch=[pltpu.VMEM(core.shape, BF), pltpu.SemaphoreType.DMA],
    )[0]


def solution(mesh):
    rows_spec = P(("wide", "narrow"), None)
    col_spec = P(None, "narrow")
    vec_spec = P("narrow")
    row_spec = P("narrow", None)
    full = P()
    return jax.shard_map(
        local,
        mesh=mesh,
        in_specs=(
            rows_spec, P("wide"), col_spec, vec_spec, col_spec, col_spec, vec_spec, row_spec, full,
            full, full, col_spec, vec_spec, row_spec, full, full, full, rows_spec,
        ),
        out_specs=(
            rows_spec, rows_spec, col_spec, vec_spec, col_spec, col_spec, vec_spec, row_spec, full,
            full, full, col_spec, vec_spec, row_spec, full, full, full,
        ),
        check_vma=False,
    )
```

```python
import functools

import jax
import jax.numpy as jnp
from jax import lax
from jax.experimental import pallas as pl
from jax.experimental.pallas import tpu as pltpu
from jax.sharding import PartitionSpec as P

HD = 64
F32 = jnp.float32
BF = jnp.bfloat16
MIB = 1 << 20

norm_eps = 1e-12
masked_shift = 1e30
half_root = 0.7071067811865476
inv_root_two_pi = 0.3989422804014327
score_scale = HD**-0.5

VM = pl.BlockSpec(memory_space=pltpu.VMEM)
SM = pl.BlockSpec(memory_space=pltpu.SMEM)
ANY = pl.BlockSpec(memory_space=pl.ANY)


def dot(left, right):
    return jnp.dot(left, right, preferred_element_type=F32)


def contract_rows(left, right):
    return lax.dot_general(left, right, (((0,), (0,)), ((), ())), preferred_element_type=F32)


def contract_cols(left, right):
    return lax.dot_general(left, right, (((1,), (1,)), ((), ())), preferred_element_type=F32)


def shape(dims, dtype):
    return jax.ShapeDtypeStruct(dims, dtype)


def row(ref):
    return ref[...].astype(F32).reshape(1, -1)


class Arriving:
    def __init__(self, source, buffer, sem):
        self.buffer = buffer
        self.shape = buffer.shape
        self.dtype = buffer.dtype
        self.copy = pltpu.make_async_copy(source, buffer, sem)
        self.started = False
        self.waiting = True
        self.then = []

    def start(self):
        if not self.started:
            self.copy.start()
            self.started = True

    def wait(self):
        self.start()
        if self.waiting:
            self.copy.wait()
            self.waiting = False
            for other in self.then:
                other.start()

    def __getitem__(self, index):
        self.wait()
        return self.buffer[index]


class Leaving:
    def __init__(self, target, buffer, sem):
        self.buffer = buffer
        self.shape = buffer.shape
        self.dtype = buffer.dtype
        self.copy = pltpu.make_async_copy(buffer, target, sem)
        self.sent = False

    def __getitem__(self, index):
        return self.buffer[index]

    def __setitem__(self, index, value):
        self.buffer[index] = value

    def send(self):
        if not self.sent:
            self.copy.start()
            self.sent = True


def call(
    kernel, name, out_shape, args, smem=0, scratch=(), vmem=60, after=(), raw=(), part=(), first=0,
    stay=(), stay_out=(),
):
    count = len(args)
    outs = len(out_shape)
    loaded = [i for i in range(smem, count) if i not in raw and i not in stay]
    leaving_out = [n for n in range(outs) if n not in stay_out]
    part = dict(part)

    def held(i):
        dims = (part[i][1], *args[i].shape[1:]) if i in part else args[i].shape
        return pltpu.VMEM(dims, args[i].dtype)

    buffers = [held(i) for i in loaded]
    buffers += [pltpu.VMEM(out_shape[n].shape, out_shape[n].dtype) for n in leaving_out]

    def body(*refs):
        given = list(refs[:count])
        refs = refs[count + len(after) :]
        results, refs = list(refs[:outs]), refs[outs:]
        own, refs = refs[: len(buffers)], refs[len(buffers) :]
        in_sems, out_sems, refs = refs[0], refs[1], refs[2:]
        for n, i in enumerate(loaded):
            source = given[i].at[pl.ds(*part[i])] if i in part else given[i]
            given[i] = Arriving(source, own[n], in_sems.at[n])
        late = [given[i] for i in loaded if first and i >= first]
        for i in loaded:
            if given[i] not in late:
                given[i].start()
                given[i].then = late
        for m, n in enumerate(leaving_out):
            results[n] = Leaving(results[n], own[len(loaded) + m], out_sems.at[m])
        kernel(*given, *results, *refs)
        for i in loaded:
            given[i].wait()
        for n in leaving_out:
            results[n].send()
        for n in leaving_out:
            results[n].copy.wait()

    in_specs = [SM] * smem + [VM if i in stay else ANY for i in range(smem, count)]
    return pl.pallas_call(
        body,
        out_shape=tuple(out_shape),
        in_specs=in_specs + [ANY] * len(after),
        out_specs=tuple(VM if n in stay_out else ANY for n in range(outs)),
        scratch_shapes=[
            *buffers, pltpu.SemaphoreType.DMA((max(len(loaded), 1),)),
            pltpu.SemaphoreType.DMA((max(len(leaving_out), 1),)), *scratch,
        ],
        compiler_params=pltpu.CompilerParams(vmem_limit_bytes=vmem * MIB),
        cost_estimate=pl.CostEstimate(flops=1000, transcendentals=0, bytes_accessed=1000),
        name=name,
    )(*args, *after)


def send(ref):
    if isinstance(ref, Leaving):
        ref.send()


def arrive(*refs):
    for ref in refs:
        if isinstance(ref, Arriving):
            ref.wait()


def chunks(extent, size, body):
    def step(i, carry):
        body(pl.ds(pl.multiple_of(i * size, size), size))
        return carry

    lax.fori_loop(0, extent // size, step, 0)


def masked(picked, a):
    return jnp.where(picked, a.astype(F32), 0.0).astype(BF)


def joint_kernel(wq_ref, wk_ref, wv_ref, wo_ref, bq_ref, bv_ref, bu_ref, out_ref, tail_s):
    cols = wq_ref.shape[0]
    for i, ref in enumerate((wq_ref, wk_ref, wv_ref, wo_ref)):
        out_ref[i * cols : (i + 1) * cols] = ref[...]
    tail_s[...] = jnp.zeros_like(tail_s)
    tail_s[0:1, 0:cols] = row(bq_ref)
    tail_s[1:2, 0:cols] = row(bv_ref)
    tail_s[2:3, :] = row(bu_ref)
    out_ref[4 * cols : 4 * cols + 16] = tail_s[...].astype(BF)


def pack_joint(w_query, w_key, w_value, w_out, b_query, b_value, b_up):
    width, cols = w_query.shape
    return call(
        joint_kernel, "pack_joint", [shape((4 * cols + 16, width), BF)],
        (w_query.T, w_key.T, w_value.T, w_out, b_query, b_value, b_up),
        scratch=[pltpu.VMEM((16, width), F32)],
    )[0]


def neighbour(lens_ref, me_ref, rows):
    me = me_ref[0]
    here = me * rows
    first = jnp.int32(0)
    start = jnp.int32(0)
    length = jnp.int32(0)
    for j in range(lens_ref.shape[0]):
        n = lens_ref[j]
        inside = (first <= here) & (here < first + n)
        start = jnp.where(inside, first, start)
        length = jnp.where(inside, n, length)
        first = first + n
    other = jnp.where(start == here, me + 1, me - 1)
    return length > rows, other == (me ^ 1)


def pick_other(use_core, core_ref, mid_ref, buffer, sem):
    from_core = pltpu.make_async_copy(core_ref, buffer, sem)
    from_mid = pltpu.make_async_copy(mid_ref, buffer, sem)

    @pl.when(use_core)
    def _():
        from_core.start()

    @pl.when(jnp.logical_not(use_core))
    def _():
        from_mid.start()

    return from_core


def attend_block(flag, own_ref, oth_s, a_ref, outs, scratch):
    ctx_ref, ct_ref, lse_ref, q_ref, k_ref, v_ref = outs
    qt_s, vt_s = scratch
    rows, cols = q_ref.shape
    tail = a_ref[4 * cols : 4 * cols + 16].astype(F32)
    wk = a_ref[cols : 2 * cols]
    wv = a_ref[2 * cols : 3 * cols]
    near = slice(0, rows)
    far = slice(rows, 2 * rows)
    q = (contract_cols(own_ref[...], a_ref[0:cols]) + tail[0:1, 0:cols]).astype(BF)
    q = q * jnp.asarray(score_scale, BF)
    q_ref[...] = q
    qt_s[...] = q.T
    for part, tok_ref in ((near, own_ref), (far, oth_s)):
        k_ref[part] = contract_cols(tok_ref[...], wk).astype(BF)
        v = (contract_cols(tok_ref[...], wv) + tail[1:2, 0:cols]).astype(BF)
        v_ref[part] = v
        vt_s[:, part] = v.T
    head_of_row = lax.broadcasted_iota(jnp.int32, (cols, 1), 0) // HD

    def head(h, carry):
        hs = pl.ds(pl.multiple_of(h * HD, HD), HD)
        q_h = masked(head_of_row == h, qt_s[...])
        s_own = dot(k_ref[near], q_h)
        s_other = dot(k_ref[far], q_h)
        top_own = jnp.max(s_own, axis=0, keepdims=True)
        top_other = jnp.max(s_other, axis=0, keepdims=True)
        top = jnp.where(flag, jnp.maximum(top_own, top_other), top_own)
        p_own = jnp.exp(s_own - top)
        p_other = jnp.exp(s_other - jnp.where(flag, top, masked_shift))
        total = jnp.sum(p_own, axis=0, keepdims=True) + jnp.sum(p_other, axis=0, keepdims=True)
        c = dot(vt_s[hs, near], p_own.astype(BF)) + dot(vt_s[hs, far], p_other.astype(BF))
        ct_ref[hs] = c * (1.0 / total)
        lse_ref[pl.ds(h, 1)] = top + jnp.log(total)
        return carry

    lax.fori_loop(0, cols // HD, head, 0)
    ctx_ref[...] = ct_ref[...].T.astype(BF)


def block_outs(rows, cols):
    return [
        shape((rows, cols), BF), shape((cols, rows), F32), shape((cols // HD, rows), F32),
        shape((rows, cols), BF), shape((2 * rows, cols), BF), shape((2 * rows, cols), BF),
    ]


def attend_scratch(rows, width, cols):
    return [
        pltpu.VMEM((rows, width), BF), pltpu.SemaphoreType.DMA,
        pltpu.VMEM((cols, rows), BF), pltpu.VMEM((cols, 2 * rows), BF),
    ]


class Once:
    def __init__(self, copy, buffer):
        self.copy = copy
        self.buffer = buffer

    def __call__(self):
        if self.copy is not None:
            self.copy.wait()
            self.copy = None
        return self.buffer[...]


def attend_pair_kernel(
    lens_ref, me_ref, core_ref, mid_ref, own_ref, a0_ref, a1_ref, *refs, after
):
    targets = refs[after : after + 12]
    own_s, a_s, *held = refs[after + 12 : after + 20]
    own_sem, a_sem, out_sem, oth_s, oth_sem, qt_s, vt_s = refs[after + 20 :]
    own_copy = pltpu.make_async_copy(own_ref, own_s, own_sem)
    own_copy.start()
    weights = [
        pltpu.make_async_copy(ref, a_s.at[i], a_sem.at[i]) for i, ref in enumerate((a0_ref, a1_ref))
    ]
    weights[0].start()
    flag, use_core = neighbour(lens_ref, me_ref, own_ref.shape[0])
    other = pick_other(use_core, core_ref, mid_ref, oth_s, oth_sem)
    leaving = [
        [
            pltpu.make_async_copy(buffer.at[i], targets[6 * i + n], out_sem.at[i, n])
            for n, buffer in enumerate(held)
        ]
        for i in range(2)
    ]
    own_copy.wait()

    def block(i, carry):
        @pl.when(i == 0)
        def _():
            weights[0].wait()
            other.wait()
            weights[1].start()

        @pl.when(i == 1)
        def _():
            weights[1].wait()

        attend_block(
            flag, own_s, oth_s, a_s.at[i], [buffer.at[i] for buffer in held], (qt_s, vt_s)
        )
        for n in range(2):

            @pl.when(i == n)
            def _():
                for copy in leaving[n]:
                    copy.start()

        return carry

    lax.fori_loop(0, 2, block, 0)
    for copies in leaving:
        for copy in copies:
            copy.wait()


def attend_pair(name, lens, me, own, tok_core, tok_mid, blocks, after=()):
    rows, width = own.shape
    cols = (blocks[0].shape[0] - 16) // 4
    outs = block_outs(rows, cols)
    got = pl.pallas_call(
        functools.partial(attend_pair_kernel, after=len(after)),
        out_shape=tuple(outs * 2),
        in_specs=[SM, SM] + [ANY] * (5 + len(after)),
        out_specs=tuple([ANY] * 12),
        scratch_shapes=[
            pltpu.VMEM(own.shape, BF), pltpu.VMEM((2, *blocks[0].shape), BF),
            *[pltpu.VMEM((2, *o.shape), o.dtype) for o in outs],
            pltpu.SemaphoreType.DMA, pltpu.SemaphoreType.DMA((2,)), pltpu.SemaphoreType.DMA((2, 6)),
            *attend_scratch(rows, width, cols),
        ],
        compiler_params=pltpu.CompilerParams(vmem_limit_bytes=60 * MIB),
        cost_estimate=pl.CostEstimate(flops=1000, transcendentals=0, bytes_accessed=1000),
        name=name,
    )(lens, me, tok_core, tok_mid, own, *blocks, *after)
    return got[:6], got[6:]


def norm_near_kernel(
    own_ref, c0_ref, w0_ref, c1_ref, w1_ref, c2_ref, w2_ref, c3_ref, w3_ref, bo_ref, gain_ref, shift_ref,
    u0_ref, bias0_ref, d0_ref, u1_ref, bias1_ref, d1_ref,
    unit_ref, inv_ref, low_ref, act0_ref, sl0_ref, act1_ref, sl1_ref, sum_ref,
):
    pairs = ((c0_ref, w0_ref), (c1_ref, w1_ref), (c2_ref, w2_ref), (c3_ref, w3_ref))
    vectors = row(bo_ref), row(gain_ref), row(shift_ref)
    for pair in pairs:
        arrive(*pair)
    arrive(own_ref)

    def rows_of(rs):
        resid = own_ref[rs].astype(F32) + vectors[0]
        for c_ref, w_ref in pairs:
            resid = resid + dot(c_ref[rs], w_ref[...])
        unit, inverse = unit_of(resid)
        unit_ref[rs] = unit
        inv_ref[rs] = inverse
        low_ref[rs] = (unit * vectors[1] + vectors[2]).astype(BF)

    chunks(own_ref.shape[0], 256, rows_of)
    send(unit_ref)
    send(inv_ref)
    send(low_ref)
    up_down(low_ref, bias0_ref, (u0_ref,), d0_ref, act0_ref, sl0_ref, sum_ref, True)
    up_down(low_ref, bias1_ref, (u1_ref,), d1_ref, act1_ref, sl1_ref, sum_ref, False)


def norm_near(own, ctxs, joints, b_out, gain, shift, ups, downs, after=()):
    rows, width = own.shape
    units = downs[0].shape[0]
    at = joints[0].shape[0] - 16
    piece = shape((rows, units), BF)
    cols = ctxs[0].shape[1]
    terms = [x for pair in zip(ctxs, joints) for x in pair]
    return call(
        norm_near_kernel, "norm_near",
        [
            shape((rows, width), F32), shape((rows, 1), F32), shape((rows, width), BF),
            piece, piece, piece, piece, shape((rows, width), F32),
        ],
        (
            own, *terms, b_out, gain, shift,
            ups[0], joints[0], downs[0], ups[1], joints[1], downs[1],
        ),
        part={2 * i + 2: (3 * cols, cols) for i in range(4)} | {13: (at, 16), 16: (at, 16)},
        after=after, first=0,
    )


def attend_back_block(
    flag, g_ref, wo_ref, saved, own_ref, other, grad_ref, sums, b_s, bu_ref, vec_ref, scratch
):
    ct_ref, lse_ref, q_ref, k_ref, v_ref = saved
    d_s = sums
    gt_s, qt_s, kt_s, dqt_s, p_s, ds_s, dk_s, dv_s, dot_s, g_s, t_s = scratch
    rows, cols = q_ref.shape
    near = slice(0, rows)
    far = slice(rows, 2 * rows)
    arrive(g_ref, wo_ref)
    other = other()
    arrive(q_ref)

    def query_rows(rs):
        g = contract_cols(g_ref[rs], wo_ref[...]).astype(BF)
        g_s[rs] = g
        gt_s[:, rs] = g.T
        qt_s[:, rs] = q_ref[rs].T

    chunks(rows, 256, query_rows)
    arrive(k_ref)

    def key_rows(rs):
        kt_s[:, rs] = k_ref[rs].T

    chunks(2 * rows, 256, key_rows)
    dot_s[...] = gt_s[...].astype(F32) * ct_ref[...]
    dk_s[...] = jnp.zeros(dk_s.shape, F32)
    dv_s[...] = jnp.zeros(dv_s.shape, F32)
    head_of_row = lax.broadcasted_iota(jnp.int32, (cols, 1), 0) // HD
    head_of_lane = lax.broadcasted_iota(jnp.int32, (1, cols), 1) // HD
    arrive(q_ref, k_ref, v_ref, lse_ref)

    def head(h, carry):
        hs = pl.ds(pl.multiple_of(h * HD, HD), HD)
        row_dot = jnp.sum(dot_s[hs], axis=0, keepdims=True)
        q_h = masked(head_of_row == h, qt_s[...])
        g_h = masked(head_of_row == h, gt_s[...])
        lse = lse_ref[pl.ds(h, 1)]
        for part, shift in ((near, lse), (far, jnp.where(flag, lse, masked_shift))):
            p = jnp.exp(dot(k_ref[part], q_h) - shift)
            p_s[part] = p.astype(BF)
            ds_s[part] = (p * (dot(v_ref[part], g_h) - row_dot)).astype(BF)
        dqt_s[hs] = dot(kt_s[hs], ds_s[...])
        dk_s[...] += dot(ds_s[...], masked(head_of_lane == h, q_ref[...]))
        dv_s[...] += dot(p_s[...], masked(head_of_lane == h, g_s[...]))
        return carry

    lax.fori_loop(0, cols // HD, head, 0)
    dqt = (dqt_s[...] * score_scale).astype(BF)
    dq = dqt.T
    d_s[near, 0:cols] = dq
    d_s[far, 0:cols] = jnp.zeros((rows, cols), BF)
    t_s[0:cols, near] = dqt
    b_s[...] = jnp.zeros(b_s.shape, F32)

    def grad_rows(rs):
        dk = dk_s[rs].astype(BF)
        dv = dv_s[rs].astype(BF)
        d_s[rs, cols : 2 * cols] = dk
        d_s[rs, 2 * cols : 3 * cols] = dv
        t_s[cols : 2 * cols, rs] = dk.T
        t_s[2 * cols : 3 * cols, rs] = dv.T
        b_s[1:2, 0:cols] += jnp.sum(dv.astype(F32), axis=0, keepdims=True)

    chunks(2 * rows, 256, grad_rows)
    t_s[3 * cols : 4 * cols, near] = ct_ref[...].astype(BF)
    b_s[0:1, 0:cols] = jnp.sum(dq.astype(F32), axis=0, keepdims=True)
    b_s[2:3] = bu_ref[...]
    b_s[8:16] = vec_ref[...]
    at = 2 * cols
    grad_ref[at : at + 16] = b_s[...].astype(BF)
    grad_ref[at + 16 : at + 64] = jnp.zeros((48, b_s.shape[1]), BF)
    other()
    send(d_s)
    arrive(own_ref)
    width = own_ref.shape[1]

    def weight_terms(cs):
        tok = own_ref[:, cs]
        grad_ref[0:cols, cs] = dot(t_s[0:cols, near], tok).astype(BF)
        terms = (
            dot(t_s[cols : 3 * cols, near], tok) + dot(t_s[cols : 3 * cols, far], other.buffer[:, cs])
        ).astype(BF)
        grad_ref[cols : 2 * cols, cs] = terms[0:cols]
        grad_ref[at + 64 : at + 64 + cols, cs] = terms[cols : 2 * cols]
        grad_ref[at + 64 + cols : at + 64 + 2 * cols, cs] = dot(
            t_s[3 * cols : 4 * cols, near], g_ref[:, cs]
        ).astype(BF)

    chunks(width, 256, weight_terms)
    send(grad_ref)


def attend_back_kernel(
    lens_ref, me_ref, core_ref, mid_ref,
    g_ref, wo_ref, q_ref, k_ref, lse_ref, v_ref, ct_ref, own_ref, bu_ref, vec_ref,
    grad_ref, d_ref, oth_s, oth_sem, b_s, *scratch,
):
    flag, use_core = neighbour(lens_ref, me_ref, own_ref.shape[0])
    attend_back_block(
        flag, g_ref, wo_ref, (ct_ref, lse_ref, q_ref, k_ref, v_ref), own_ref,
        lambda: Once(pick_other(use_core, core_ref, mid_ref, oth_s, oth_sem), oth_s),
        grad_ref, d_ref, b_s, bu_ref, vec_ref, scratch,
    )


def attend_back(lens, me, own, tok_core, tok_mid, g, block, bu, vecs, after=()):
    rows, width = own.shape
    a, (_, ct, lse, q, k, v) = block
    cols = q.shape[1]
    args = (lens, me, tok_core, tok_mid, g, a, q, k, lse, v, ct, own, bu, vecs)
    return call(
        attend_back_kernel, "attend_back",
        [shape((4 * cols + 64, width), BF), shape((2 * rows, 3 * cols), BF)],
        args, smem=2, raw=(2, 3), after=after, first=0, part={5: (3 * cols, cols)},
        scratch=[
            pltpu.VMEM((rows, width), BF), pltpu.SemaphoreType.DMA, pltpu.VMEM((16, width), F32),
            pltpu.VMEM((cols, rows), BF), pltpu.VMEM((cols, rows), BF),
            pltpu.VMEM((cols, 2 * rows), BF), pltpu.VMEM((cols, rows), F32),
            pltpu.VMEM((2 * rows, rows), BF), pltpu.VMEM((2 * rows, rows), BF),
            pltpu.VMEM((2 * rows, cols), F32), pltpu.VMEM((2 * rows, cols), F32),
            pltpu.VMEM((cols, rows), F32), pltpu.VMEM((rows, cols), BF),
            pltpu.VMEM((4 * cols, 2 * rows), BF),
        ],
    )


def other_grad_kernel(*refs):
    ds, weights, out_ref = refs[0:4], refs[4:8], refs[8]
    arrive(*ds, *weights)
    depth = ds[0].shape[1]

    def features_of(cs):
        total = dot(ds[0][...], weights[0][0:depth, cs])
        for d_ref, w_ref in zip(ds[1:], weights[1:]):
            total = total + dot(d_ref[...], w_ref[0:depth, cs])
        out_ref[:, cs] = total.astype(out_ref.dtype)

    chunks(out_ref.shape[1], 256, features_of)


def other_grad(ds, joints, rows, after=()):
    width = joints[0].shape[1]
    return call(
        other_grad_kernel, "other_grad", [shape((rows, width), BF)], (*ds, *joints), after=after,
        part={i: (rows, rows) for i in range(4)} | {i: (0, ds[0].shape[1]) for i in range(4, 8)},
    )[0]


def unit_of(residual):
    centre = jnp.mean(residual, axis=1, keepdims=True)
    spread = residual - centre
    inverse = lax.rsqrt(jnp.mean(spread * spread, axis=1, keepdims=True) + norm_eps)
    return spread * inverse, inverse


def norm_back(upstream, unit_rows, inverse, gain):
    unit_grad = upstream * gain
    return inverse * (
        unit_grad
        - jnp.mean(unit_grad, axis=1, keepdims=True)
        - unit_rows * jnp.mean(unit_grad * unit_rows, axis=1, keepdims=True)
    )


def up_down(low_ref, bias_ref, up_refs, down_ref, act_ref, slope_ref, sum_ref, start):
    up_ref = up_refs[0]
    arrive(low_ref, bias_ref, up_ref)

    def units_of(cs):
        pre = bias_ref[:, cs].astype(F32)[2:3] + dot(low_ref[...], up_ref[:, cs])
        phi = 0.5 + 0.5 * lax.erf(pre * half_root)
        act_ref[:, cs] = (pre * phi).astype(BF)
        slope_ref[:, cs] = (phi + pre * jnp.exp(-0.5 * pre * pre) * inv_root_two_pi).astype(BF)

    chunks(up_ref.shape[1], 256, units_of)
    send(act_ref)
    send(slope_ref)
    arrive(down_ref)

    def features_of(cs):
        part = dot(act_ref[...], down_ref[:, cs])
        sum_ref[:, cs] = part if start else sum_ref[:, cs] + part

    chunks(down_ref.shape[1], 256, features_of)


def ffn_back_block(
    g_ref, low_ref, act_ref, slope_ref, down_ref, up_refs, outs, sum_in_ref, sum_ref, pre_s
):
    down_grad_ref, up_grad_ref, bias_ref = outs
    up_ref = up_refs[0]
    arrive(g_ref, act_ref, slope_ref, down_ref)

    def units_of(cs):
        g = g_ref[...]
        down_grad_ref[cs] = contract_rows(act_ref[:, cs], g).astype(BF)
        pre = (contract_cols(g, down_ref[cs]) * slope_ref[:, cs].astype(F32)).astype(BF)
        pre_s[:, cs] = pre
        bias_ref[:, cs] = jnp.sum(pre.astype(F32), axis=0, keepdims=True)

    chunks(down_ref.shape[0], 256, units_of)
    send(down_grad_ref)
    arrive(low_ref, up_ref, sum_in_ref)

    def features_of(cs):
        pre = pre_s[...]
        up_grad_ref[cs] = contract_rows(low_ref[:, cs], pre).astype(BF)
        sum_ref[:, cs] = sum_in_ref[:, cs] + contract_cols(pre, up_ref[cs])

    chunks(up_ref.shape[0], 256, features_of)
    send(up_grad_ref)


def ffn_grad_outs(width, units):
    return [shape((units, width), BF), shape((width, units), BF), shape((1, units), F32)]


def ffn_far_kernel(
    low_ref, u2_ref, bias2_ref, d2_ref, u3_ref, bias3_ref, d3_ref,
    sum_in_ref, unit_ref, gain1_ref, shift1_ref, bd_ref, gain2_ref, shift2_ref, out_grad_ref,
    act2_ref, sl2_ref, out_ref, low_grad_ref, vec_ref,
    down_grad_ref, up_grad_ref, bu_ref, sum_ref,
    act3_s, sl3_s, pre_s, part_s,
):
    up_down(low_ref, bias2_ref, (u2_ref,), d2_ref, act2_ref, sl2_ref, part_s, True)
    up_down(low_ref, bias3_ref, (u3_ref,), d3_ref, act3_s, sl3_s, part_s, False)
    gain1, gain2, shift2 = row(gain1_ref), row(gain2_ref), row(shift2_ref)
    shift1 = row(shift1_ref) + row(bd_ref)
    arrive(unit_ref, sum_in_ref, out_grad_ref)
    vec_ref[...] = jnp.zeros(vec_ref.shape, F32)

    def rows_of(rs):
        resid = unit_ref[rs] * gain1 + shift1 + sum_in_ref[rs] + part_s[rs]
        unit, inverse = unit_of(resid)
        out_ref[rs] = (unit * gain2 + shift2).astype(BF)
        upstream = out_grad_ref[rs].astype(F32)
        vec_ref[0:1] += jnp.sum(upstream * unit, axis=0, keepdims=True)
        vec_ref[1:2] += jnp.sum(upstream, axis=0, keepdims=True)
        back = norm_back(upstream, unit, inverse, gain2)
        sum_ref[rs] = back
        g = back.astype(BF)
        low_grad_ref[rs] = g
        vec_ref[2:3] += jnp.sum(g.astype(F32), axis=0, keepdims=True)

    chunks(unit_ref.shape[0], 256, rows_of)
    send(out_ref)
    send(low_grad_ref)
    ffn_back_block(
        low_grad_ref, low_ref, act3_s, sl3_s, d3_ref, (u3_ref,),
        (down_grad_ref, up_grad_ref, bu_ref), sum_ref, sum_ref, pre_s,
    )


def ffn_far(
    low, joints, ups, downs, near, unit, gain1, shift1, b_down, gain2, shift2, out_grad, after=()
):
    rows, width = low.shape
    units = downs[0].shape[0]
    at = joints[0].shape[0] - 16
    piece = shape((rows, units), BF)
    return call(
        ffn_far_kernel, "ffn_far",
        [
            piece, piece, shape((rows, width), BF), shape((rows, width), BF), shape((8, width), F32),
            *ffn_grad_outs(width, units), shape((rows, width), F32),
        ],
        (
            low, ups[0], joints[0], downs[0], ups[1], joints[1], downs[1], near, unit,
            gain1, shift1, b_down, gain2, shift2, out_grad,
        ),
        part={2: (at, 16), 5: (at, 16)}, first=0, after=after,
        scratch=[pltpu.VMEM((rows, units), BF)] * 3 + [pltpu.VMEM((rows, width), F32)],
    )


def ffn_back_kernel(
    g_ref, act_ref, down_ref, slope_ref, low_ref, up_ref, sum_in_ref,
    down_grad_ref, up_grad_ref, bu_ref, sum_ref, pre_s,
):
    ffn_back_block(
        g_ref, low_ref, act_ref, slope_ref, down_ref, (up_ref,),
        (down_grad_ref, up_grad_ref, bu_ref), sum_in_ref, sum_ref, pre_s,
    )


def ffn_back(g, low, act, slope, up, down, acc, after=()):
    rows, width = low.shape
    units = down.shape[0]
    return call(
        ffn_back_kernel, "ffn_back",
        [*ffn_grad_outs(width, units), shape((rows, width), F32)],
        (g, act, down, slope, low, up, acc), after=after, first=0,
        scratch=[pltpu.VMEM((rows, units), BF)],
    )


def ffn_last_kernel(
    g_ref, act1_ref, d1_ref, sl1_ref, low_ref, u1_ref, act0_ref, d0_ref, sl0_ref, u0_ref, sum_in_ref,
    unit_ref, inv_ref, gain_ref, vec_in_ref, *refs,
):
    low_ref_out, resid_ref, vec_ref = refs[6:9]
    sum_s, pre_s = refs[9:]
    ffn_back_block(
        g_ref, low_ref, act1_ref, sl1_ref, d1_ref, (u1_ref,), refs[0:3], sum_in_ref, sum_s, pre_s
    )
    ffn_back_block(
        g_ref, low_ref, act0_ref, sl0_ref, d0_ref, (u0_ref,), refs[3:6], sum_s, sum_s, pre_s
    )
    gain = row(gain_ref)
    arrive(unit_ref, inv_ref)
    vec_ref[...] = vec_in_ref[...]

    def rows_of(rs):
        upstream = sum_s[rs]
        unit = unit_ref[rs]
        vec_ref[4:5] += jnp.sum(upstream * unit, axis=0, keepdims=True)
        vec_ref[5:6] += jnp.sum(upstream, axis=0, keepdims=True)
        back = norm_back(upstream, unit, inv_ref[rs], gain)
        resid_ref[rs] = back
        low = back.astype(BF)
        low_ref_out[rs] = low
        vec_ref[6:7] += jnp.sum(low.astype(F32), axis=0, keepdims=True)

    chunks(unit_ref.shape[0], 256, rows_of)
    send(resid_ref)
    send(low_ref_out)


def ffn_last(g, low, acts, slopes, ups, downs, acc, unit, inverse, gain, vecs, after=()):
    rows, width = low.shape
    units = downs[0].shape[0]
    return call(
        ffn_last_kernel, "ffn_last",
        [
            *ffn_grad_outs(width, units), *ffn_grad_outs(width, units),
            shape((rows, width), BF), shape((rows, width), F32), shape((8, width), F32),
        ],
        (
            g, acts[1], downs[1], slopes[1], low, ups[1], acts[0], downs[0], slopes[0], ups[0], acc,
            unit, inverse, gain, vecs,
        ),
        after=after, first=0,
        scratch=[pltpu.VMEM((rows, width), F32), pltpu.VMEM((rows, units), BF)],
    )


def spread_small_kernel(in_ref, bq_ref, bv_ref, bu_ref, *rest):
    sums = in_ref[...]
    cols = bq_ref.shape[0]
    bq_ref[...] = sums[0:1, 0:cols].reshape(cols)
    bv_ref[...] = sums[1:2, 0:cols].reshape(cols)
    bu_ref[...] = sums[2:3].reshape(-1)
    for at, ref in zip((8, 9, 10, 12, 13, 14), rest):
        ref[...] = sums[at : at + 1].reshape(-1)


def spread_small(sums, cols, units):
    width = sums.shape[1]
    return call(
        spread_small_kernel, "spread_small",
        [shape((cols,), F32), shape((cols,), F32), shape((units,), F32)] + [shape((width,), F32)] * 6,
        (sums,), part={0: (2 * cols, 16)},
    )


def swap(a, axis, distance):
    size = lax.axis_size(axis)
    return lax.ppermute(a, axis, [(i, i ^ distance) for i in range(size)])


def to_core(a):
    return swap(a, "narrow", 1)


def to_chip(a):
    return swap(a, "narrow", 2)


def to_middle(a):
    return lax.ppermute(a, "narrow", [(1, 2), (2, 1)])


def wide_bits():
    size = lax.axis_size("wide")
    bits = []
    while size > 1:
        assert size % 2 == 0
        bits.append(len(bits))
        size //= 2
    return bits


def part_of(a, which, parts):
    rows = a.shape[0] // parts
    return lax.dynamic_slice_in_dim(a, which * rows, rows, 0)


def in_order(side, mine, got):
    return jnp.where(side == 0, jnp.concatenate([mine, got]), jnp.concatenate([got, mine]))


def hold(a, *others):
    return lax.optimization_barrier((a, *others))[0]


def add_low(*terms):
    total = terms[0].astype(F32)
    for term in terms[1:]:
        total = total + term.astype(F32)
    return total.astype(BF)


def side_of(bit):
    return (lax.axis_index("wide") >> bit) & 1


def own_piece(a):
    at = 0
    for bit in wide_bits():
        at = 2 * at + side_of(bit)
    return part_of(a, at, lax.axis_size("wide"))


class WideSum:
    def __init__(self, a):
        self.a = a
        self.step = 0
        self.send()

    def send(self):
        bit = self.step
        if bit < 3:
            side = side_of(bit)
            self.keep = part_of(self.a, side, 2)
            self.sent = part_of(self.a, 1 - side, 2)
        else:
            self.keep = self.sent = self.a
        self.got = swap(self.sent, "wide", 1 << bit)

    def advance(self, *waits):
        got = hold(self.got, *waits) if waits else self.got
        self.a = add_low(self.keep, got)
        self.step += 1
        if self.step < len(wide_bits()):
            self.send()

    def piece(self, *waits):
        while self.step < len(wide_bits()):
            self.advance(*waits)
            waits = ()
        return self.a


class WideGather:
    def __init__(self, a, bits=(2, 1, 0)):
        self.a = self.sent = a
        self.bits = bits
        self.step = 0
        self.send()

    def send(self):
        self.sent = self.a
        self.got = swap(self.a, "wide", 1 << self.bits[self.step])

    def advance(self, *waits):
        got = hold(self.got, *waits) if waits else self.got
        self.a = in_order(side_of(self.bits[self.step]), self.a, got)
        self.step += 1
        if self.step < len(self.bits):
            self.send()

    def whole(self, *waits):
        while self.step < len(self.bits):
            self.advance(*waits)
            waits = ()
        return self.a


def local(
    tokens, item_lengths, w_query, b_query, w_key, w_value, b_value, w_out, b_out,
    gain_attn, shift_attn, w_up, b_up, w_down, b_down, gain_ffn, shift_ffn, out_grad,
):
    rows, width = tokens.shape
    cols = w_query.shape[1]
    units = w_up.shape[1]
    assert lax.axis_size("narrow") == 4
    me = lax.axis_index("narrow").reshape(1)

    tok_mid = to_middle(tokens)
    tok_core = to_core(tokens)
    pieces = to_chip(own_piece(w_down))
    joint = pack_joint(w_query, w_key, w_value, w_out, b_query, b_value, b_up)
    joint_core = to_core(joint)
    joint_chip = to_chip(hold(joint, pieces, tok_mid))
    down_gather = WideGather(pieces, wide_bits()[::-1])
    while down_gather.step < len(down_gather.bits) - 2:
        down_gather.advance(joint_core)
    near0, near1 = attend_pair(
        "attend_near", item_lengths, me, tokens, tok_core, tok_mid, [joint, joint_core],
        (down_gather.sent,),
    )
    down_gather.advance(near1[2])
    gate = down_gather.sent
    joint_chip = hold(joint_chip, gate)
    joint_diag = to_core(joint_chip)
    up_chip = to_chip(hold(w_up, joint_chip))
    up_core = to_core(hold(w_up, joint_chip))
    down_core = to_core(hold(w_down, joint_chip))
    far2, far3 = attend_pair(
        "attend_far", item_lengths, me, tokens, tok_core, tok_mid, [joint_chip, joint_diag], (gate,)
    )
    joints = [joint, joint_core, joint_chip, joint_diag]
    saved = [near0, near1, far2, far3]
    unit_one, inv_one, low, act0, sl0, act1, sl1, near_sum = norm_near(
        tokens, [s[0] for s in saved], joints, b_out, gain_attn, shift_attn,
        [w_up, up_core], [w_down, down_core],
    )
    down_chip = down_gather.whole(inv_one)
    down_diag = to_core(down_chip)
    up_chip = hold(up_chip, down_chip)
    up_diag = to_core(up_chip)
    act2, sl2, layer_out, ffn_grad, vecs, down_d, up_d, bu_d, acc = ffn_far(
        low, joints[2:], [up_chip, up_diag], [down_chip, down_diag],
        near_sum, unit_one, gain_attn, shift_attn, b_down, gain_ffn, shift_ffn, out_grad,
    )

    up_from_core = to_core(up_d)
    down_from_core = to_core(down_d)
    down_x, up_x, bu_x, acc = ffn_back(ffn_grad, low, act2, sl2, up_chip, down_chip, acc)
    up_far = add_low(up_x, hold(up_from_core, bu_x))
    up_sum = to_chip(up_far)
    down_far = add_low(down_x, hold(down_from_core, up_far))
    down_sum = to_chip(down_far)
    down_c, up_c, bu_c, down_o, up_o, bu_o, attn_grad, resid_one, vecs = ffn_last(
        ffn_grad, low, (act0, act1), (sl0, sl1), (w_up, up_core), (w_down, down_core), acc,
        unit_one, inv_one, gain_attn, vecs, (up_far, down_far),
    )
    up_back = to_core(up_c)
    down_back = to_core(down_c)
    grads, parts = [None] * 4, [None] * 4
    bus = (bu_o, bu_c, bu_x, bu_d)

    def back_attend(r, *after):
        grads[r], parts[r] = attend_back(
            item_lengths, me, tokens, tok_core, tok_mid, attn_grad, (joints[r], saved[r]),
            bus[r], vecs, after,
        )
        return grads[r]

    mark = back_attend(3)
    up_sum = hold(up_sum, mark)
    near_up = WideSum(add_low(up_o, hold(up_back, up_sum), up_sum))
    down_near = add_low(down_o, hold(down_back, near_up.sent))
    joint_from_core = to_core(hold(grads[3], down_near))
    mark = back_attend(2, near_up.sent, down_near)
    down_sum = hold(down_sum, mark)
    near_down = WideSum(add_low(down_near, down_sum))
    joint_far = add_low(grads[2], hold(joint_from_core, near_down.a))
    joint_sum = to_chip(joint_far)
    near_up.advance(joint_far)
    mark = back_attend(1, joint_far, near_up.sent, near_down.sent)
    near_up.advance(mark)
    near_down.advance(near_up.sent)
    joint_back = to_core(hold(grads[1], near_down.sent))
    mark = back_attend(0, near_up.sent, near_down.sent)
    joint_sum = hold(joint_sum, mark)
    joint_back = hold(joint_back, joint_sum)

    def rows_of(a, part):
        return a[: 2 * cols + 64] if part == 0 else a[2 * cols + 64 :]

    def joint_part(i, own, got):
        return WideSum(add_low(rows_of(own, i), rows_of(got, i), rows_of(joint_back, i)))

    first = joint_part(0, grads[0], joint_sum)
    second = joint_part(1, grads[0], hold(joint_sum, first.sent))
    up_gather = WideGather(near_up.piece(second.sent))
    near_down.advance(up_gather.sent)
    first.advance(near_down.sent)
    down_gather = WideGather(near_down.piece(first.sent))
    up_gather.advance(down_gather.sent)
    second.advance(up_gather.sent)
    oth_low = other_grad(parts, joints, rows, (second.sent,))
    first.advance(oth_low)
    up_gather.advance(first.sent)
    down_gather.advance(up_gather.sent)
    oth_core, oth_mid = to_core(hold(oth_low, down_gather.sent)), to_middle(hold(oth_low, down_gather.sent))
    second.advance(down_gather.sent)
    first = WideGather(first.piece(second.sent))
    down_gather.advance(first.sent)
    second = WideGather(second.piece(down_gather.sent))
    first.advance(second.sent)
    token_grad = take_back(
        item_lengths, me, hold(oth_core, first.sent), hold(oth_mid, first.sent), resid_one,
        parts, joints, (first.sent, second.sent),
    )
    second.advance(token_grad)
    first.advance(second.sent)
    w_up_grad = up_gather.whole(first.sent).astype(F32)
    second.advance(w_up_grad)
    w_down_grad = down_gather.whole(second.sent).astype(F32)
    qk_grad = first.whole(w_down_grad).astype(F32)
    bq, bv, bu, gain_ffn_g, shift_ffn_g, b_down_g, gain_attn_g, shift_attn_g, b_out_g = spread_small(
        qk_grad, cols, units
    )
    vo_grad = second.whole(qk_grad).astype(F32)
    joint_grads = [qk_grad[:cols], qk_grad[cols : 2 * cols], vo_grad[:cols]]
    w_out_grad = vo_grad[cols:]
    return (
        layer_out,
        token_grad,
        joint_grads[0].T,
        bq,
        joint_grads[1].T,
        joint_grads[2].T,
        bv,
        w_out_grad,
        b_out_g,
        gain_attn_g,
        shift_attn_g,
        w_up_grad,
        bu,
        w_down_grad,
        b_down_g,
        gain_ffn_g,
        shift_ffn_g,
    )


def take_back_kernel(lens_ref, me_ref, core_ref, mid_ref, *refs):
    ds, weights, resid_ref, out_ref, oth_s, oth_sem = refs[0:4], refs[4:8], *refs[8:]
    flag, use_core = neighbour(lens_ref, me_ref, resid_ref.shape[0])
    other = pick_other(use_core, core_ref, mid_ref, oth_s, oth_sem)
    arrive(*ds, *weights, resid_ref)
    other.wait()
    depth = ds[0].shape[1]

    def features_of(cs):
        total = resid_ref[:, cs] + jnp.where(flag, oth_s[:, cs].astype(F32), 0.0)
        for d_ref, w_ref in zip(ds, weights):
            total = total + dot(d_ref[...], w_ref[0:depth, cs])
        out_ref[:, cs] = total

    chunks(out_ref.shape[1], 256, features_of)


def take_back(lens, me, core, mid, resid, ds, joints, after):
    rows, width = resid.shape
    depth = ds[0].shape[1]
    return call(
        take_back_kernel, "take_back", [shape((rows, width), F32)],
        (lens, me, core, mid, *ds, *joints, resid), smem=2, raw=(2, 3), after=after,
        part={i: (0, rows) for i in range(4, 8)} | {i: (0, depth) for i in range(8, 12)},
        scratch=[pltpu.VMEM(core.shape, BF), pltpu.SemaphoreType.DMA],
    )[0]


def solution(mesh):
    rows_spec = P(("wide", "narrow"), None)
    col_spec = P(None, "narrow")
    vec_spec = P("narrow")
    row_spec = P("narrow", None)
    full = P()
    return jax.shard_map(
        local,
        mesh=mesh,
        in_specs=(
            rows_spec, P("wide"), col_spec, vec_spec, col_spec, col_spec, vec_spec, row_spec, full,
            full, full, col_spec, vec_spec, row_spec, full, full, full, rows_spec,
        ),
        out_specs=(
            rows_spec, rows_spec, col_spec, vec_spec, col_spec, col_spec, vec_spec, row_spec, full,
            full, full, col_spec, vec_spec, row_spec, full, full, full,
        ),
        check_vma=False,
    )
```

```python
import functools

import jax
import jax.numpy as jnp
from jax import lax
from jax.experimental import pallas as pl
from jax.experimental.pallas import tpu as pltpu
from jax.sharding import PartitionSpec as P

HD = 64
F32 = jnp.float32
BF = jnp.bfloat16
MIB = 1 << 20

norm_eps = 1e-12
masked_shift = 1e30
half_root = 0.7071067811865476
inv_root_two_pi = 0.3989422804014327
score_scale = HD**-0.5

VM = pl.BlockSpec(memory_space=pltpu.VMEM)
SM = pl.BlockSpec(memory_space=pltpu.SMEM)
ANY = pl.BlockSpec(memory_space=pl.ANY)


def dot(left, right):
    return jnp.dot(left, right, preferred_element_type=F32)


def contract_rows(left, right):
    return lax.dot_general(left, right, (((0,), (0,)), ((), ())), preferred_element_type=F32)


def contract_cols(left, right):
    return lax.dot_general(left, right, (((1,), (1,)), ((), ())), preferred_element_type=F32)


def shape(dims, dtype):
    return jax.ShapeDtypeStruct(dims, dtype)


def row(ref):
    return ref[...].astype(F32).reshape(1, -1)


class Arriving:
    def __init__(self, source, buffer, sem):
        self.buffer = buffer
        self.shape = buffer.shape
        self.dtype = buffer.dtype
        self.copy = pltpu.make_async_copy(source, buffer, sem)
        self.started = False
        self.waiting = True
        self.then = []

    def start(self):
        if not self.started:
            self.copy.start()
            self.started = True

    def wait(self):
        self.start()
        if self.waiting:
            self.copy.wait()
            self.waiting = False
            for other in self.then:
                other.start()

    def __getitem__(self, index):
        self.wait()
        return self.buffer[index]


class Leaving:
    def __init__(self, target, buffer, sem):
        self.buffer = buffer
        self.shape = buffer.shape
        self.dtype = buffer.dtype
        self.copy = pltpu.make_async_copy(buffer, target, sem)
        self.sent = False

    def __getitem__(self, index):
        return self.buffer[index]

    def __setitem__(self, index, value):
        self.buffer[index] = value

    def send(self):
        if not self.sent:
            self.copy.start()
            self.sent = True


def call(
    kernel, name, out_shape, args, smem=0, scratch=(), vmem=60, after=(), raw=(), part=(), first=0,
    stay=(), stay_out=(),
):
    count = len(args)
    outs = len(out_shape)
    loaded = [i for i in range(smem, count) if i not in raw and i not in stay]
    leaving_out = [n for n in range(outs) if n not in stay_out]
    part = dict(part)

    def held(i):
        dims = (part[i][1], *args[i].shape[1:]) if i in part else args[i].shape
        return pltpu.VMEM(dims, args[i].dtype)

    buffers = [held(i) for i in loaded]
    buffers += [pltpu.VMEM(out_shape[n].shape, out_shape[n].dtype) for n in leaving_out]

    def body(*refs):
        given = list(refs[:count])
        refs = refs[count + len(after) :]
        results, refs = list(refs[:outs]), refs[outs:]
        own, refs = refs[: len(buffers)], refs[len(buffers) :]
        in_sems, out_sems, refs = refs[0], refs[1], refs[2:]
        for n, i in enumerate(loaded):
            source = given[i].at[pl.ds(*part[i])] if i in part else given[i]
            given[i] = Arriving(source, own[n], in_sems.at[n])
        late = [given[i] for i in loaded if first and i >= first]
        for i in loaded:
            if given[i] not in late:
                given[i].start()
                given[i].then = late
        for m, n in enumerate(leaving_out):
            results[n] = Leaving(results[n], own[len(loaded) + m], out_sems.at[m])
        kernel(*given, *results, *refs)
        for i in loaded:
            given[i].wait()
        for n in leaving_out:
            results[n].send()
        for n in leaving_out:
            results[n].copy.wait()

    in_specs = [SM] * smem + [VM if i in stay else ANY for i in range(smem, count)]
    return pl.pallas_call(
        body,
        out_shape=tuple(out_shape),
        in_specs=in_specs + [ANY] * len(after),
        out_specs=tuple(VM if n in stay_out else ANY for n in range(outs)),
        scratch_shapes=[
            *buffers, pltpu.SemaphoreType.DMA((max(len(loaded), 1),)),
            pltpu.SemaphoreType.DMA((max(len(leaving_out), 1),)), *scratch,
        ],
        compiler_params=pltpu.CompilerParams(vmem_limit_bytes=vmem * MIB),
        cost_estimate=pl.CostEstimate(flops=1000, transcendentals=0, bytes_accessed=1000),
        name=name,
    )(*args, *after)


def send(ref):
    if isinstance(ref, Leaving):
        ref.send()


def arrive(*refs):
    for ref in refs:
        if isinstance(ref, Arriving):
            ref.wait()


def chunks(extent, size, body):
    def step(i, carry):
        body(pl.ds(pl.multiple_of(i * size, size), size))
        return carry

    lax.fori_loop(0, extent // size, step, 0)


def masked(picked, a):
    return jnp.where(picked, a.astype(F32), 0.0).astype(BF)


def joint_kernel(wq_ref, wk_ref, wv_ref, wo_ref, bq_ref, bv_ref, bu_ref, out_ref, tail_s):
    cols = wq_ref.shape[0]
    for i, ref in enumerate((wq_ref, wk_ref, wv_ref, wo_ref)):
        out_ref[i * cols : (i + 1) * cols] = ref[...]
    tail_s[...] = jnp.zeros_like(tail_s)
    tail_s[0:1, 0:cols] = row(bq_ref)
    tail_s[1:2, 0:cols] = row(bv_ref)
    tail_s[2:3, :] = row(bu_ref)
    out_ref[4 * cols : 4 * cols + 16] = tail_s[...].astype(BF)


def pack_joint(w_query, w_key, w_value, w_out, b_query, b_value, b_up):
    width, cols = w_query.shape
    return call(
        joint_kernel, "pack_joint", [shape((4 * cols + 16, width), BF)],
        (w_query.T, w_key.T, w_value.T, w_out, b_query, b_value, b_up),
        scratch=[pltpu.VMEM((16, width), F32)],
    )[0]


def neighbour(lens_ref, me_ref, rows):
    me = me_ref[0]
    here = me * rows
    first = jnp.int32(0)
    start = jnp.int32(0)
    length = jnp.int32(0)
    for j in range(lens_ref.shape[0]):
        n = lens_ref[j]
        inside = (first <= here) & (here < first + n)
        start = jnp.where(inside, first, start)
        length = jnp.where(inside, n, length)
        first = first + n
    other = jnp.where(start == here, me + 1, me - 1)
    return length > rows, other == (me ^ 1)


def pick_other(use_core, core_ref, mid_ref, buffer, sem):
    from_core = pltpu.make_async_copy(core_ref, buffer, sem)
    from_mid = pltpu.make_async_copy(mid_ref, buffer, sem)

    @pl.when(use_core)
    def _():
        from_core.start()

    @pl.when(jnp.logical_not(use_core))
    def _():
        from_mid.start()

    return from_core


def attend_block(flag, own_ref, oth_s, a_ref, outs, scratch):
    ctx_ref, ct_ref, lse_ref, q_ref, k_ref, v_ref = outs
    qt_s, vt_s = scratch
    rows, cols = q_ref.shape
    tail = a_ref[4 * cols : 4 * cols + 16].astype(F32)
    wk = a_ref[cols : 2 * cols]
    wv = a_ref[2 * cols : 3 * cols]
    near = slice(0, rows)
    far = slice(rows, 2 * rows)
    q = (contract_cols(own_ref[...], a_ref[0:cols]) + tail[0:1, 0:cols]).astype(BF)
    q = q * jnp.asarray(score_scale, BF)
    q_ref[...] = q
    qt_s[...] = q.T
    for part, tok_ref in ((near, own_ref), (far, oth_s)):
        k_ref[part] = contract_cols(tok_ref[...], wk).astype(BF)
        v = (contract_cols(tok_ref[...], wv) + tail[1:2, 0:cols]).astype(BF)
        v_ref[part] = v
        vt_s[:, part] = v.T
    head_of_row = lax.broadcasted_iota(jnp.int32, (cols, 1), 0) // HD

    def head(h, carry):
        hs = pl.ds(pl.multiple_of(h * HD, HD), HD)
        q_h = masked(head_of_row == h, qt_s[...])
        s_own = dot(k_ref[near], q_h)
        s_other = dot(k_ref[far], q_h)
        top_own = jnp.max(s_own, axis=0, keepdims=True)
        top_other = jnp.max(s_other, axis=0, keepdims=True)
        top = jnp.where(flag, jnp.maximum(top_own, top_other), top_own)
        p_own = jnp.exp(s_own - top)
        p_other = jnp.exp(s_other - jnp.where(flag, top, masked_shift))
        total = jnp.sum(p_own, axis=0, keepdims=True) + jnp.sum(p_other, axis=0, keepdims=True)
        c = dot(vt_s[hs, near], p_own.astype(BF)) + dot(vt_s[hs, far], p_other.astype(BF))
        ct_ref[hs] = c * (1.0 / total)
        lse_ref[pl.ds(h, 1)] = top + jnp.log(total)
        return carry

    lax.fori_loop(0, cols // HD, head, 0)
    ctx_ref[...] = ct_ref[...].T.astype(BF)


def block_outs(rows, cols):
    return [
        shape((rows, cols), BF), shape((cols, rows), F32), shape((cols // HD, rows), F32),
        shape((rows, cols), BF), shape((2 * rows, cols), BF), shape((2 * rows, cols), BF),
    ]


def attend_scratch(rows, width, cols):
    return [
        pltpu.VMEM((rows, width), BF), pltpu.SemaphoreType.DMA,
        pltpu.VMEM((cols, rows), BF), pltpu.VMEM((cols, 2 * rows), BF),
    ]


class Once:
    def __init__(self, copy, buffer):
        self.copy = copy
        self.buffer = buffer

    def __call__(self):
        if self.copy is not None:
            self.copy.wait()
            self.copy = None
        return self.buffer[...]


def attend_pair_kernel(
    lens_ref, me_ref, core_ref, mid_ref, own_ref, a0_ref, a1_ref, *refs, after
):
    targets = refs[after : after + 12]
    own_s, a_s, *held = refs[after + 12 : after + 20]
    own_sem, a_sem, out_sem, oth_s, oth_sem, qt_s, vt_s = refs[after + 20 :]
    own_copy = pltpu.make_async_copy(own_ref, own_s, own_sem)
    own_copy.start()
    weights = [
        pltpu.make_async_copy(ref, a_s.at[i], a_sem.at[i]) for i, ref in enumerate((a0_ref, a1_ref))
    ]
    weights[0].start()
    flag, use_core = neighbour(lens_ref, me_ref, own_ref.shape[0])
    other = pick_other(use_core, core_ref, mid_ref, oth_s, oth_sem)
    leaving = [
        [
            pltpu.make_async_copy(buffer.at[i], targets[6 * i + n], out_sem.at[i, n])
            for n, buffer in enumerate(held)
        ]
        for i in range(2)
    ]
    own_copy.wait()

    def block(i, carry):
        @pl.when(i == 0)
        def _():
            weights[0].wait()
            other.wait()
            weights[1].start()

        @pl.when(i == 1)
        def _():
            weights[1].wait()

        attend_block(
            flag, own_s, oth_s, a_s.at[i], [buffer.at[i] for buffer in held], (qt_s, vt_s)
        )
        for n in range(2):

            @pl.when(i == n)
            def _():
                for copy in leaving[n]:
                    copy.start()

        return carry

    lax.fori_loop(0, 2, block, 0)
    for copies in leaving:
        for copy in copies:
            copy.wait()


def attend_pair(name, lens, me, own, tok_core, tok_mid, blocks, after=()):
    rows, width = own.shape
    cols = (blocks[0].shape[0] - 16) // 4
    outs = block_outs(rows, cols)
    got = pl.pallas_call(
        functools.partial(attend_pair_kernel, after=len(after)),
        out_shape=tuple(outs * 2),
        in_specs=[SM, SM] + [ANY] * (5 + len(after)),
        out_specs=tuple([ANY] * 12),
        scratch_shapes=[
            pltpu.VMEM(own.shape, BF), pltpu.VMEM((2, *blocks[0].shape), BF),
            *[pltpu.VMEM((2, *o.shape), o.dtype) for o in outs],
            pltpu.SemaphoreType.DMA, pltpu.SemaphoreType.DMA((2,)), pltpu.SemaphoreType.DMA((2, 6)),
            *attend_scratch(rows, width, cols),
        ],
        compiler_params=pltpu.CompilerParams(vmem_limit_bytes=60 * MIB),
        cost_estimate=pl.CostEstimate(flops=1000, transcendentals=0, bytes_accessed=1000),
        name=name,
    )(lens, me, tok_core, tok_mid, own, *blocks, *after)
    return got[:6], got[6:]


def norm_near_kernel(
    own_ref, c0_ref, w0_ref, c1_ref, w1_ref, c2_ref, w2_ref, c3_ref, w3_ref, bo_ref, gain_ref, shift_ref,
    u0_ref, bias0_ref, d0_ref, u1_ref, bias1_ref, d1_ref,
    unit_ref, inv_ref, low_ref, act0_ref, sl0_ref, act1_ref, sl1_ref, sum_ref,
):
    pairs = ((c0_ref, w0_ref), (c1_ref, w1_ref), (c2_ref, w2_ref), (c3_ref, w3_ref))
    vectors = row(bo_ref), row(gain_ref), row(shift_ref)
    for pair in pairs:
        arrive(*pair)
    arrive(own_ref)

    def rows_of(rs):
        resid = own_ref[rs].astype(F32) + vectors[0]
        for c_ref, w_ref in pairs:
            resid = resid + dot(c_ref[rs], w_ref[...])
        unit, inverse = unit_of(resid)
        unit_ref[rs] = unit
        inv_ref[rs] = inverse
        low_ref[rs] = (unit * vectors[1] + vectors[2]).astype(BF)

    chunks(own_ref.shape[0], 256, rows_of)
    send(unit_ref)
    send(inv_ref)
    send(low_ref)
    up_down(low_ref, bias0_ref, (u0_ref,), d0_ref, act0_ref, sl0_ref, sum_ref, True)
    up_down(low_ref, bias1_ref, (u1_ref,), d1_ref, act1_ref, sl1_ref, sum_ref, False)


def norm_near(own, ctxs, joints, b_out, gain, shift, ups, downs, after=()):
    rows, width = own.shape
    units = downs[0].shape[0]
    at = joints[0].shape[0] - 16
    piece = shape((rows, units), BF)
    cols = ctxs[0].shape[1]
    terms = [x for pair in zip(ctxs, joints) for x in pair]
    return call(
        norm_near_kernel, "norm_near",
        [
            shape((rows, width), F32), shape((rows, 1), F32), shape((rows, width), BF),
            piece, piece, piece, piece, shape((rows, width), F32),
        ],
        (
            own, *terms, b_out, gain, shift,
            ups[0], joints[0], downs[0], ups[1], joints[1], downs[1],
        ),
        part={2 * i + 2: (3 * cols, cols) for i in range(4)} | {13: (at, 16), 16: (at, 16)},
        after=after, first=0,
    )


def attend_back_block(
    flag, g_ref, wo_ref, saved, own_ref, other, grad_ref, sums, b_s, bu_ref, vec_ref, scratch
):
    ct_ref, lse_ref, q_ref, k_ref, v_ref = saved
    d_s = sums
    gt_s, qt_s, kt_s, dqt_s, p_s, ds_s, dk_s, dv_s, dot_s, g_s, t_s = scratch
    rows, cols = q_ref.shape
    near = slice(0, rows)
    far = slice(rows, 2 * rows)
    arrive(g_ref, wo_ref)
    other = other()
    arrive(q_ref)

    def query_rows(rs):
        g = contract_cols(g_ref[rs], wo_ref[...]).astype(BF)
        g_s[rs] = g
        gt_s[:, rs] = g.T
        qt_s[:, rs] = q_ref[rs].T

    chunks(rows, 256, query_rows)
    arrive(k_ref)

    def key_rows(rs):
        kt_s[:, rs] = k_ref[rs].T

    chunks(2 * rows, 256, key_rows)
    dot_s[...] = gt_s[...].astype(F32) * ct_ref[...]
    dk_s[...] = jnp.zeros(dk_s.shape, F32)
    dv_s[...] = jnp.zeros(dv_s.shape, F32)
    head_of_row = lax.broadcasted_iota(jnp.int32, (cols, 1), 0) // HD
    head_of_lane = lax.broadcasted_iota(jnp.int32, (1, cols), 1) // HD
    arrive(q_ref, k_ref, v_ref, lse_ref)

    def head(h, carry):
        hs = pl.ds(pl.multiple_of(h * HD, HD), HD)
        row_dot = jnp.sum(dot_s[hs], axis=0, keepdims=True)
        q_h = masked(head_of_row == h, qt_s[...])
        g_h = masked(head_of_row == h, gt_s[...])
        lse = lse_ref[pl.ds(h, 1)]
        for part, shift in ((near, lse), (far, jnp.where(flag, lse, masked_shift))):
            p = jnp.exp(dot(k_ref[part], q_h) - shift)
            p_s[part] = p.astype(BF)
            ds_s[part] = (p * (dot(v_ref[part], g_h) - row_dot)).astype(BF)
        dqt_s[hs] = dot(kt_s[hs], ds_s[...])
        dk_s[...] += dot(ds_s[...], masked(head_of_lane == h, q_ref[...]))
        dv_s[...] += dot(p_s[...], masked(head_of_lane == h, g_s[...]))
        return carry

    lax.fori_loop(0, cols // HD, head, 0)
    dqt = (dqt_s[...] * score_scale).astype(BF)
    dq = dqt.T
    d_s[near, 0:cols] = dq
    d_s[far, 0:cols] = jnp.zeros((rows, cols), BF)
    t_s[0:cols, near] = dqt
    b_s[...] = jnp.zeros(b_s.shape, F32)

    def grad_rows(rs):
        dk = dk_s[rs].astype(BF)
        dv = dv_s[rs].astype(BF)
        d_s[rs, cols : 2 * cols] = dk
        d_s[rs, 2 * cols : 3 * cols] = dv
        t_s[cols : 2 * cols, rs] = dk.T
        t_s[2 * cols : 3 * cols, rs] = dv.T
        b_s[1:2, 0:cols] += jnp.sum(dv.astype(F32), axis=0, keepdims=True)

    chunks(2 * rows, 256, grad_rows)
    t_s[3 * cols : 4 * cols, near] = ct_ref[...].astype(BF)
    b_s[0:1, 0:cols] = jnp.sum(dq.astype(F32), axis=0, keepdims=True)
    b_s[2:3] = bu_ref[...]
    b_s[8:16] = vec_ref[...]
    at = 2 * cols
    grad_ref[at : at + 16] = b_s[...].astype(BF)
    grad_ref[at + 16 : at + 32] = jnp.zeros((16, b_s.shape[1]), BF)
    other()
    send(d_s)
    arrive(own_ref)
    width = own_ref.shape[1]

    def weight_terms(cs):
        tok = own_ref[:, cs]
        grad_ref[0:cols, cs] = dot(t_s[0:cols, near], tok).astype(BF)
        terms = (
            dot(t_s[cols : 3 * cols, near], tok) + dot(t_s[cols : 3 * cols, far], other.buffer[:, cs])
        ).astype(BF)
        grad_ref[cols : 2 * cols, cs] = terms[0:cols]
        grad_ref[at + 32 : at + 32 + cols, cs] = terms[cols : 2 * cols]
        grad_ref[at + 32 + cols : at + 32 + 2 * cols, cs] = dot(
            t_s[3 * cols : 4 * cols, near], g_ref[:, cs]
        ).astype(BF)

    chunks(width, 256, weight_terms)
    send(grad_ref)


def attend_back_kernel(
    lens_ref, me_ref, core_ref, mid_ref,
    g_ref, wo_ref, q_ref, k_ref, lse_ref, v_ref, ct_ref, own_ref, bu_ref, vec_ref,
    grad_ref, d_ref, oth_s, oth_sem, b_s, *scratch,
):
    flag, use_core = neighbour(lens_ref, me_ref, own_ref.shape[0])
    attend_back_block(
        flag, g_ref, wo_ref, (ct_ref, lse_ref, q_ref, k_ref, v_ref), own_ref,
        lambda: Once(pick_other(use_core, core_ref, mid_ref, oth_s, oth_sem), oth_s),
        grad_ref, d_ref, b_s, bu_ref, vec_ref, scratch,
    )


def attend_back(lens, me, own, tok_core, tok_mid, g, block, bu, vecs, after=()):
    rows, width = own.shape
    a, (_, ct, lse, q, k, v) = block
    cols = q.shape[1]
    args = (lens, me, tok_core, tok_mid, g, a, q, k, lse, v, ct, own, bu, vecs)
    return call(
        attend_back_kernel, "attend_back",
        [shape((4 * cols + 32, width), BF), shape((2 * rows, 3 * cols), BF)],
        args, smem=2, raw=(2, 3), after=after, first=0, part={5: (3 * cols, cols)},
        scratch=[
            pltpu.VMEM((rows, width), BF), pltpu.SemaphoreType.DMA, pltpu.VMEM((16, width), F32),
            pltpu.VMEM((cols, rows), BF), pltpu.VMEM((cols, rows), BF),
            pltpu.VMEM((cols, 2 * rows), BF), pltpu.VMEM((cols, rows), F32),
            pltpu.VMEM((2 * rows, rows), BF), pltpu.VMEM((2 * rows, rows), BF),
            pltpu.VMEM((2 * rows, cols), F32), pltpu.VMEM((2 * rows, cols), F32),
            pltpu.VMEM((cols, rows), F32), pltpu.VMEM((rows, cols), BF),
            pltpu.VMEM((4 * cols, 2 * rows), BF),
        ],
    )


def other_grad_kernel(*refs):
    ds, weights, out_ref = refs[0:4], refs[4:8], refs[8]
    arrive(*ds, *weights)
    depth = ds[0].shape[1]

    def features_of(cs):
        total = dot(ds[0][...], weights[0][0:depth, cs])
        for d_ref, w_ref in zip(ds[1:], weights[1:]):
            total = total + dot(d_ref[...], w_ref[0:depth, cs])
        out_ref[:, cs] = total.astype(out_ref.dtype)

    chunks(out_ref.shape[1], 256, features_of)


def other_grad(ds, joints, rows, after=()):
    width = joints[0].shape[1]
    return call(
        other_grad_kernel, "other_grad", [shape((rows, width), BF)], (*ds, *joints), after=after,
        part={i: (rows, rows) for i in range(4)} | {i: (0, ds[0].shape[1]) for i in range(4, 8)},
    )[0]


def unit_of(residual):
    centre = jnp.mean(residual, axis=1, keepdims=True)
    spread = residual - centre
    inverse = lax.rsqrt(jnp.mean(spread * spread, axis=1, keepdims=True) + norm_eps)
    return spread * inverse, inverse


def norm_back(upstream, unit_rows, inverse, gain):
    unit_grad = upstream * gain
    return inverse * (
        unit_grad
        - jnp.mean(unit_grad, axis=1, keepdims=True)
        - unit_rows * jnp.mean(unit_grad * unit_rows, axis=1, keepdims=True)
    )


def up_down(low_ref, bias_ref, up_refs, down_ref, act_ref, slope_ref, sum_ref, start):
    up_ref = up_refs[0]
    arrive(low_ref, bias_ref, up_ref)

    def units_of(cs):
        pre = bias_ref[:, cs].astype(F32)[2:3] + dot(low_ref[...], up_ref[:, cs])
        phi = 0.5 + 0.5 * lax.erf(pre * half_root)
        act_ref[:, cs] = (pre * phi).astype(BF)
        slope_ref[:, cs] = (phi + pre * jnp.exp(-0.5 * pre * pre) * inv_root_two_pi).astype(BF)

    chunks(up_ref.shape[1], 256, units_of)
    send(act_ref)
    send(slope_ref)
    arrive(down_ref)

    def features_of(cs):
        part = dot(act_ref[...], down_ref[:, cs])
        sum_ref[:, cs] = part if start else sum_ref[:, cs] + part

    chunks(down_ref.shape[1], 256, features_of)


def ffn_back_block(
    g_ref, low_ref, act_ref, slope_ref, down_ref, up_refs, outs, sum_in_ref, sum_ref, pre_s
):
    down_grad_ref, up_grad_ref, bias_ref = outs
    up_ref = up_refs[0]
    arrive(g_ref, act_ref, slope_ref, down_ref)

    def units_of(cs):
        g = g_ref[...]
        down_grad_ref[cs] = contract_rows(act_ref[:, cs], g).astype(BF)
        pre = (contract_cols(g, down_ref[cs]) * slope_ref[:, cs].astype(F32)).astype(BF)
        pre_s[:, cs] = pre
        bias_ref[:, cs] = jnp.sum(pre.astype(F32), axis=0, keepdims=True)

    chunks(down_ref.shape[0], 256, units_of)
    send(down_grad_ref)
    arrive(low_ref, up_ref, sum_in_ref)

    def features_of(cs):
        pre = pre_s[...]
        up_grad_ref[cs] = contract_rows(low_ref[:, cs], pre).astype(BF)
        sum_ref[:, cs] = sum_in_ref[:, cs] + contract_cols(pre, up_ref[cs])

    chunks(up_ref.shape[0], 256, features_of)
    send(up_grad_ref)


def ffn_grad_outs(width, units):
    return [shape((units, width), BF), shape((width, units), BF), shape((1, units), F32)]


def ffn_far_kernel(
    low_ref, u2_ref, bias2_ref, d2_ref, u3_ref, bias3_ref, d3_ref,
    sum_in_ref, unit_ref, gain1_ref, shift1_ref, bd_ref, gain2_ref, shift2_ref, out_grad_ref,
    act2_ref, sl2_ref, out_ref, low_grad_ref, vec_ref,
    down_grad_ref, up_grad_ref, bu_ref, sum_ref,
    act3_s, sl3_s, pre_s, part_s,
):
    up_down(low_ref, bias2_ref, (u2_ref,), d2_ref, act2_ref, sl2_ref, part_s, True)
    up_down(low_ref, bias3_ref, (u3_ref,), d3_ref, act3_s, sl3_s, part_s, False)
    gain1, gain2, shift2 = row(gain1_ref), row(gain2_ref), row(shift2_ref)
    shift1 = row(shift1_ref) + row(bd_ref)
    arrive(unit_ref, sum_in_ref, out_grad_ref)
    vec_ref[...] = jnp.zeros(vec_ref.shape, F32)

    def rows_of(rs):
        resid = unit_ref[rs] * gain1 + shift1 + sum_in_ref[rs] + part_s[rs]
        unit, inverse = unit_of(resid)
        out_ref[rs] = (unit * gain2 + shift2).astype(BF)
        upstream = out_grad_ref[rs].astype(F32)
        vec_ref[0:1] += jnp.sum(upstream * unit, axis=0, keepdims=True)
        vec_ref[1:2] += jnp.sum(upstream, axis=0, keepdims=True)
        back = norm_back(upstream, unit, inverse, gain2)
        sum_ref[rs] = back
        g = back.astype(BF)
        low_grad_ref[rs] = g
        vec_ref[2:3] += jnp.sum(g.astype(F32), axis=0, keepdims=True)

    chunks(unit_ref.shape[0], 256, rows_of)
    send(out_ref)
    send(low_grad_ref)
    ffn_back_block(
        low_grad_ref, low_ref, act3_s, sl3_s, d3_ref, (u3_ref,),
        (down_grad_ref, up_grad_ref, bu_ref), sum_ref, sum_ref, pre_s,
    )


def ffn_far(
    low, joints, ups, downs, near, unit, gain1, shift1, b_down, gain2, shift2, out_grad, after=()
):
    rows, width = low.shape
    units = downs[0].shape[0]
    at = joints[0].shape[0] - 16
    piece = shape((rows, units), BF)
    return call(
        ffn_far_kernel, "ffn_far",
        [
            piece, piece, shape((rows, width), BF), shape((rows, width), BF), shape((8, width), F32),
            *ffn_grad_outs(width, units), shape((rows, width), F32),
        ],
        (
            low, ups[0], joints[0], downs[0], ups[1], joints[1], downs[1], near, unit,
            gain1, shift1, b_down, gain2, shift2, out_grad,
        ),
        part={2: (at, 16), 5: (at, 16)}, first=0, after=after,
        scratch=[pltpu.VMEM((rows, units), BF)] * 3 + [pltpu.VMEM((rows, width), F32)],
    )


def ffn_back_kernel(
    g_ref, act_ref, down_ref, slope_ref, low_ref, up_ref, sum_in_ref,
    down_grad_ref, up_grad_ref, bu_ref, sum_ref, pre_s,
):
    ffn_back_block(
        g_ref, low_ref, act_ref, slope_ref, down_ref, (up_ref,),
        (down_grad_ref, up_grad_ref, bu_ref), sum_in_ref, sum_ref, pre_s,
    )


def ffn_back(g, low, act, slope, up, down, acc, after=()):
    rows, width = low.shape
    units = down.shape[0]
    return call(
        ffn_back_kernel, "ffn_back",
        [*ffn_grad_outs(width, units), shape((rows, width), F32)],
        (g, act, down, slope, low, up, acc), after=after, first=0,
        scratch=[pltpu.VMEM((rows, units), BF)],
    )


def ffn_last_kernel(
    g_ref, act1_ref, d1_ref, sl1_ref, low_ref, u1_ref, act0_ref, d0_ref, sl0_ref, u0_ref, sum_in_ref,
    unit_ref, inv_ref, gain_ref, vec_in_ref, *refs,
):
    low_ref_out, resid_ref, vec_ref = refs[6:9]
    sum_s, pre_s = refs[9:]
    ffn_back_block(
        g_ref, low_ref, act1_ref, sl1_ref, d1_ref, (u1_ref,), refs[0:3], sum_in_ref, sum_s, pre_s
    )
    ffn_back_block(
        g_ref, low_ref, act0_ref, sl0_ref, d0_ref, (u0_ref,), refs[3:6], sum_s, sum_s, pre_s
    )
    gain = row(gain_ref)
    arrive(unit_ref, inv_ref)
    vec_ref[...] = vec_in_ref[...]

    def rows_of(rs):
        upstream = sum_s[rs]
        unit = unit_ref[rs]
        vec_ref[4:5] += jnp.sum(upstream * unit, axis=0, keepdims=True)
        vec_ref[5:6] += jnp.sum(upstream, axis=0, keepdims=True)
        back = norm_back(upstream, unit, inv_ref[rs], gain)
        resid_ref[rs] = back
        low = back.astype(BF)
        low_ref_out[rs] = low
        vec_ref[6:7] += jnp.sum(low.astype(F32), axis=0, keepdims=True)

    chunks(unit_ref.shape[0], 256, rows_of)
    send(resid_ref)
    send(low_ref_out)


def ffn_last(g, low, acts, slopes, ups, downs, acc, unit, inverse, gain, vecs, after=()):
    rows, width = low.shape
    units = downs[0].shape[0]
    return call(
        ffn_last_kernel, "ffn_last",
        [
            *ffn_grad_outs(width, units), *ffn_grad_outs(width, units),
            shape((rows, width), BF), shape((rows, width), F32), shape((8, width), F32),
        ],
        (
            g, acts[1], downs[1], slopes[1], low, ups[1], acts[0], downs[0], slopes[0], ups[0], acc,
            unit, inverse, gain, vecs,
        ),
        after=after, first=0,
        scratch=[pltpu.VMEM((rows, width), F32), pltpu.VMEM((rows, units), BF)],
    )


def spread_small_kernel(in_ref, bq_ref, bv_ref, bu_ref, *rest):
    sums = in_ref[...]
    cols = bq_ref.shape[0]
    bq_ref[...] = sums[0:1, 0:cols].reshape(cols)
    bv_ref[...] = sums[1:2, 0:cols].reshape(cols)
    bu_ref[...] = sums[2:3].reshape(-1)
    for at, ref in zip((8, 9, 10, 12, 13, 14), rest):
        ref[...] = sums[at : at + 1].reshape(-1)


def spread_small(sums, cols, units):
    width = sums.shape[1]
    return call(
        spread_small_kernel, "spread_small",
        [shape((cols,), F32), shape((cols,), F32), shape((units,), F32)] + [shape((width,), F32)] * 6,
        (sums,), part={0: (2 * cols, 16)},
    )


def swap(a, axis, distance):
    size = lax.axis_size(axis)
    return lax.ppermute(a, axis, [(i, i ^ distance) for i in range(size)])


def to_core(a):
    return swap(a, "narrow", 1)


def to_chip(a):
    return swap(a, "narrow", 2)


def to_middle(a):
    return lax.ppermute(a, "narrow", [(1, 2), (2, 1)])


def wide_bits():
    size = lax.axis_size("wide")
    bits = []
    while size > 1:
        assert size % 2 == 0
        bits.append(len(bits))
        size //= 2
    return bits


def part_of(a, which, parts):
    rows = a.shape[0] // parts
    return lax.dynamic_slice_in_dim(a, which * rows, rows, 0)


def in_order(side, mine, got):
    return jnp.where(side == 0, jnp.concatenate([mine, got]), jnp.concatenate([got, mine]))


def hold(a, *others):
    return lax.optimization_barrier((a, *others))[0]


def add_low(*terms):
    total = terms[0].astype(F32)
    for term in terms[1:]:
        total = total + term.astype(F32)
    return total.astype(BF)


def side_of(bit):
    return (lax.axis_index("wide") >> bit) & 1


def own_piece(a):
    at = 0
    for bit in wide_bits():
        at = 2 * at + side_of(bit)
    return part_of(a, at, lax.axis_size("wide"))


class WideSum:
    def __init__(self, a):
        self.a = a
        self.step = 0
        self.send()

    def send(self):
        bit = self.step
        if bit < 3:
            side = side_of(bit)
            self.keep = part_of(self.a, side, 2)
            self.sent = part_of(self.a, 1 - side, 2)
        else:
            self.keep = self.sent = self.a
        self.got = swap(self.sent, "wide", 1 << bit)

    def advance(self, *waits):
        got = hold(self.got, *waits) if waits else self.got
        self.a = add_low(self.keep, got)
        self.step += 1
        if self.step < len(wide_bits()):
            self.send()

    def piece(self, *waits):
        while self.step < len(wide_bits()):
            self.advance(*waits)
            waits = ()
        return self.a


class WideGather:
    def __init__(self, a, bits=(2, 1, 0)):
        self.a = self.sent = a
        self.bits = bits
        self.step = 0
        self.send()

    def send(self):
        self.sent = self.a
        self.got = swap(self.a, "wide", 1 << self.bits[self.step])

    def advance(self, *waits):
        got = hold(self.got, *waits) if waits else self.got
        self.a = in_order(side_of(self.bits[self.step]), self.a, got)
        self.step += 1
        if self.step < len(self.bits):
            self.send()

    def whole(self, *waits):
        while self.step < len(self.bits):
            self.advance(*waits)
            waits = ()
        return self.a


def local(
    tokens, item_lengths, w_query, b_query, w_key, w_value, b_value, w_out, b_out,
    gain_attn, shift_attn, w_up, b_up, w_down, b_down, gain_ffn, shift_ffn, out_grad,
):
    rows, width = tokens.shape
    cols = w_query.shape[1]
    units = w_up.shape[1]
    assert lax.axis_size("narrow") == 4
    me = lax.axis_index("narrow").reshape(1)

    tok_mid = to_middle(tokens)
    tok_core = to_core(tokens)
    pieces = to_chip(own_piece(w_down))
    joint = pack_joint(w_query, w_key, w_value, w_out, b_query, b_value, b_up)
    joint_core = to_core(joint)
    joint_chip = to_chip(hold(joint, pieces, tok_mid))
    down_gather = WideGather(pieces, wide_bits()[::-1])
    while down_gather.step < len(down_gather.bits) - 2:
        down_gather.advance(joint_core)
    near0, near1 = attend_pair(
        "attend_near", item_lengths, me, tokens, tok_core, tok_mid, [joint, joint_core],
        (down_gather.sent,),
    )
    down_gather.advance(near1[2])
    gate = down_gather.sent
    joint_chip = hold(joint_chip, gate)
    joint_diag = to_core(joint_chip)
    up_chip = to_chip(hold(w_up, joint_chip))
    up_core = to_core(hold(w_up, joint_chip))
    down_core = to_core(hold(w_down, joint_chip))
    far2, far3 = attend_pair(
        "attend_far", item_lengths, me, tokens, tok_core, tok_mid, [joint_chip, joint_diag], (gate,)
    )
    joints = [joint, joint_core, joint_chip, joint_diag]
    saved = [near0, near1, far2, far3]
    unit_one, inv_one, low, act0, sl0, act1, sl1, near_sum = norm_near(
        tokens, [s[0] for s in saved], joints, b_out, gain_attn, shift_attn,
        [w_up, up_core], [w_down, down_core],
    )
    down_chip = down_gather.whole(inv_one)
    down_diag = to_core(down_chip)
    up_chip = hold(up_chip, down_chip)
    up_diag = to_core(up_chip)
    act2, sl2, layer_out, ffn_grad, vecs, down_d, up_d, bu_d, acc = ffn_far(
        low, joints[2:], [up_chip, up_diag], [down_chip, down_diag],
        near_sum, unit_one, gain_attn, shift_attn, b_down, gain_ffn, shift_ffn, out_grad,
    )

    up_from_core = to_core(up_d)
    down_from_core = to_core(down_d)
    down_x, up_x, bu_x, acc = ffn_back(ffn_grad, low, act2, sl2, up_chip, down_chip, acc)
    up_far = add_low(up_x, hold(up_from_core, bu_x))
    up_sum = to_chip(up_far)
    down_far = add_low(down_x, hold(down_from_core, up_far))
    down_sum = to_chip(down_far)
    down_c, up_c, bu_c, down_o, up_o, bu_o, attn_grad, resid_one, vecs = ffn_last(
        ffn_grad, low, (act0, act1), (sl0, sl1), (w_up, up_core), (w_down, down_core), acc,
        unit_one, inv_one, gain_attn, vecs, (up_far, down_far),
    )
    up_back = to_core(up_c)
    down_back = to_core(down_c)
    grads, parts = [None] * 4, [None] * 4
    bus = (bu_o, bu_c, bu_x, bu_d)

    def back_attend(r, *after):
        grads[r], parts[r] = attend_back(
            item_lengths, me, tokens, tok_core, tok_mid, attn_grad, (joints[r], saved[r]),
            bus[r], vecs, after,
        )
        return grads[r]

    mark = back_attend(3)
    up_sum = hold(up_sum, mark)
    near_up = WideSum(add_low(up_o, hold(up_back, up_sum), up_sum))
    down_near = add_low(down_o, hold(down_back, near_up.sent))
    joint_from_core = to_core(hold(grads[3], down_near))
    mark = back_attend(2, near_up.sent, down_near)
    down_sum = hold(down_sum, mark)
    near_down = WideSum(add_low(down_near, down_sum))
    joint_far = add_low(grads[2], hold(joint_from_core, near_down.a))
    joint_sum = to_chip(joint_far)
    near_up.advance(joint_far)
    mark = back_attend(1, joint_far, near_up.sent, near_down.sent)
    near_up.advance(mark)
    near_down.advance(near_up.sent)
    joint_back = to_core(hold(grads[1], near_down.sent))
    mark = back_attend(0, near_up.sent, near_down.sent)
    joint_sum = hold(joint_sum, mark)
    joint_back = hold(joint_back, joint_sum)

    def rows_of(a, part):
        return a[: 2 * cols + 32] if part == 0 else a[2 * cols + 32 :]

    def joint_part(i, own, got):
        return WideSum(add_low(rows_of(own, i), rows_of(got, i), rows_of(joint_back, i)))

    first = joint_part(0, grads[0], joint_sum)
    second = joint_part(1, grads[0], hold(joint_sum, first.sent))
    up_gather = WideGather(near_up.piece(second.sent))
    near_down.advance(up_gather.sent)
    first.advance(near_down.sent)
    down_gather = WideGather(near_down.piece(first.sent))
    up_gather.advance(down_gather.sent)
    second.advance(up_gather.sent)
    oth_low = other_grad(parts, joints, rows, (second.sent,))
    first.advance(oth_low)
    up_gather.advance(first.sent)
    down_gather.advance(up_gather.sent)
    oth_core, oth_mid = to_core(hold(oth_low, down_gather.sent)), to_middle(hold(oth_low, down_gather.sent))
    second.advance(down_gather.sent)
    first = WideGather(first.piece(second.sent))
    down_gather.advance(first.sent)
    second = WideGather(second.piece(down_gather.sent))
    first.advance(second.sent)
    token_grad = take_back(
        item_lengths, me, hold(oth_core, first.sent), hold(oth_mid, first.sent), resid_one,
        parts, joints, (first.sent, second.sent),
    )
    second.advance(token_grad)
    first.advance(second.sent)
    w_up_grad = up_gather.whole(first.sent).astype(F32)
    second.advance(w_up_grad)
    w_down_grad = down_gather.whole(second.sent).astype(F32)
    qk_grad = first.whole(w_down_grad).astype(F32)
    bq, bv, bu, gain_ffn_g, shift_ffn_g, b_down_g, gain_attn_g, shift_attn_g, b_out_g = spread_small(
        qk_grad, cols, units
    )
    vo_grad = second.whole(qk_grad).astype(F32)
    joint_grads = [qk_grad[:cols], qk_grad[cols : 2 * cols], vo_grad[:cols]]
    w_out_grad = vo_grad[cols:]
    return (
        layer_out,
        token_grad,
        joint_grads[0].T,
        bq,
        joint_grads[1].T,
        joint_grads[2].T,
        bv,
        w_out_grad,
        b_out_g,
        gain_attn_g,
        shift_attn_g,
        w_up_grad,
        bu,
        w_down_grad,
        b_down_g,
        gain_ffn_g,
        shift_ffn_g,
    )


def take_back_kernel(lens_ref, me_ref, core_ref, mid_ref, *refs):
    ds, weights, resid_ref, out_ref, oth_s, oth_sem = refs[0:4], refs[4:8], *refs[8:]
    flag, use_core = neighbour(lens_ref, me_ref, resid_ref.shape[0])
    other = pick_other(use_core, core_ref, mid_ref, oth_s, oth_sem)
    arrive(*ds, *weights, resid_ref)
    other.wait()
    depth = ds[0].shape[1]

    def features_of(cs):
        total = resid_ref[:, cs] + jnp.where(flag, oth_s[:, cs].astype(F32), 0.0)
        for d_ref, w_ref in zip(ds, weights):
            total = total + dot(d_ref[...], w_ref[0:depth, cs])
        out_ref[:, cs] = total

    chunks(out_ref.shape[1], 256, features_of)


def take_back(lens, me, core, mid, resid, ds, joints, after):
    rows, width = resid.shape
    depth = ds[0].shape[1]
    return call(
        take_back_kernel, "take_back", [shape((rows, width), F32)],
        (lens, me, core, mid, *ds, *joints, resid), smem=2, raw=(2, 3), after=after,
        part={i: (0, rows) for i in range(4, 8)} | {i: (0, depth) for i in range(8, 12)},
        scratch=[pltpu.VMEM(core.shape, BF), pltpu.SemaphoreType.DMA],
    )[0]


def solution(mesh):
    rows_spec = P(("wide", "narrow"), None)
    col_spec = P(None, "narrow")
    vec_spec = P("narrow")
    row_spec = P("narrow", None)
    full = P()
    return jax.shard_map(
        local,
        mesh=mesh,
        in_specs=(
            rows_spec, P("wide"), col_spec, vec_spec, col_spec, col_spec, vec_spec, row_spec, full,
            full, full, col_spec, vec_spec, row_spec, full, full, full, rows_spec,
        ),
        out_specs=(
            rows_spec, rows_spec, col_spec, vec_spec, col_spec, col_spec, vec_spec, row_spec, full,
            full, full, col_spec, vec_spec, row_spec, full, full, full,
        ),
        check_vma=False,
    )
```

```python
import functools

import jax
import jax.numpy as jnp
from jax import lax
from jax.experimental import pallas as pl
from jax.experimental.pallas import tpu as pltpu
from jax.sharding import PartitionSpec as P

HD = 64
F32 = jnp.float32
BF = jnp.bfloat16
MIB = 1 << 20

norm_eps = 1e-12
masked_shift = 1e30
half_root = 0.7071067811865476
inv_root_two_pi = 0.3989422804014327
score_scale = HD**-0.5

VM = pl.BlockSpec(memory_space=pltpu.VMEM)
SM = pl.BlockSpec(memory_space=pltpu.SMEM)
ANY = pl.BlockSpec(memory_space=pl.ANY)


def dot(left, right):
    return jnp.dot(left, right, preferred_element_type=F32)


def contract_rows(left, right):
    return lax.dot_general(left, right, (((0,), (0,)), ((), ())), preferred_element_type=F32)


def contract_cols(left, right):
    return lax.dot_general(left, right, (((1,), (1,)), ((), ())), preferred_element_type=F32)


def shape(dims, dtype):
    return jax.ShapeDtypeStruct(dims, dtype)


def row(ref):
    return ref[...].astype(F32).reshape(1, -1)


class Arriving:
    def __init__(self, source, buffer, sem):
        self.buffer = buffer
        self.shape = buffer.shape
        self.dtype = buffer.dtype
        self.copy = pltpu.make_async_copy(source, buffer, sem)
        self.started = False
        self.waiting = True
        self.then = []

    def start(self):
        if not self.started:
            self.copy.start()
            self.started = True

    def wait(self):
        self.start()
        if self.waiting:
            self.copy.wait()
            self.waiting = False
            for other in self.then:
                other.start()

    def __getitem__(self, index):
        self.wait()
        return self.buffer[index]


class Leaving:
    def __init__(self, target, buffer, sem):
        self.buffer = buffer
        self.shape = buffer.shape
        self.dtype = buffer.dtype
        self.copy = pltpu.make_async_copy(buffer, target, sem)
        self.sent = False

    def __getitem__(self, index):
        return self.buffer[index]

    def __setitem__(self, index, value):
        self.buffer[index] = value

    def send(self):
        if not self.sent:
            self.copy.start()
            self.sent = True


def call(
    kernel, name, out_shape, args, smem=0, scratch=(), vmem=60, after=(), raw=(), part=(), first=0,
    stay=(), stay_out=(),
):
    count = len(args)
    outs = len(out_shape)
    loaded = [i for i in range(smem, count) if i not in raw and i not in stay]
    leaving_out = [n for n in range(outs) if n not in stay_out]
    part = dict(part)

    def held(i):
        dims = (part[i][1], *args[i].shape[1:]) if i in part else args[i].shape
        return pltpu.VMEM(dims, args[i].dtype)

    buffers = [held(i) for i in loaded]
    buffers += [pltpu.VMEM(out_shape[n].shape, out_shape[n].dtype) for n in leaving_out]

    def body(*refs):
        given = list(refs[:count])
        refs = refs[count + len(after) :]
        results, refs = list(refs[:outs]), refs[outs:]
        own, refs = refs[: len(buffers)], refs[len(buffers) :]
        in_sems, out_sems, refs = refs[0], refs[1], refs[2:]
        for n, i in enumerate(loaded):
            source = given[i].at[pl.ds(*part[i])] if i in part else given[i]
            given[i] = Arriving(source, own[n], in_sems.at[n])
        late = [given[i] for i in loaded if first and i >= first]
        for i in loaded:
            if given[i] not in late:
                given[i].start()
                given[i].then = late
        for m, n in enumerate(leaving_out):
            results[n] = Leaving(results[n], own[len(loaded) + m], out_sems.at[m])
        kernel(*given, *results, *refs)
        for i in loaded:
            given[i].wait()
        for n in leaving_out:
            results[n].send()
        for n in leaving_out:
            results[n].copy.wait()

    in_specs = [SM] * smem + [VM if i in stay else ANY for i in range(smem, count)]
    return pl.pallas_call(
        body,
        out_shape=tuple(out_shape),
        in_specs=in_specs + [ANY] * len(after),
        out_specs=tuple(VM if n in stay_out else ANY for n in range(outs)),
        scratch_shapes=[
            *buffers, pltpu.SemaphoreType.DMA((max(len(loaded), 1),)),
            pltpu.SemaphoreType.DMA((max(len(leaving_out), 1),)), *scratch,
        ],
        compiler_params=pltpu.CompilerParams(vmem_limit_bytes=vmem * MIB),
        cost_estimate=pl.CostEstimate(flops=1000, transcendentals=0, bytes_accessed=1000),
        name=name,
    )(*args, *after)


def send(ref):
    if isinstance(ref, Leaving):
        ref.send()


def arrive(*refs):
    for ref in refs:
        if isinstance(ref, Arriving):
            ref.wait()


def chunks(extent, size, body):
    def step(i, carry):
        body(pl.ds(pl.multiple_of(i * size, size), size))
        return carry

    lax.fori_loop(0, extent // size, step, 0)


def masked(picked, a):
    return jnp.where(picked, a.astype(F32), 0.0).astype(BF)


def joint_kernel(wq_ref, wk_ref, wv_ref, wo_ref, bq_ref, bv_ref, bu_ref, out_ref, tail_s):
    cols = wq_ref.shape[0]
    for i, ref in enumerate((wq_ref, wk_ref, wv_ref, wo_ref)):
        out_ref[i * cols : (i + 1) * cols] = ref[...]
    tail_s[...] = jnp.zeros_like(tail_s)
    tail_s[0:1, 0:cols] = row(bq_ref)
    tail_s[1:2, 0:cols] = row(bv_ref)
    tail_s[2:3, :] = row(bu_ref)
    out_ref[4 * cols : 4 * cols + 16] = tail_s[...].astype(BF)


def pack_joint(w_query, w_key, w_value, w_out, b_query, b_value, b_up):
    width, cols = w_query.shape
    return call(
        joint_kernel, "pack_joint", [shape((4 * cols + 16, width), BF)],
        (w_query.T, w_key.T, w_value.T, w_out, b_query, b_value, b_up),
        scratch=[pltpu.VMEM((16, width), F32)],
    )[0]


def neighbour(lens_ref, me_ref, rows):
    me = me_ref[0]
    here = me * rows
    first = jnp.int32(0)
    start = jnp.int32(0)
    length = jnp.int32(0)
    for j in range(lens_ref.shape[0]):
        n = lens_ref[j]
        inside = (first <= here) & (here < first + n)
        start = jnp.where(inside, first, start)
        length = jnp.where(inside, n, length)
        first = first + n
    other = jnp.where(start == here, me + 1, me - 1)
    return length > rows, other == (me ^ 1)


def pick_other(use_core, core_ref, mid_ref, buffer, sem):
    from_core = pltpu.make_async_copy(core_ref, buffer, sem)
    from_mid = pltpu.make_async_copy(mid_ref, buffer, sem)

    @pl.when(use_core)
    def _():
        from_core.start()

    @pl.when(jnp.logical_not(use_core))
    def _():
        from_mid.start()

    return from_core


def attend_block(flag, own_ref, oth_s, a_ref, outs, scratch):
    ctx_ref, ct_ref, lse_ref, q_ref, k_ref, v_ref = outs
    qt_s, vt_s = scratch
    rows, cols = q_ref.shape
    tail = a_ref[4 * cols : 4 * cols + 16].astype(F32)
    wk = a_ref[cols : 2 * cols]
    wv = a_ref[2 * cols : 3 * cols]
    near = slice(0, rows)
    far = slice(rows, 2 * rows)
    q = (contract_cols(own_ref[...], a_ref[0:cols]) + tail[0:1, 0:cols]).astype(BF)
    q = q * jnp.asarray(score_scale, BF)
    q_ref[...] = q
    qt_s[...] = q.T
    for part, tok_ref in ((near, own_ref), (far, oth_s)):
        k_ref[part] = contract_cols(tok_ref[...], wk).astype(BF)
        v = (contract_cols(tok_ref[...], wv) + tail[1:2, 0:cols]).astype(BF)
        v_ref[part] = v
        vt_s[:, part] = v.T
    head_of_row = lax.broadcasted_iota(jnp.int32, (cols, 1), 0) // HD

    def head(h, carry):
        hs = pl.ds(pl.multiple_of(h * HD, HD), HD)
        q_h = masked(head_of_row == h, qt_s[...])
        s_own = dot(k_ref[near], q_h)
        s_other = dot(k_ref[far], q_h)
        top_own = jnp.max(s_own, axis=0, keepdims=True)
        top_other = jnp.max(s_other, axis=0, keepdims=True)
        top = jnp.where(flag, jnp.maximum(top_own, top_other), top_own)
        p_own = jnp.exp(s_own - top)
        p_other = jnp.exp(s_other - jnp.where(flag, top, masked_shift))
        total = jnp.sum(p_own, axis=0, keepdims=True) + jnp.sum(p_other, axis=0, keepdims=True)
        c = dot(vt_s[hs, near], p_own.astype(BF)) + dot(vt_s[hs, far], p_other.astype(BF))
        ct_ref[hs] = c * (1.0 / total)
        lse_ref[pl.ds(h, 1)] = top + jnp.log(total)
        return carry

    lax.fori_loop(0, cols // HD, head, 0)
    ctx_ref[...] = ct_ref[...].T.astype(BF)


def block_outs(rows, cols):
    return [
        shape((rows, cols), BF), shape((cols, rows), F32), shape((cols // HD, rows), F32),
        shape((rows, cols), BF), shape((2 * rows, cols), BF), shape((2 * rows, cols), BF),
    ]


def attend_scratch(rows, width, cols):
    return [
        pltpu.VMEM((rows, width), BF), pltpu.SemaphoreType.DMA,
        pltpu.VMEM((cols, rows), BF), pltpu.VMEM((cols, 2 * rows), BF),
    ]


class Once:
    def __init__(self, copy, buffer):
        self.copy = copy
        self.buffer = buffer

    def __call__(self):
        if self.copy is not None:
            self.copy.wait()
            self.copy = None
        return self.buffer[...]


def attend_pair_kernel(
    lens_ref, me_ref, core_ref, mid_ref, own_ref, a0_ref, a1_ref, *refs, after
):
    targets = refs[after : after + 12]
    own_s, a_s, *held = refs[after + 12 : after + 20]
    own_sem, a_sem, out_sem, oth_s, oth_sem, qt_s, vt_s = refs[after + 20 :]
    own_copy = pltpu.make_async_copy(own_ref, own_s, own_sem)
    own_copy.start()
    weights = [
        pltpu.make_async_copy(ref, a_s.at[i], a_sem.at[i]) for i, ref in enumerate((a0_ref, a1_ref))
    ]
    weights[0].start()
    flag, use_core = neighbour(lens_ref, me_ref, own_ref.shape[0])
    other = pick_other(use_core, core_ref, mid_ref, oth_s, oth_sem)
    leaving = [
        [
            pltpu.make_async_copy(buffer.at[i], targets[6 * i + n], out_sem.at[i, n])
            for n, buffer in enumerate(held)
        ]
        for i in range(2)
    ]
    own_copy.wait()

    def block(i, carry):
        @pl.when(i == 0)
        def _():
            weights[0].wait()
            other.wait()
            weights[1].start()

        @pl.when(i == 1)
        def _():
            weights[1].wait()

        attend_block(
            flag, own_s, oth_s, a_s.at[i], [buffer.at[i] for buffer in held], (qt_s, vt_s)
        )
        for n in range(2):

            @pl.when(i == n)
            def _():
                for copy in leaving[n]:
                    copy.start()

        return carry

    lax.fori_loop(0, 2, block, 0)
    for copies in leaving:
        for copy in copies:
            copy.wait()


def attend_pair(name, lens, me, own, tok_core, tok_mid, blocks, after=()):
    rows, width = own.shape
    cols = (blocks[0].shape[0] - 16) // 4
    outs = block_outs(rows, cols)
    got = pl.pallas_call(
        functools.partial(attend_pair_kernel, after=len(after)),
        out_shape=tuple(outs * 2),
        in_specs=[SM, SM] + [ANY] * (5 + len(after)),
        out_specs=tuple([ANY] * 12),
        scratch_shapes=[
            pltpu.VMEM(own.shape, BF), pltpu.VMEM((2, *blocks[0].shape), BF),
            *[pltpu.VMEM((2, *o.shape), o.dtype) for o in outs],
            pltpu.SemaphoreType.DMA, pltpu.SemaphoreType.DMA((2,)), pltpu.SemaphoreType.DMA((2, 6)),
            *attend_scratch(rows, width, cols),
        ],
        compiler_params=pltpu.CompilerParams(vmem_limit_bytes=60 * MIB),
        cost_estimate=pl.CostEstimate(flops=1000, transcendentals=0, bytes_accessed=1000),
        name=name,
    )(lens, me, tok_core, tok_mid, own, *blocks, *after)
    return got[:6], got[6:]


def norm_near_kernel(
    own_ref, c0_ref, w0_ref, c1_ref, w1_ref, c2_ref, w2_ref, c3_ref, w3_ref, bo_ref, gain_ref, shift_ref,
    u0_ref, bias0_ref, d0_ref, u1_ref, bias1_ref, d1_ref,
    unit_ref, inv_ref, low_ref, act0_ref, sl0_ref, act1_ref, sl1_ref, sum_ref,
):
    pairs = ((c0_ref, w0_ref), (c1_ref, w1_ref), (c2_ref, w2_ref), (c3_ref, w3_ref))
    vectors = row(bo_ref), row(gain_ref), row(shift_ref)
    for pair in pairs:
        arrive(*pair)
    arrive(own_ref)

    def rows_of(rs):
        resid = own_ref[rs].astype(F32) + vectors[0]
        for c_ref, w_ref in pairs:
            resid = resid + dot(c_ref[rs], w_ref[...])
        unit, inverse = unit_of(resid)
        unit_ref[rs] = unit
        inv_ref[rs] = inverse
        low_ref[rs] = (unit * vectors[1] + vectors[2]).astype(BF)

    chunks(own_ref.shape[0], 256, rows_of)
    send(unit_ref)
    send(inv_ref)
    send(low_ref)
    up_down(low_ref, bias0_ref, (u0_ref,), d0_ref, act0_ref, sl0_ref, sum_ref, True)
    up_down(low_ref, bias1_ref, (u1_ref,), d1_ref, act1_ref, sl1_ref, sum_ref, False)


def norm_near(own, ctxs, joints, b_out, gain, shift, ups, downs, after=()):
    rows, width = own.shape
    units = downs[0].shape[0]
    at = joints[0].shape[0] - 16
    piece = shape((rows, units), BF)
    cols = ctxs[0].shape[1]
    terms = [x for pair in zip(ctxs, joints) for x in pair]
    return call(
        norm_near_kernel, "norm_near",
        [
            shape((rows, width), F32), shape((rows, 1), F32), shape((rows, width), BF),
            piece, piece, piece, piece, shape((rows, width), F32),
        ],
        (
            own, *terms, b_out, gain, shift,
            ups[0], joints[0], downs[0], ups[1], joints[1], downs[1],
        ),
        part={2 * i + 2: (3 * cols, cols) for i in range(4)} | {13: (at, 16), 16: (at, 16)},
        after=after, first=0,
    )


def attend_back_block(
    flag, g_ref, wo_ref, saved, own_ref, other, grad_ref, sums, b_s, bu_ref, vec_ref, scratch
):
    ct_ref, lse_ref, q_ref, k_ref, v_ref = saved
    d_s = sums
    gt_s, qt_s, kt_s, dqt_s, p_s, ds_s, dk_s, dv_s, dot_s, g_s, t_s = scratch
    rows, cols = q_ref.shape
    near = slice(0, rows)
    far = slice(rows, 2 * rows)
    arrive(g_ref, wo_ref)
    other = other()
    arrive(q_ref)

    def query_rows(rs):
        g = contract_cols(g_ref[rs], wo_ref[...]).astype(BF)
        g_s[rs] = g
        gt_s[:, rs] = g.T
        qt_s[:, rs] = q_ref[rs].T

    chunks(rows, 256, query_rows)
    arrive(k_ref)

    def key_rows(rs):
        kt_s[:, rs] = k_ref[rs].T

    chunks(2 * rows, 256, key_rows)
    dot_s[...] = gt_s[...].astype(F32) * ct_ref[...]
    dk_s[...] = jnp.zeros(dk_s.shape, F32)
    dv_s[...] = jnp.zeros(dv_s.shape, F32)
    head_of_row = lax.broadcasted_iota(jnp.int32, (cols, 1), 0) // HD
    head_of_lane = lax.broadcasted_iota(jnp.int32, (1, cols), 1) // HD
    arrive(q_ref, k_ref, v_ref, lse_ref)

    def head(h, carry):
        hs = pl.ds(pl.multiple_of(h * HD, HD), HD)
        row_dot = jnp.sum(dot_s[hs], axis=0, keepdims=True)
        q_h = masked(head_of_row == h, qt_s[...])
        g_h = masked(head_of_row == h, gt_s[...])
        lse = lse_ref[pl.ds(h, 1)]
        for part, shift in ((near, lse), (far, jnp.where(flag, lse, masked_shift))):
            p = jnp.exp(dot(k_ref[part], q_h) - shift)
            p_s[part] = p.astype(BF)
            ds_s[part] = (p * (dot(v_ref[part], g_h) - row_dot)).astype(BF)
        dqt_s[hs] = dot(kt_s[hs], ds_s[...])
        dk_s[...] += dot(ds_s[...], masked(head_of_lane == h, q_ref[...]))
        dv_s[...] += dot(p_s[...], masked(head_of_lane == h, g_s[...]))
        return carry

    lax.fori_loop(0, cols // HD, head, 0)
    dqt = (dqt_s[...] * score_scale).astype(BF)
    dq = dqt.T
    d_s[near, 0:cols] = dq
    d_s[far, 0:cols] = jnp.zeros((rows, cols), BF)
    t_s[0:cols, near] = dqt
    b_s[...] = jnp.zeros(b_s.shape, F32)

    def grad_rows(rs):
        dk = dk_s[rs].astype(BF)
        dv = dv_s[rs].astype(BF)
        d_s[rs, cols : 2 * cols] = dk
        d_s[rs, 2 * cols : 3 * cols] = dv
        t_s[cols : 2 * cols, rs] = dk.T
        t_s[2 * cols : 3 * cols, rs] = dv.T
        b_s[1:2, 0:cols] += jnp.sum(dv.astype(F32), axis=0, keepdims=True)

    chunks(2 * rows, 256, grad_rows)
    t_s[3 * cols : 4 * cols, near] = ct_ref[...].astype(BF)
    b_s[0:1, 0:cols] = jnp.sum(dq.astype(F32), axis=0, keepdims=True)
    b_s[2:3] = bu_ref[...]
    b_s[8:16] = vec_ref[...]
    at = 2 * cols
    grad_ref[at : at + 16] = b_s[...].astype(BF)
    other()
    send(d_s)
    arrive(own_ref)
    width = own_ref.shape[1]

    def weight_terms(cs):
        tok = own_ref[:, cs]
        grad_ref[0:cols, cs] = dot(t_s[0:cols, near], tok).astype(BF)
        terms = (
            dot(t_s[cols : 3 * cols, near], tok) + dot(t_s[cols : 3 * cols, far], other.buffer[:, cs])
        ).astype(BF)
        grad_ref[cols : 2 * cols, cs] = terms[0:cols]
        grad_ref[at + 16 : at + 16 + cols, cs] = terms[cols : 2 * cols]
        grad_ref[at + 16 + cols : at + 16 + 2 * cols, cs] = dot(
            t_s[3 * cols : 4 * cols, near], g_ref[:, cs]
        ).astype(BF)

    chunks(width, 256, weight_terms)
    send(grad_ref)


def attend_back_kernel(
    lens_ref, me_ref, core_ref, mid_ref,
    g_ref, wo_ref, q_ref, k_ref, lse_ref, v_ref, ct_ref, own_ref, bu_ref, vec_ref,
    grad_ref, d_ref, oth_s, oth_sem, b_s, *scratch,
):
    flag, use_core = neighbour(lens_ref, me_ref, own_ref.shape[0])
    attend_back_block(
        flag, g_ref, wo_ref, (ct_ref, lse_ref, q_ref, k_ref, v_ref), own_ref,
        lambda: Once(pick_other(use_core, core_ref, mid_ref, oth_s, oth_sem), oth_s),
        grad_ref, d_ref, b_s, bu_ref, vec_ref, scratch,
    )


def attend_back(lens, me, own, tok_core, tok_mid, g, block, bu, vecs, after=()):
    rows, width = own.shape
    a, (_, ct, lse, q, k, v) = block
    cols = q.shape[1]
    args = (lens, me, tok_core, tok_mid, g, a, q, k, lse, v, ct, own, bu, vecs)
    return call(
        attend_back_kernel, "attend_back",
        [shape((4 * cols + 16, width), BF), shape((2 * rows, 3 * cols), BF)],
        args, smem=2, raw=(2, 3), after=after, first=0, part={5: (3 * cols, cols)},
        scratch=[
            pltpu.VMEM((rows, width), BF), pltpu.SemaphoreType.DMA, pltpu.VMEM((16, width), F32),
            pltpu.VMEM((cols, rows), BF), pltpu.VMEM((cols, rows), BF),
            pltpu.VMEM((cols, 2 * rows), BF), pltpu.VMEM((cols, rows), F32),
            pltpu.VMEM((2 * rows, rows), BF), pltpu.VMEM((2 * rows, rows), BF),
            pltpu.VMEM((2 * rows, cols), F32), pltpu.VMEM((2 * rows, cols), F32),
            pltpu.VMEM((cols, rows), F32), pltpu.VMEM((rows, cols), BF),
            pltpu.VMEM((4 * cols, 2 * rows), BF),
        ],
    )


def other_grad_kernel(*refs):
    ds, weights, out_ref = refs[0:4], refs[4:8], refs[8]
    arrive(*ds, *weights)
    depth = ds[0].shape[1]

    def features_of(cs):
        total = dot(ds[0][...], weights[0][0:depth, cs])
        for d_ref, w_ref in zip(ds[1:], weights[1:]):
            total = total + dot(d_ref[...], w_ref[0:depth, cs])
        out_ref[:, cs] = total.astype(out_ref.dtype)

    chunks(out_ref.shape[1], 256, features_of)


def other_grad(ds, joints, rows, after=()):
    width = joints[0].shape[1]
    return call(
        other_grad_kernel, "other_grad", [shape((rows, width), BF)], (*ds, *joints), after=after,
        part={i: (rows, rows) for i in range(4)} | {i: (0, ds[0].shape[1]) for i in range(4, 8)},
    )[0]


def unit_of(residual):
    centre = jnp.mean(residual, axis=1, keepdims=True)
    spread = residual - centre
    inverse = lax.rsqrt(jnp.mean(spread * spread, axis=1, keepdims=True) + norm_eps)
    return spread * inverse, inverse


def norm_back(upstream, unit_rows, inverse, gain):
    unit_grad = upstream * gain
    return inverse * (
        unit_grad
        - jnp.mean(unit_grad, axis=1, keepdims=True)
        - unit_rows * jnp.mean(unit_grad * unit_rows, axis=1, keepdims=True)
    )


def up_down(low_ref, bias_ref, up_refs, down_ref, act_ref, slope_ref, sum_ref, start):
    up_ref = up_refs[0]
    arrive(low_ref, bias_ref, up_ref)

    def units_of(cs):
        pre = bias_ref[:, cs].astype(F32)[2:3] + dot(low_ref[...], up_ref[:, cs])
        phi = 0.5 + 0.5 * lax.erf(pre * half_root)
        act_ref[:, cs] = (pre * phi).astype(BF)
        slope_ref[:, cs] = (phi + pre * jnp.exp(-0.5 * pre * pre) * inv_root_two_pi).astype(BF)

    chunks(up_ref.shape[1], 256, units_of)
    send(act_ref)
    send(slope_ref)
    arrive(down_ref)

    def features_of(cs):
        part = dot(act_ref[...], down_ref[:, cs])
        sum_ref[:, cs] = part if start else sum_ref[:, cs] + part

    chunks(down_ref.shape[1], 256, features_of)


def ffn_back_block(
    g_ref, low_ref, act_ref, slope_ref, down_ref, up_refs, outs, sum_in_ref, sum_ref, pre_s
):
    down_grad_ref, up_grad_ref, bias_ref = outs
    up_ref = up_refs[0]
    arrive(g_ref, act_ref, slope_ref, down_ref)

    def units_of(cs):
        g = g_ref[...]
        down_grad_ref[cs] = contract_rows(act_ref[:, cs], g).astype(BF)
        pre = (contract_cols(g, down_ref[cs]) * slope_ref[:, cs].astype(F32)).astype(BF)
        pre_s[:, cs] = pre
        bias_ref[:, cs] = jnp.sum(pre.astype(F32), axis=0, keepdims=True)

    chunks(down_ref.shape[0], 256, units_of)
    send(down_grad_ref)
    arrive(low_ref, up_ref, sum_in_ref)

    def features_of(cs):
        pre = pre_s[...]
        up_grad_ref[cs] = contract_rows(low_ref[:, cs], pre).astype(BF)
        sum_ref[:, cs] = sum_in_ref[:, cs] + contract_cols(pre, up_ref[cs])

    chunks(up_ref.shape[0], 256, features_of)
    send(up_grad_ref)


def ffn_grad_outs(width, units):
    return [shape((units, width), BF), shape((width, units), BF), shape((1, units), F32)]


def ffn_far_kernel(
    low_ref, u2_ref, bias2_ref, d2_ref, u3_ref, bias3_ref, d3_ref,
    sum_in_ref, unit_ref, gain1_ref, shift1_ref, bd_ref, gain2_ref, shift2_ref, out_grad_ref,
    act2_ref, sl2_ref, out_ref, low_grad_ref, vec_ref,
    down_grad_ref, up_grad_ref, bu_ref, sum_ref,
    act3_s, sl3_s, pre_s, part_s,
):
    up_down(low_ref, bias2_ref, (u2_ref,), d2_ref, act2_ref, sl2_ref, part_s, True)
    up_down(low_ref, bias3_ref, (u3_ref,), d3_ref, act3_s, sl3_s, part_s, False)
    gain1, gain2, shift2 = row(gain1_ref), row(gain2_ref), row(shift2_ref)
    shift1 = row(shift1_ref) + row(bd_ref)
    arrive(unit_ref, sum_in_ref, out_grad_ref)
    vec_ref[...] = jnp.zeros(vec_ref.shape, F32)

    def rows_of(rs):
        resid = unit_ref[rs] * gain1 + shift1 + sum_in_ref[rs] + part_s[rs]
        unit, inverse = unit_of(resid)
        out_ref[rs] = (unit * gain2 + shift2).astype(BF)
        upstream = out_grad_ref[rs].astype(F32)
        vec_ref[0:1] += jnp.sum(upstream * unit, axis=0, keepdims=True)
        vec_ref[1:2] += jnp.sum(upstream, axis=0, keepdims=True)
        back = norm_back(upstream, unit, inverse, gain2)
        sum_ref[rs] = back
        g = back.astype(BF)
        low_grad_ref[rs] = g
        vec_ref[2:3] += jnp.sum(g.astype(F32), axis=0, keepdims=True)

    chunks(unit_ref.shape[0], 256, rows_of)
    send(out_ref)
    send(low_grad_ref)
    ffn_back_block(
        low_grad_ref, low_ref, act3_s, sl3_s, d3_ref, (u3_ref,),
        (down_grad_ref, up_grad_ref, bu_ref), sum_ref, sum_ref, pre_s,
    )


def ffn_far(
    low, joints, ups, downs, near, unit, gain1, shift1, b_down, gain2, shift2, out_grad, after=()
):
    rows, width = low.shape
    units = downs[0].shape[0]
    at = joints[0].shape[0] - 16
    piece = shape((rows, units), BF)
    return call(
        ffn_far_kernel, "ffn_far",
        [
            piece, piece, shape((rows, width), BF), shape((rows, width), BF), shape((8, width), F32),
            *ffn_grad_outs(width, units), shape((rows, width), F32),
        ],
        (
            low, ups[0], joints[0], downs[0], ups[1], joints[1], downs[1], near, unit,
            gain1, shift1, b_down, gain2, shift2, out_grad,
        ),
        part={2: (at, 16), 5: (at, 16)}, first=0, after=after,
        scratch=[pltpu.VMEM((rows, units), BF)] * 3 + [pltpu.VMEM((rows, width), F32)],
    )


def ffn_back_kernel(
    g_ref, act_ref, down_ref, slope_ref, low_ref, up_ref, sum_in_ref,
    down_grad_ref, up_grad_ref, bu_ref, sum_ref, pre_s,
):
    ffn_back_block(
        g_ref, low_ref, act_ref, slope_ref, down_ref, (up_ref,),
        (down_grad_ref, up_grad_ref, bu_ref), sum_in_ref, sum_ref, pre_s,
    )


def ffn_back(g, low, act, slope, up, down, acc, after=()):
    rows, width = low.shape
    units = down.shape[0]
    return call(
        ffn_back_kernel, "ffn_back",
        [*ffn_grad_outs(width, units), shape((rows, width), F32)],
        (g, act, down, slope, low, up, acc), after=after, first=0,
        scratch=[pltpu.VMEM((rows, units), BF)],
    )


def ffn_last_kernel(
    g_ref, act1_ref, d1_ref, sl1_ref, low_ref, u1_ref, act0_ref, d0_ref, sl0_ref, u0_ref, sum_in_ref,
    unit_ref, inv_ref, gain_ref, vec_in_ref, *refs,
):
    low_ref_out, resid_ref, vec_ref = refs[6:9]
    sum_s, pre_s = refs[9:]
    ffn_back_block(
        g_ref, low_ref, act1_ref, sl1_ref, d1_ref, (u1_ref,), refs[0:3], sum_in_ref, sum_s, pre_s
    )
    ffn_back_block(
        g_ref, low_ref, act0_ref, sl0_ref, d0_ref, (u0_ref,), refs[3:6], sum_s, sum_s, pre_s
    )
    gain = row(gain_ref)
    arrive(unit_ref, inv_ref)
    vec_ref[...] = vec_in_ref[...]

    def rows_of(rs):
        upstream = sum_s[rs]
        unit = unit_ref[rs]
        vec_ref[4:5] += jnp.sum(upstream * unit, axis=0, keepdims=True)
        vec_ref[5:6] += jnp.sum(upstream, axis=0, keepdims=True)
        back = norm_back(upstream, unit, inv_ref[rs], gain)
        resid_ref[rs] = back
        low = back.astype(BF)
        low_ref_out[rs] = low
        vec_ref[6:7] += jnp.sum(low.astype(F32), axis=0, keepdims=True)

    chunks(unit_ref.shape[0], 256, rows_of)
    send(resid_ref)
    send(low_ref_out)


def ffn_last(g, low, acts, slopes, ups, downs, acc, unit, inverse, gain, vecs, after=()):
    rows, width = low.shape
    units = downs[0].shape[0]
    return call(
        ffn_last_kernel, "ffn_last",
        [
            *ffn_grad_outs(width, units), *ffn_grad_outs(width, units),
            shape((rows, width), BF), shape((rows, width), F32), shape((8, width), F32),
        ],
        (
            g, acts[1], downs[1], slopes[1], low, ups[1], acts[0], downs[0], slopes[0], ups[0], acc,
            unit, inverse, gain, vecs,
        ),
        after=after, first=0,
        scratch=[pltpu.VMEM((rows, width), F32), pltpu.VMEM((rows, units), BF)],
    )


def spread_small_kernel(in_ref, bq_ref, bv_ref, bu_ref, *rest):
    sums = in_ref[...]
    cols = bq_ref.shape[0]
    bq_ref[...] = sums[0:1, 0:cols].reshape(cols)
    bv_ref[...] = sums[1:2, 0:cols].reshape(cols)
    bu_ref[...] = sums[2:3].reshape(-1)
    for at, ref in zip((8, 9, 10, 12, 13, 14), rest):
        ref[...] = sums[at : at + 1].reshape(-1)


def spread_small(sums, cols, units):
    width = sums.shape[1]
    return call(
        spread_small_kernel, "spread_small",
        [shape((cols,), F32), shape((cols,), F32), shape((units,), F32)] + [shape((width,), F32)] * 6,
        (sums,), part={0: (2 * cols, 16)},
    )


def swap(a, axis, distance):
    size = lax.axis_size(axis)
    return lax.ppermute(a, axis, [(i, i ^ distance) for i in range(size)])


def to_core(a):
    return swap(a, "narrow", 1)


def to_chip(a):
    return swap(a, "narrow", 2)


def to_middle(a):
    return lax.ppermute(a, "narrow", [(1, 2), (2, 1)])


def wide_bits():
    size = lax.axis_size("wide")
    bits = []
    while size > 1:
        assert size % 2 == 0
        bits.append(len(bits))
        size //= 2
    return bits


def part_of(a, which, parts):
    rows = a.shape[0] // parts
    return lax.dynamic_slice_in_dim(a, which * rows, rows, 0)


def in_order(side, mine, got):
    return jnp.where(side == 0, jnp.concatenate([mine, got]), jnp.concatenate([got, mine]))


def hold(a, *others):
    return lax.optimization_barrier((a, *others))[0]


def add_low(*terms):
    total = terms[0].astype(F32)
    for term in terms[1:]:
        total = total + term.astype(F32)
    return total.astype(BF)


def side_of(bit):
    return (lax.axis_index("wide") >> bit) & 1


def own_piece(a):
    at = 0
    for bit in wide_bits():
        at = 2 * at + side_of(bit)
    return part_of(a, at, lax.axis_size("wide"))


class WideSum:
    def __init__(self, a):
        self.a = a
        self.step = 0
        self.send()

    def send(self):
        bit = self.step
        if bit < 3:
            side = side_of(bit)
            self.keep = part_of(self.a, side, 2)
            self.sent = part_of(self.a, 1 - side, 2)
        else:
            self.keep = self.sent = self.a
        self.got = swap(self.sent, "wide", 1 << bit)

    def advance(self, *waits):
        got = hold(self.got, *waits) if waits else self.got
        self.a = add_low(self.keep, got)
        self.step += 1
        if self.step < len(wide_bits()):
            self.send()

    def piece(self, *waits):
        while self.step < len(wide_bits()):
            self.advance(*waits)
            waits = ()
        return self.a


class WideGather:
    def __init__(self, a, bits=(2, 1, 0)):
        self.a = self.sent = a
        self.bits = bits
        self.step = 0
        self.send()

    def send(self):
        self.sent = self.a
        self.got = swap(self.a, "wide", 1 << self.bits[self.step])

    def advance(self, *waits):
        got = hold(self.got, *waits) if waits else self.got
        self.a = in_order(side_of(self.bits[self.step]), self.a, got)
        self.step += 1
        if self.step < len(self.bits):
            self.send()

    def whole(self, *waits):
        while self.step < len(self.bits):
            self.advance(*waits)
            waits = ()
        return self.a


def local(
    tokens, item_lengths, w_query, b_query, w_key, w_value, b_value, w_out, b_out,
    gain_attn, shift_attn, w_up, b_up, w_down, b_down, gain_ffn, shift_ffn, out_grad,
):
    rows, width = tokens.shape
    cols = w_query.shape[1]
    units = w_up.shape[1]
    assert lax.axis_size("narrow") == 4
    me = lax.axis_index("narrow").reshape(1)

    tok_mid = to_middle(tokens)
    tok_core = to_core(tokens)
    pieces = to_chip(own_piece(w_down))
    joint = pack_joint(w_query, w_key, w_value, w_out, b_query, b_value, b_up)
    joint_core = to_core(joint)
    joint_chip = to_chip(hold(joint, pieces, tok_mid))
    down_gather = WideGather(pieces, wide_bits()[::-1])
    while down_gather.step < len(down_gather.bits) - 2:
        down_gather.advance(joint_core)
    near0, near1 = attend_pair(
        "attend_near", item_lengths, me, tokens, tok_core, tok_mid, [joint, joint_core],
        (down_gather.sent,),
    )
    down_gather.advance(near1[2])
    gate = down_gather.sent
    joint_chip = hold(joint_chip, gate)
    joint_diag = to_core(joint_chip)
    up_chip = to_chip(hold(w_up, joint_chip))
    up_core = to_core(hold(w_up, joint_chip))
    down_core = to_core(hold(w_down, joint_chip))
    far2, far3 = attend_pair(
        "attend_far", item_lengths, me, tokens, tok_core, tok_mid, [joint_chip, joint_diag], (gate,)
    )
    joints = [joint, joint_core, joint_chip, joint_diag]
    saved = [near0, near1, far2, far3]
    unit_one, inv_one, low, act0, sl0, act1, sl1, near_sum = norm_near(
        tokens, [s[0] for s in saved], joints, b_out, gain_attn, shift_attn,
        [w_up, up_core], [w_down, down_core],
    )
    down_chip = down_gather.whole(inv_one)
    down_diag = to_core(down_chip)
    up_chip = hold(up_chip, down_chip)
    up_diag = to_core(up_chip)
    act2, sl2, layer_out, ffn_grad, vecs, down_d, up_d, bu_d, acc = ffn_far(
        low, joints[2:], [up_chip, up_diag], [down_chip, down_diag],
        near_sum, unit_one, gain_attn, shift_attn, b_down, gain_ffn, shift_ffn, out_grad,
    )

    up_from_core = to_core(up_d)
    down_from_core = to_core(down_d)
    down_x, up_x, bu_x, acc = ffn_back(ffn_grad, low, act2, sl2, up_chip, down_chip, acc)
    up_far = add_low(up_x, hold(up_from_core, bu_x))
    up_sum = to_chip(up_far)
    down_far = add_low(down_x, hold(down_from_core, up_far))
    down_sum = to_chip(down_far)
    down_c, up_c, bu_c, down_o, up_o, bu_o, attn_grad, resid_one, vecs = ffn_last(
        ffn_grad, low, (act0, act1), (sl0, sl1), (w_up, up_core), (w_down, down_core), acc,
        unit_one, inv_one, gain_attn, vecs, (up_far, down_far),
    )
    up_back = to_core(up_c)
    down_back = to_core(down_c)
    grads, parts = [None] * 4, [None] * 4
    bus = (bu_o, bu_c, bu_x, bu_d)

    def back_attend(r, *after):
        grads[r], parts[r] = attend_back(
            item_lengths, me, tokens, tok_core, tok_mid, attn_grad, (joints[r], saved[r]),
            bus[r], vecs, after,
        )
        return grads[r]

    mark = back_attend(3)
    up_sum = hold(up_sum, mark)
    near_up = WideSum(add_low(up_o, hold(up_back, up_sum), up_sum))
    down_near = add_low(down_o, hold(down_back, near_up.sent))
    joint_from_core = to_core(hold(grads[3], down_near))
    mark = back_attend(2, near_up.sent, down_near)
    down_sum = hold(down_sum, mark)
    near_down = WideSum(add_low(down_near, down_sum))
    joint_far = add_low(grads[2], hold(joint_from_core, near_down.a))
    joint_sum = to_chip(joint_far)
    near_up.advance(joint_far)
    mark = back_attend(1, joint_far, near_up.sent, near_down.sent)
    near_up.advance(mark)
    near_down.advance(near_up.sent)
    joint_back = to_core(hold(grads[1], near_down.sent))
    mark = back_attend(0, near_up.sent, near_down.sent)
    joint_sum = hold(joint_sum, mark)
    joint_back = hold(joint_back, joint_sum)

    def rows_of(a, part):
        return a[: 2 * cols + 16] if part == 0 else a[2 * cols + 16 :]

    def joint_part(i, own, got):
        return WideSum(add_low(rows_of(own, i), rows_of(got, i), rows_of(joint_back, i)))

    first = joint_part(0, grads[0], joint_sum)
    second = joint_part(1, grads[0], hold(joint_sum, first.sent))
    up_gather = WideGather(near_up.piece(second.sent))
    near_down.advance(up_gather.sent)
    first.advance(near_down.sent)
    down_gather = WideGather(near_down.piece(first.sent))
    up_gather.advance(down_gather.sent)
    second.advance(up_gather.sent)
    oth_low = other_grad(parts, joints, rows, (second.sent,))
    first.advance(oth_low)
    up_gather.advance(first.sent)
    down_gather.advance(up_gather.sent)
    oth_core, oth_mid = to_core(hold(oth_low, down_gather.sent)), to_middle(hold(oth_low, down_gather.sent))
    second.advance(down_gather.sent)
    first = WideGather(first.piece(second.sent))
    down_gather.advance(first.sent)
    second = WideGather(second.piece(down_gather.sent))
    first.advance(second.sent)
    token_grad = take_back(
        item_lengths, me, hold(oth_core, first.sent), hold(oth_mid, first.sent), resid_one,
        parts, joints, (first.sent, second.sent),
    )
    second.advance(token_grad)
    first.advance(second.sent)
    w_up_grad = up_gather.whole(first.sent).astype(F32)
    second.advance(w_up_grad)
    w_down_grad = down_gather.whole(second.sent).astype(F32)
    qk_grad = first.whole(w_down_grad).astype(F32)
    bq, bv, bu, gain_ffn_g, shift_ffn_g, b_down_g, gain_attn_g, shift_attn_g, b_out_g = spread_small(
        qk_grad, cols, units
    )
    vo_grad = second.whole(qk_grad).astype(F32)
    joint_grads = [qk_grad[:cols], qk_grad[cols : 2 * cols], vo_grad[:cols]]
    w_out_grad = vo_grad[cols:]
    return (
        layer_out,
        token_grad,
        joint_grads[0].T,
        bq,
        joint_grads[1].T,
        joint_grads[2].T,
        bv,
        w_out_grad,
        b_out_g,
        gain_attn_g,
        shift_attn_g,
        w_up_grad,
        bu,
        w_down_grad,
        b_down_g,
        gain_ffn_g,
        shift_ffn_g,
    )


def take_back_kernel(lens_ref, me_ref, core_ref, mid_ref, *refs):
    ds, weights, resid_ref, out_ref, oth_s, oth_sem = refs[0:4], refs[4:8], *refs[8:]
    flag, use_core = neighbour(lens_ref, me_ref, resid_ref.shape[0])
    other = pick_other(use_core, core_ref, mid_ref, oth_s, oth_sem)
    arrive(*ds, *weights, resid_ref)
    other.wait()
    depth = ds[0].shape[1]

    def features_of(cs):
        total = resid_ref[:, cs] + jnp.where(flag, oth_s[:, cs].astype(F32), 0.0)
        for d_ref, w_ref in zip(ds, weights):
            total = total + dot(d_ref[...], w_ref[0:depth, cs])
        out_ref[:, cs] = total

    chunks(out_ref.shape[1], 256, features_of)


def take_back(lens, me, core, mid, resid, ds, joints, after):
    rows, width = resid.shape
    depth = ds[0].shape[1]
    return call(
        take_back_kernel, "take_back", [shape((rows, width), F32)],
        (lens, me, core, mid, *ds, *joints, resid), smem=2, raw=(2, 3), after=after,
        part={i: (0, rows) for i in range(4, 8)} | {i: (0, depth) for i in range(8, 12)},
        scratch=[pltpu.VMEM(core.shape, BF), pltpu.SemaphoreType.DMA],
    )[0]


def solution(mesh):
    rows_spec = P(("wide", "narrow"), None)
    col_spec = P(None, "narrow")
    vec_spec = P("narrow")
    row_spec = P("narrow", None)
    full = P()
    return jax.shard_map(
        local,
        mesh=mesh,
        in_specs=(
            rows_spec, P("wide"), col_spec, vec_spec, col_spec, col_spec, vec_spec, row_spec, full,
            full, full, col_spec, vec_spec, row_spec, full, full, full, rows_spec,
        ),
        out_specs=(
            rows_spec, rows_spec, col_spec, vec_spec, col_spec, col_spec, vec_spec, row_spec, full,
            full, full, col_spec, vec_spec, row_spec, full, full, full,
        ),
        check_vma=False,
    )
```
